128 devices in a mesh: req: 32 (over z, y, core), head: 4 (over x).
Axes of the slice: x: 4, y: 4, z: 4, core: 2. Of those that a mesh axis runs over, the one named last changes fastest.
Arguments:
- hidden_in: bfloat16 [512, 2048], P(None, 'req'), may hold values from -6 to 6
- lengths: int32 [512], P('req'), may hold values from 16 to 3072, as said below
- w_qkv: bfloat16 [3, 2048, 2048], P(None, 'req', 'head'), may hold values from -4 to 4, as said below
- qk_gain: float32 [2, 2048], P(None, 'head'), may hold values from 0.25 to 1.75
- cache_keys: bfloat16 [131072, 2048], P('req', 'head'), may hold values from -240 to 240
- cache_values: bfloat16 [131072, 2048], P('req', 'head'), may hold values from -6 to 6
- w_out: bfloat16 [2048, 2048], P('req', 'head'), may hold values from -3 to 3, as said below
- norm_gain: float32 [2, 2048], P(None, 'req'), may hold values from 0.25 to 1.75
- w_gate_up: bfloat16 [2, 2048, 8192], P(None, 'req', 'head'), may hold values from -0.125 to 0.125
- w_down: bfloat16 [2048, 8192], P('req', 'head'), may hold values from -3 to 3, as said below
Outputs:
- hidden_out: bfloat16 [512, 2048], P(None, 'req')
- new_keys: bfloat16 [512, 2048], P('req', 'head')
- new_values: bfloat16 [512, 2048], P('req', 'head')
The draws below stay inside these ranges and needn't reach their ends.
Inputs may be any that keep to these rules, and one draw needn't show every extreme that they name: `lengths`: in each aligned group of requests 8 * 16 * k to 8 * 16 * k + 8 * 16 - 1 exactly one request, at a place drawn from the seed, has length 3072; every other length lies between 16 and 64. `w_qkv`: entries have magnitude at most 26 / sqrt(2048). `w_out`: entries have magnitude at most 23 / sqrt(2048). `w_down`: entries have magnitude at most 23 / sqrt(8192).
All inputs are finite; a program needn't handle non-finite values.
Results may differ from the reference program's by a relative error of at most 0.015.
Values may be sent and summed in bfloat16 or wider, within the bound.
No kernel may reach another device: no remote copies, remote signals or barrier semaphores. Data moves between devices by JAX's collectives and lax.ppermute only.
A program may use at most 128 MiB of HBM per device.

```python
import jax
import jax.numpy as jnp
from jax import lax

D = 2048
HEADS = 16
HEAD_DIM = 128
FF = 8192
REQ_DEV = 16
SHORT_MAX = 64
LONG = 3072
REQUESTS = 512
POOL_DEV = 4096
POOL = 131072
N_REQ = 32


def draw_lengths(key, part):
    first, second = jax.random.split(key)
    drawn = jax.random.randint(first, (REQUESTS,), SHORT_MAX // 4, SHORT_MAX + 1)
    span = 8 * REQ_DEV
    groups = REQUESTS // span
    picked = jax.random.randint(second, (groups,), 0, span)
    places = jnp.arange(REQUESTS, dtype=jnp.int32)
    chosen = places % span == picked[places // span]
    return jnp.where(chosen, LONG, drawn).astype(jnp.int32)


def draw_w_qkv(key, part):
    first, second = jax.random.split(jax.random.fold_in(key, 7))
    columns = jnp.arange(D, dtype=jnp.float32)[None, None, :] / D - 0.5
    jitter = jax.random.uniform(second, (3, 1, D), jnp.float32, -0.3, 0.3)
    base = jnp.clip(jax.random.normal(first, (3, D, D), jnp.float32), -6.0, 6.0)
    factor = jnp.exp(jnp.log(4.0) * columns + jitter)
    return (base * factor * D ** (-0.5)).astype(jnp.bfloat16)


def draw_cache_keys(key, part):
    first = jax.random.fold_in(key, 0)
    base = jnp.clip(jax.random.normal(first, (POOL, D), jnp.float32), -6.0, 6.0)
    return base.astype(jnp.bfloat16)


def scaled_rows(key, rows_total, cols_total):
    first, second = jax.random.split(key)
    base = jnp.clip(jax.random.normal(first, (rows_total, cols_total), jnp.float32), -6.0, 6.0)
    spread = jax.random.uniform(second, (rows_total, 1), jnp.float32, -1.15, 1.15)
    rising = jnp.log(3.0) * (jnp.arange(rows_total, dtype=jnp.float32)[:, None] / rows_total - 0.5)
    return base * jnp.exp(spread + rising) * cols_total ** (-0.5) / 1.47


def draw_w_out(key, part):
    return scaled_rows(key, D, D).astype(jnp.bfloat16)


def draw_w_down(key, part):
    return scaled_rows(key, D, FF).astype(jnp.bfloat16)


def steps_of(key, shape, pieces, low, high):
    def one(dim, shards_of):
        draws = jax.random.uniform(jax.random.fold_in(jax.random.fold_in(key, 6), dim), (shards_of,), jnp.float32, low / len(pieces), high / len(pieces))
        return jnp.repeat(jnp.exp(draws), shape[dim] // shards_of).reshape((-1,) + (1,) * (len(shape) - dim - 1))

    level = one(*pieces[0])
    for cut in pieces[1:]:
        level = level * one(*cut)
    return level


def scatter_about(rng, shape, deviation, limit, pieces=(), kind=jnp.bfloat16):
    values = deviation * jax.random.normal(rng, shape, jnp.float32)
    if pieces:
        values = values * steps_of(rng, shape, pieces, -0.22, 0.18)
    return jnp.clip(values, -limit, limit).astype(kind)


def setup_inputs(seed: int = 0) -> dict:
    arg_keys = jax.random.split(jax.random.key(seed), 11)
    hidden_in = scatter_about(arg_keys[0], (REQUESTS, D), 1.0, 6.0, ((1, 32),))
    lengths = draw_lengths(jax.random.fold_in(arg_keys[10], 71), 0)
    w_qkv = draw_w_qkv(jax.random.fold_in(arg_keys[10], 71), 0)
    qk_gain = jnp.clip(1.0 + 0.15 * jax.random.normal(arg_keys[3], (2, D), jnp.float32), 0.25, 1.75)
    cache_keys = draw_cache_keys(jax.random.fold_in(arg_keys[10], 71), 0)
    cache_values = scatter_about(arg_keys[5], (POOL, D), 1.0, 6.0, ((0, 32), (1, 4)))
    w_out = draw_w_out(jax.random.fold_in(arg_keys[10], 71), 0)
    norm_gain = jnp.clip(1.0 + 0.15 * jax.random.normal(arg_keys[7], (2, D), jnp.float32), 0.25, 1.75)
    w_gate_up = scatter_about(arg_keys[8], (2, D, FF), D ** -0.5, 0.125, ((1, 32), (2, 4)))
    w_down = draw_w_down(jax.random.fold_in(arg_keys[10], 71), 0)
    return {"hidden_in": hidden_in, "lengths": lengths, "w_qkv": w_qkv, "qk_gain": qk_gain, "cache_keys": cache_keys, "cache_values": cache_values, "w_out": w_out, "norm_gain": norm_gain, "w_gate_up": w_gate_up, "w_down": w_down}


EPS = 1e-06
THETA = 500000.0

def rotate(values, positions):
    half = values.shape[-1] // 2
    freqs = jnp.power(THETA, -(jnp.arange(half, dtype=jnp.float32) * 2.0 / values.shape[-1]))
    angles = positions.astype(jnp.float32)[:, None] * freqs[None, :]
    cosine = jnp.cos(angles)[:, None, :]
    sine = jnp.sin(angles)[:, None, :]
    first = values[..., :half]
    second = values[..., half:]
    return jnp.concatenate([first * cosine - second * sine, second * cosine + first * sine], axis=-1)

def normalize(values, gain):
    power = lax.optimization_barrier(jnp.mean(values * values, axis=-1, keepdims=True))
    return values * lax.rsqrt(power + EPS) * gain

def attend_device(items):
    query, key_self, value_self, counts, stored_keys, stored_values = items
    scale = HEAD_DIM ** (-0.5)
    starts = jnp.cumsum(counts) - counts
    ends = starts + counts
    positions = jnp.arange(POOL_DEV, dtype=jnp.int32)
    inside = (positions[None, :] >= starts[:, None]) & (positions[None, :] < ends[:, None])
    query_wide = query.astype(jnp.float32)
    scores = jnp.einsum('rhd,phd->rhp', query_wide, stored_keys.astype(jnp.float32)) * scale
    scores = jnp.where(inside[:, None, :], scores, -jnp.inf)
    own_score = lax.optimization_barrier(jnp.sum(query_wide * key_self.astype(jnp.float32), axis=2)) * scale
    highest = jnp.maximum(lax.optimization_barrier(jnp.max(scores, axis=2)), own_score)
    weights = lax.optimization_barrier(jnp.exp(scores - highest[:, :, None]).astype(jnp.bfloat16)).astype(jnp.float32)
    own_weight = lax.optimization_barrier(jnp.exp(own_score - highest).astype(jnp.bfloat16)).astype(jnp.float32)
    denominator = lax.optimization_barrier(jnp.sum(weights, axis=2)) + own_weight
    numerator = jnp.einsum('rhp,phd->rhd', weights, stored_values.astype(jnp.float32))
    numerator = numerator + own_weight[:, :, None] * value_self.astype(jnp.float32)
    return (numerator / denominator[:, :, None]).astype(jnp.bfloat16)

def reference(hidden_in, lengths, w_qkv, qk_gain, cache_keys, cache_values, w_out, norm_gain, w_gate_up, w_down):
    query = jnp.dot(hidden_in, w_qkv[0], preferred_element_type=jnp.float32)
    key_new = jnp.dot(hidden_in, w_qkv[1], preferred_element_type=jnp.float32)
    value_new = jnp.dot(hidden_in, w_qkv[2], preferred_element_type=jnp.float32).astype(jnp.bfloat16)
    query = normalize(query, qk_gain[0])
    key_new = normalize(key_new, qk_gain[1])
    query_rot = rotate(query.reshape(REQUESTS, HEADS, HEAD_DIM), lengths).astype(jnp.bfloat16)
    key_rot = rotate(key_new.reshape(REQUESTS, HEADS, HEAD_DIM), lengths).astype(jnp.bfloat16)
    grouped = (query_rot.reshape(N_REQ, REQ_DEV, HEADS, HEAD_DIM), key_rot.reshape(N_REQ, REQ_DEV, HEADS, HEAD_DIM), value_new.reshape(N_REQ, REQ_DEV, HEADS, HEAD_DIM), lengths.reshape(N_REQ, REQ_DEV), cache_keys.reshape(N_REQ, POOL_DEV, HEADS, HEAD_DIM), cache_values.reshape(N_REQ, POOL_DEV, HEADS, HEAD_DIM))
    attended = lax.map(attend_device, grouped).reshape(REQUESTS, D)
    attn_full = jnp.dot(attended, w_out.T, preferred_element_type=jnp.float32)
    hidden_mid = (hidden_in.astype(jnp.float32) + normalize(attn_full, norm_gain[0])).astype(jnp.bfloat16)
    gated = jnp.dot(hidden_mid, w_gate_up[0], preferred_element_type=jnp.float32)
    lifted = jnp.dot(hidden_mid, w_gate_up[1], preferred_element_type=jnp.float32)
    activated = (jax.nn.silu(gated) * lifted).astype(jnp.bfloat16)
    ffn_full = jnp.dot(activated, w_down.T, preferred_element_type=jnp.float32)
    hidden_out = (hidden_mid.astype(jnp.float32) + normalize(ffn_full, norm_gain[1])).astype(jnp.bfloat16)
    return (hidden_out, key_rot.reshape(REQUESTS, D), value_new)
```

```python
import functools

import jax
import jax.numpy as jnp
from jax import lax
from jax.experimental import pallas as pl
from jax.experimental.pallas import tpu as pltpu
from jax.sharding import Mesh, PartitionSpec as P

HEAD_DIM = 128
EPS = 1e-06
THETA = 500000.0
NT = (((1,), (1,)), ((), ()))
BLOCK = 512


def rotate(values, cosine, sine):
    half = HEAD_DIM // 2
    first = values[..., :half]
    second = values[..., half:]
    return jnp.concatenate(
        [first * cosine - second * sine, second * cosine + first * sine], axis=-1
    )


def attend_kernel(len_ref, q_ref, kn_ref, vn_ref, bounds_ref, keys_hbm, values_hbm, out_ref,
                  kbuf, vbuf, score, acc, top, total, ksem, vsem):
    rows, width = q_ref.shape
    heads = width // HEAD_DIM
    wide = rows * heads
    pool = keys_hbm.shape[0]
    blocks = pool // BLOCK
    used = len_ref[0]
    for r in range(1, rows):
        used = used + len_ref[r]

    def key_copy(i):
        return pltpu.make_async_copy(keys_hbm.at[pl.ds(i * BLOCK, BLOCK)], kbuf.at[i], ksem.at[i])

    def value_copy(i):
        return pltpu.make_async_copy(values_hbm.at[pl.ds(i * BLOCK, BLOCK)], vbuf.at[i], vsem.at[i])

    for i in range(blocks):
        @pl.when(i * BLOCK < used)
        def _():
            key_copy(i).start()
    for i in range(blocks):
        @pl.when(i * BLOCK < used)
        def _():
            value_copy(i).start()

    scale = HEAD_DIM ** (-0.5)
    row_head = lax.broadcasted_iota(jnp.int32, (wide, width), 0) // rows
    col_head = lax.broadcasted_iota(jnp.int32, (wide, width), 1) // HEAD_DIM
    own_head = row_head == col_head
    q = q_ref[...].astype(jnp.float32)
    kn = kn_ref[...].astype(jnp.float32)
    q_all = jnp.concatenate([q] * heads, axis=0)
    kn_all = jnp.concatenate([kn] * heads, axis=0)
    vn_all = jnp.concatenate([vn_ref[...].astype(jnp.float32)] * heads, axis=0)
    q_all = jnp.where(own_head, q_all, 0.0)
    own_score = jnp.sum(q_all * kn_all, axis=1, keepdims=True) * scale
    q_block = q_all.astype(jnp.bfloat16)
    starts = bounds_ref[:, 0:1]
    ends = bounds_ref[:, 1:2]
    top[...] = jnp.broadcast_to(own_score, top.shape)

    for i in range(blocks):
        @pl.when(i * BLOCK < used)
        def _():
            key_copy(i).wait()
            s = lax.dot_general(q_block, kbuf[i], NT, preferred_element_type=jnp.float32) * scale
            place = lax.broadcasted_iota(jnp.int32, s.shape, 1) + i * BLOCK
            s = jnp.where((place >= starts) & (place < ends), s, -jnp.inf)
            score[i] = s
            top[...] = jnp.maximum(top[...], jnp.max(s, axis=1, keepdims=True))

    highest = top[:, 0:1]
    own_weight = jnp.exp(own_score - highest).astype(jnp.bfloat16).astype(jnp.float32)
    total[...] = jnp.broadcast_to(own_weight, total.shape)
    acc[...] = own_weight * vn_all

    for i in range(blocks):
        @pl.when(i * BLOCK < used)
        def _():
            value_copy(i).wait()
            w = jnp.exp(score[i] - highest).astype(jnp.bfloat16)
            total[...] += jnp.sum(w.astype(jnp.float32), axis=1, keepdims=True)
            acc[...] += jnp.dot(w, vbuf[i], preferred_element_type=jnp.float32)

    result = acc[...] / total[:, 0:1]
    out_ref[...] = jnp.concatenate(
        [
            result[h * rows : (h + 1) * rows, h * HEAD_DIM : (h + 1) * HEAD_DIM]
            for h in range(heads)
        ],
        axis=1,
    ).astype(out_ref.dtype)


def attend(lengths, query, key_new, value_new, cache_keys, cache_values):
    rows, width = query.shape
    heads = width // HEAD_DIM
    wide = rows * heads
    pool = cache_keys.shape[0]
    blocks = pool // BLOCK
    ends = jnp.cumsum(lengths)
    starts = ends - lengths
    bounds = jnp.tile(jnp.stack([starts, ends], axis=1), (heads, 1))
    vmem = pl.BlockSpec(memory_space=pltpu.VMEM)
    return pl.pallas_call(
        attend_kernel,
        out_shape=jax.ShapeDtypeStruct((rows, width), jnp.bfloat16),
        in_specs=[pl.BlockSpec(memory_space=pltpu.SMEM), vmem, vmem, vmem, vmem,
                  pl.BlockSpec(memory_space=pl.ANY), pl.BlockSpec(memory_space=pl.ANY)],
        out_specs=vmem,
        scratch_shapes=[
            pltpu.VMEM((blocks, BLOCK, width), jnp.bfloat16),
            pltpu.VMEM((blocks, BLOCK, width), jnp.bfloat16),
            pltpu.VMEM((blocks, wide, BLOCK), jnp.float32),
            pltpu.VMEM((wide, width), jnp.float32),
            pltpu.VMEM((wide, 128), jnp.float32),
            pltpu.VMEM((wide, 128), jnp.float32),
            pltpu.SemaphoreType.DMA((blocks,)),
            pltpu.SemaphoreType.DMA((blocks,)),
        ],
        compiler_params=pltpu.CompilerParams(vmem_limit_bytes=24 * 1024 * 1024),
        cost_estimate=pl.CostEstimate(flops=1 << 29, bytes_accessed=8 << 20, transcendentals=1 << 18),
        name="attend",
    )(lengths, query, key_new, value_new, bounds, cache_keys, cache_values)


def ffn_kernel(a_ref, h_ref, gain_ref, w_hbm, mid_ref, out_ref, wbuf, sem):
    groups = w_hbm.shape[0]
    for g in range(groups):
        pltpu.make_async_copy(w_hbm.at[g], wbuf.at[g], sem.at[g]).start()
    a = a_ref[...].astype(jnp.float32)
    power = jnp.mean(a * a, axis=1, keepdims=True)
    mid = h_ref[...].astype(jnp.float32) + a * lax.rsqrt(power + EPS) * gain_ref[...]
    mid = mid.astype(jnp.bfloat16)
    mid_ref[...] = mid
    rows, width = mid.shape
    part = width // groups
    units = wbuf.shape[-1]
    gate = jnp.zeros((rows, units), jnp.float32)
    lift = jnp.zeros((rows, units), jnp.float32)
    for g in range(groups):
        pltpu.make_async_copy(w_hbm.at[g], wbuf.at[g], sem.at[g]).wait()
        m = mid[:, g * part : (g + 1) * part]
        gate += jnp.dot(m, wbuf[g, :, 0].reshape(part, units), preferred_element_type=jnp.float32)
        lift += jnp.dot(m, wbuf[g, :, 1].reshape(part, units), preferred_element_type=jnp.float32)
    act = (gate / (1.0 + jnp.exp(-gate)) * lift).astype(jnp.bfloat16)
    for g in range(groups):
        out_ref[:, g * part : (g + 1) * part] = lax.dot_general(
            act, wbuf[g, :, 2].reshape(part, units), NT, preferred_element_type=jnp.float32
        ).astype(out_ref.dtype)


def feed_forward(a, h, gain, weights):
    rows, width = a.shape
    vmem = pl.BlockSpec(memory_space=pltpu.VMEM)
    return pl.pallas_call(
        ffn_kernel,
        out_shape=(
            jax.ShapeDtypeStruct((rows, width), jnp.bfloat16),
            jax.ShapeDtypeStruct((rows, width), jnp.float32),
        ),
        in_specs=[vmem, vmem, vmem, pl.BlockSpec(memory_space=pl.ANY)],
        out_specs=(vmem, vmem),
        scratch_shapes=[
            pltpu.VMEM(weights.shape, jnp.bfloat16),
            pltpu.SemaphoreType.DMA((weights.shape[0],)),
        ],
        compiler_params=pltpu.CompilerParams(vmem_limit_bytes=24 * 1024 * 1024),
        cost_estimate=pl.CostEstimate(flops=1 << 29, bytes_accessed=7 << 20, transcendentals=1 << 15),
        name="feed_forward",
    )(a, h, gain, weights)


def body(hidden_in, lengths, w_qkv, qk_gain, cache_keys, cache_values, w_out, norm_gain,
         w_gate_up, w_down):
    bf16 = jnp.bfloat16
    nz, ny, nc, nx = (lax.axis_size(a) for a in ("z", "y", "c", "x"))
    core = lax.axis_index("c")
    y_here = lax.axis_index("y")
    x_here = lax.axis_index("x")
    rows = lengths.shape[0]
    width = w_qkv.shape[2]
    heads = width // HEAD_DIM
    feats = hidden_in.shape[1]
    model = width * nx
    swap = [(0, 1), (1, 0)]

    units = w_gate_up.shape[2] // ny
    stacked = jnp.concatenate([w_gate_up, w_down[None]], axis=0)

    def unit_block(i):
        return lax.dynamic_slice_in_dim(stacked, i * units, units, 2)

    pieces = [unit_block(y_here)]
    for shift in range(1, ny):
        pieces.append(
            lax.ppermute(unit_block((y_here + shift) % ny), "y",
                         [(i, (i + shift) % ny) for i in range(ny)])
        )
    piled = jnp.stack(pieces, axis=0)
    order = (y_here - jnp.arange(ny)) % ny
    mine = jnp.concatenate(
        [lax.dynamic_index_in_dim(piled, order[i], 0, keepdims=True) for i in range(ny)], axis=0
    )
    ffn_weights = lax.all_gather(mine, ("z", "c"), axis=0, tiled=False)
    out_weights = lax.all_gather(w_out, ("z", "c", "y"), axis=0, tiled=True)

    by_core = hidden_in.reshape(nz * ny, nc, rows, feats)
    own_rows = lax.dynamic_index_in_dim(by_core, core, 1, keepdims=False)
    other_rows = lax.dynamic_index_in_dim(by_core, 1 - core, 1, keepdims=False)
    mate_rows = lax.ppermute(other_rows, "c", swap)
    mate_w = lax.ppermute(w_qkv, "c", swap)
    first = core == 0
    left = jnp.where(first, own_rows, mate_rows)
    right = jnp.where(first, mate_rows, own_rows)
    both_rows = jnp.concatenate([left, right], axis=2)
    both_w = jnp.concatenate(
        [jnp.where(first, w_qkv, mate_w), jnp.where(first, mate_w, w_qkv)], axis=1
    )
    product = jnp.einsum(
        "brd,gdf->brgf", both_rows, both_w, preferred_element_type=jnp.float32
    ).astype(bf16).reshape(nz * ny, rows, 3 * width)
    message = jnp.concatenate([product, both_rows], axis=2)
    got = lax.all_to_all(message, ("z", "y"), 0, 0, tiled=True)
    summed = jnp.sum(got[:, :, : 3 * width].astype(jnp.float32), axis=0)
    query = summed[:, :width]
    key_new = summed[:, width : 2 * width]
    value_new = summed[:, 2 * width :].astype(bf16)
    rest = got[:, :, 3 * width :].reshape(nz, ny, rows, nc, feats)
    rest = lax.dynamic_index_in_dim(rest, x_here, 0, keepdims=False)
    rest = rest.transpose(1, 2, 0, 3).reshape(rows, width)

    squares = lax.psum(jnp.stack([jnp.sum(query * query, axis=1), jnp.sum(key_new * key_new, axis=1)]), "x")
    half = HEAD_DIM // 2
    freqs = jnp.power(THETA, -(jnp.arange(half, dtype=jnp.float32) * 2.0 / HEAD_DIM))
    angles = lengths.astype(jnp.float32)[:, None] * freqs[None, :]
    cosine = jnp.cos(angles)[:, None, :]
    sine = jnp.sin(angles)[:, None, :]
    query = query * lax.rsqrt(squares[0][:, None] / model + EPS) * qk_gain[0]
    key_new = key_new * lax.rsqrt(squares[1][:, None] / model + EPS) * qk_gain[1]
    query = rotate(query.reshape(rows, heads, HEAD_DIM), cosine, sine).astype(bf16).reshape(rows, width)
    key_new = rotate(key_new.reshape(rows, heads, HEAD_DIM), cosine, sine).astype(bf16).reshape(rows, width)
    attended = attend(lengths, query, key_new, value_new, cache_keys, cache_values)

    partial = lax.dot_general(attended, out_weights, NT, preferred_element_type=jnp.float32)
    partial = partial.reshape(rows, nx, width).transpose(1, 0, 2)
    branch = jnp.sum(lax.all_to_all(partial, "x", 0, 0, tiled=True), axis=0).astype(bf16)
    message = jnp.concatenate([branch, rest], axis=1)
    message = jnp.broadcast_to(message[None], (ny * nx, rows, 2 * width))
    got = lax.all_to_all(message, ("y", "x"), 0, 0, tiled=True)
    got = got.reshape(ny, nx, rows, 2, width).transpose(3, 0, 2, 1, 4).reshape(2, ny * rows, model)

    gain = lax.all_gather(norm_gain, ("z", "c", "y"), axis=1, tiled=True)
    mid, partial = feed_forward(got[0], got[1], gain[0:1], ffn_weights)
    mine_rows = rows // nx
    partial = partial.reshape(ny * nx, mine_rows, model)
    full = jnp.sum(lax.all_to_all(partial, ("y", "x"), 0, 0, tiled=True), axis=0)
    mid_here = lax.dynamic_slice_in_dim(mid, (y_here * nx + x_here) * mine_rows, mine_rows, 0)
    power = jnp.mean(full * full, axis=1, keepdims=True)
    hidden = (mid_here.astype(jnp.float32) + full * lax.rsqrt(power + EPS) * gain[1:2]).astype(bf16)
    hidden = hidden.reshape(mine_rows, nz, nc, ny, feats).transpose(1, 3, 2, 0, 4)
    hidden = jnp.broadcast_to(
        hidden[:, :, :, None], (nz, ny, nc, nx, mine_rows, feats)
    ).reshape(nz * ny * nc * nx, mine_rows, feats)
    hidden = lax.all_to_all(hidden, ("z", "y", "c", "x"), 0, 0, tiled=True)
    return hidden.reshape(-1, feats), key_new, value_new


def solution(mesh):
    fine = Mesh(mesh.devices.reshape(4, 4, 2, 4), ("z", "y", "c", "x"))
    req = ("z", "y", "c")
    return jax.shard_map(
        body,
        mesh=fine,
        in_specs=(
            P(None, req),
            P(req),
            P(None, req, "x"),
            P(None, "x"),
            P(req, "x"),
            P(req, "x"),
            P(req, "x"),
            P(None, req),
            P(None, req, "x"),
            P(req, "x"),
        ),
        out_specs=(P(None, req), P(req, "x"), P(req, "x")),
        check_vma=False,
    )
```

```python
import functools

import jax
import jax.numpy as jnp
from jax import lax
from jax.experimental import pallas as pl
from jax.experimental.pallas import tpu as pltpu
from jax.sharding import Mesh, PartitionSpec as P

HEAD_DIM = 128
EPS = 1e-06
THETA = 500000.0
NT = (((1,), (1,)), ((), ()))
BLOCK = 512
F32 = jnp.float32
BF16 = jnp.bfloat16
NZ, NY, NC, NX = 4, 4, 2, 4
VMEM = pl.BlockSpec(memory_space=pltpu.VMEM)
HBM = pl.BlockSpec(memory_space=pltpu.HBM)
ANY = pl.BlockSpec(memory_space=pl.ANY)
SMEM = pl.BlockSpec(memory_space=pltpu.SMEM)
LIMIT = 32 * 1024 * 1024


def call(kernel, out_shape, in_specs, out_specs, scratch=(), cost=(1 << 20, 1 << 20), name=None):
    return pl.pallas_call(
        kernel,
        out_shape=out_shape,
        in_specs=in_specs,
        out_specs=out_specs,
        scratch_shapes=list(scratch),
        compiler_params=pltpu.CompilerParams(vmem_limit_bytes=LIMIT),
        cost_estimate=pl.CostEstimate(flops=cost[0], bytes_accessed=cost[1], transcendentals=0),
        name=name,
    )


def shape(dims, dtype):
    return jax.ShapeDtypeStruct(dims, dtype)


def pack_kernel(gate_up, down, out_w, gains, token, *refs):
    outs, sem = refs[:NY], refs[NY]
    y = lax.axis_index("y")
    copies = []
    feats = down.shape[0]
    units = down.shape[1] // NY
    for s in range(NY):
        place = lax.rem(y + s, NY)
        cols = pl.ds(pl.multiple_of(place * units, units), units)
        sources = [gate_up.at[0, :, cols], gate_up.at[1, :, cols], down.at[:, cols], out_w, gains]
        at = 0
        for j, source in enumerate(sources):
            size = source.shape[0]
            copies.append(pltpu.make_async_copy(source, outs[s].at[pl.ds(at, size)], sem.at[s, j]))
            at += size
    for copy in copies:
        copy.start()
    for copy in copies:
        copy.wait()


def sort_kernel(*refs):
    pieces, (ffn, out_w), sem = refs[:NY], refs[NY : NY + 2], refs[NY + 2]
    y = lax.axis_index("y")
    copies = []
    size = ffn.shape[1]
    rest = out_w.shape[1]
    for s in range(NY):
        place = lax.rem(y - s + NY, NY)
        copies.append(pltpu.make_async_copy(pieces[s].at[pl.ds(size, rest)], out_w.at[place], sem.at[s, 0]))
        copies.append(pltpu.make_async_copy(pieces[s].at[pl.ds(0, size)], ffn.at[place], sem.at[s, 1]))
    for copy in copies:
        copy.start()
    for copy in copies:
        copy.wait()


def project_kernel(h_own, h_mate, w_own, w_mate, out, token, hbuf, wbuf, rows_buf):
    core = lax.axis_index("c")
    hbuf[core] = h_own[...].astype(F32)
    hbuf[1 - core] = h_mate[...].astype(F32)
    wbuf[core] = w_own[...]
    wbuf[1 - core] = w_mate[...]
    rows_buf[...] = jnp.concatenate([hbuf[0].T, hbuf[1].T], axis=1)
    blocks, rows, _ = out.shape
    width = w_own.shape[2]
    chosen = jnp.concatenate(
        [
            rows_buf[pl.ds(pl.multiple_of((2 * b + core) * rows, rows), rows), :]
            for b in range(blocks)
        ],
        axis=0,
    ).astype(BF16)
    for g in range(3):
        weights = jnp.concatenate([wbuf[0, g], wbuf[1, g]], axis=0)
        part = jnp.dot(chosen, weights, preferred_element_type=F32).astype(BF16)
        out[:, :, g * width : (g + 1) * width] = part.reshape(blocks, rows, width)
    out[:, :, 3 * width :] = chosen.reshape(blocks, rows, chosen.shape[1])
    token[...] = jnp.zeros(token.shape, F32)


def collect_kernel(got, qk, value, squares, rest):
    x = lax.axis_index("x")
    rows, width = value.shape
    total = got[0, :, : 3 * width].astype(F32)
    for i in range(1, got.shape[0]):
        total += got[i, :, : 3 * width].astype(F32)
    q = total[:, :width]
    k = total[:, width : 2 * width]
    qk[0] = q
    qk[1] = k
    value[...] = total[:, 2 * width :].astype(BF16)
    lane = lax.broadcasted_iota(jnp.int32, squares.shape, 1)
    squares[...] = jnp.where(
        lane < 64, jnp.sum(q * q, axis=1, keepdims=True), jnp.sum(k * k, axis=1, keepdims=True)
    )
    step = width // NY
    for j in range(NY):
        rest[:, j * step : (j + 1) * step] = got[x * NY + j, :, 3 * width :]


def turn(values, cosine, sine):
    heads = values.shape[1] // HEAD_DIM
    parts = []
    for h in range(heads):
        v = values[:, h * HEAD_DIM : (h + 1) * HEAD_DIM]
        parts.append(v * cosine + pltpu.roll(v, HEAD_DIM // 2, 1) * sine)
    return jnp.concatenate(parts, axis=1)


def spread(values, heads):
    rows, width = values.shape
    wide = rows * heads
    row_head = lax.broadcasted_iota(jnp.int32, (wide, width), 0) // rows
    col_head = lax.broadcasted_iota(jnp.int32, (wide, width), 1) // HEAD_DIM
    return jnp.where(row_head == col_head, jnp.concatenate([values] * heads, axis=0), 0.0)


def used_rows(lengths, rows):
    used = lengths[0]
    for r in range(1, rows):
        used = used + lengths[r]
    return used


def score_kernel(lengths, qk, gains, tables, bounds, keys, score, top, turned, kbuf, sem):
    rows, width = turned.shape
    heads = width // HEAD_DIM
    blocks = score.shape[0]
    used = used_rows(lengths, rows)

    def fetch(i):
        return pltpu.make_async_copy(keys.at[pl.ds(i * BLOCK, BLOCK)], kbuf.at[i], sem.at[i])

    for i in range(blocks):
        @pl.when(i * BLOCK < used)
        def _():
            fetch(i).start()

    q = turn(qk[0] * gains[0:1, :], tables[0], tables[1]).astype(BF16)
    turned[...] = q
    q_block = spread(q.astype(F32), heads).astype(BF16)
    starts = bounds[:, 0:1]
    ends = bounds[:, 1:2]
    top[...] = jnp.full(top.shape, -jnp.inf, F32)
    for i in range(blocks):
        @pl.when(i * BLOCK < used)
        def _():
            fetch(i).wait()
            s = lax.dot_general(q_block, kbuf[i], NT, preferred_element_type=F32)
            place = lax.broadcasted_iota(jnp.int32, s.shape, 1) + i * BLOCK
            s = jnp.where((place >= starts) & (place < ends), s, -jnp.inf)
            score[i] = s
            top[...] = jnp.maximum(top[...], jnp.max(s, axis=1, keepdims=True))


def attend_kernel(lengths, sq0, sq1, sq2, sq3, qk, turned, value, gains, tables, score, top, values, *refs):
    pieces = refs[: 2 * NZ]
    key_out, partial, gain_out = refs[2 * NZ : 2 * NZ + 3]
    vbuf, wbuf, acc, total, vsem, wsem = refs[2 * NZ + 3 :]
    rows, width = turned.shape
    heads = width // HEAD_DIM
    blocks = score.shape[0]
    model = width * NX
    used = used_rows(lengths, rows)
    z = lax.axis_index("z")
    core = lax.axis_index("c")

    def fetch(i):
        return pltpu.make_async_copy(values.at[pl.ds(i * BLOCK, BLOCK)], vbuf.at[i], vsem.at[i])

    for i in range(blocks):
        @pl.when(i * BLOCK < used)
        def _():
            fetch(i).start()
    copies = []
    for s in range(NZ):
        place = lax.rem(z - s + NZ, NZ)
        copies.append(pltpu.make_async_copy(pieces[2 * s], wbuf.at[place, core], wsem.at[s, 0]))
        copies.append(pltpu.make_async_copy(pieces[2 * s + 1], wbuf.at[place, 1 - core], wsem.at[s, 1]))
    for copy in copies:
        copy.start()

    squares = sq0[...] + sq1[...] + sq2[...] + sq3[...]
    q_factor = lax.rsqrt(squares[:, 0:1] / model + EPS)
    k_factor = lax.rsqrt(squares[:, 64:65] / model + EPS)
    new_key = turn(qk[1] * k_factor * gains[1:2, :], tables[0], tables[1]).astype(BF16)
    key_out[...] = new_key
    factor = jnp.concatenate([q_factor] * heads, axis=0) * HEAD_DIM ** (-0.5)
    q_all = spread(turned[...].astype(F32), heads)
    k_all = jnp.concatenate([new_key.astype(F32)] * heads, axis=0)
    v_all = jnp.concatenate([value[...].astype(F32)] * heads, axis=0)
    own = jnp.sum(q_all * k_all, axis=1, keepdims=True) * factor
    highest = jnp.maximum(own, top[:, 0:1] * factor)
    own_weight = jnp.exp(own - highest).astype(BF16).astype(F32)
    total[...] = jnp.broadcast_to(own_weight, total.shape)
    acc[...] = own_weight * v_all
    for i in range(blocks):
        @pl.when(i * BLOCK < used)
        def _():
            fetch(i).wait()
            w = jnp.exp(score[i] * factor - highest).astype(BF16)
            total[...] += jnp.sum(w.astype(F32), axis=1, keepdims=True)
            acc[...] += jnp.dot(w, vbuf[i], preferred_element_type=F32)
    result = acc[...] / total[:, 0:1]
    attended = jnp.concatenate(
        [
            result[h * rows : (h + 1) * rows, h * HEAD_DIM : (h + 1) * HEAD_DIM]
            for h in range(heads)
        ],
        axis=1,
    ).astype(BF16)
    for copy in copies:
        copy.wait()
    feats = width // (NY * NC)
    for b in range(NZ):
        weights = jnp.concatenate(
            [wbuf[b, c, y, :feats] for y in range(NY) for c in range(NC)], axis=0
        )
        partial[b] = lax.dot_general(attended, weights, NT, preferred_element_type=F32)
        both = wbuf[b, 0, 0, feats:].astype(F32)
        for y in range(NY):
            for c in range(NC):
                if y or c:
                    both += wbuf[b, c, y, feats:].astype(F32)
        gain_out[b, 0:1] = both[0:1] + both[1:2]
        gain_out[b, 1:2] = both[2:3] + both[3:4]


def fan_kernel(got, rest, out):
    total = got[0] + got[1] + got[2] + got[3]
    message = jnp.concatenate([total.astype(BF16), rest[...]], axis=1)
    for i in range(out.shape[0]):
        out[i] = message


def ffn_kernel(got, gains, w_hbm, own_mid, out, wbuf, mid_buf, sem):
    width = got.shape[2] // 2
    model = width * NX
    place = lax.axis_index("y") * NX + lax.axis_index("x")
    copies = [
        pltpu.make_async_copy(w_hbm.at[g], wbuf.at[g], sem.at[g]) for g in range(w_hbm.shape[0])
    ]
    for copy in copies:
        copy.start()

    def block(x, part):
        return jnp.concatenate(
            [got[y * NX + x, :, part * width : (part + 1) * width] for y in range(NY)], axis=0
        ).astype(F32)

    branch = [block(x, 0) for x in range(NX)]
    power = jnp.sum(branch[0] * branch[0], axis=1, keepdims=True)
    for x in range(1, NX):
        power += jnp.sum(branch[x] * branch[x], axis=1, keepdims=True)
    factor = lax.rsqrt(power / model + EPS)
    mid = []
    for x in range(NX):
        m = (block(x, 1) + branch[x] * factor * gains[x, 0:1]).astype(BF16)
        mid_buf[:, x * width : (x + 1) * width] = m.astype(F32)
        mid.append(m)
    feats = wbuf.shape[2] // 3

    def weights(z, part):
        return jnp.concatenate(
            [
                wbuf[z * NC + c, y, part * feats : (part + 1) * feats]
                for y in range(NY)
                for c in range(NC)
            ],
            axis=0,
        )

    gate = lift = None
    for z in range(NZ):
        copies[2 * z].wait()
        copies[2 * z + 1].wait()
        g = jnp.dot(mid[z], weights(z, 0), preferred_element_type=F32)
        u = jnp.dot(mid[z], weights(z, 1), preferred_element_type=F32)
        gate = g if gate is None else gate + g
        lift = u if lift is None else lift + u
    act = (gate / (1.0 + jnp.exp(-gate)) * lift).astype(BF16)
    own = out.shape[1]
    for z in range(NZ):
        f = lax.dot_general(act, weights(z, 2), NT, preferred_element_type=F32)
        for d in range(out.shape[0]):
            out[d, :, z * width : (z + 1) * width] = f[d * own : (d + 1) * own]
    pair = mid_buf[pl.ds(pl.multiple_of(place // 2 * 8, 8), 8), :]
    own_mid[...] = jnp.where(lax.rem(place, 2) == 0, pair[:own], pair[own:])


def finish_kernel(got, own_mid, gains, out):
    total = got[0]
    for i in range(1, got.shape[0]):
        total += got[i]
    model = total.shape[1]
    power = jnp.sum(total * total, axis=1, keepdims=True) / model
    gain = jnp.concatenate([gains[z, 1:2] for z in range(NZ)], axis=1)
    hidden = (own_mid[...] + total * lax.rsqrt(power + EPS) * gain).astype(BF16)
    feats = out.shape[2]
    for r in range(model // feats):
        part = hidden[:, r * feats : (r + 1) * feats]
        for x in range(NX):
            out[r * NX + x] = part


def ring(shift, size):
    return [(i, (i + shift) % size) for i in range(size)]


def body(hidden_in, lengths, w_qkv, qk_gain, cache_keys, cache_values, w_out, norm_gain,
         w_gate_up, w_down):
    rows = lengths.shape[0]
    width = w_qkv.shape[2]
    heads = width // HEAD_DIM
    feats = hidden_in.shape[1]
    model = width * NX
    wide = rows * heads
    blocks = cache_keys.shape[0] // BLOCK
    y_here = lax.axis_index("y")
    c_here = lax.axis_index("c")

    flipped = hidden_in.T
    mate_rows = lax.ppermute(flipped, "c", ring(1, NC))
    mate_w = lax.ppermute(w_qkv, "c", ring(1, NC))
    message, token = call(
        project_kernel,
        (shape((NZ * NY, rows, 3 * width + 2 * feats), BF16), shape((8, 128), F32)),
        [VMEM] * 4,
        (VMEM, VMEM),
        [
            pltpu.VMEM((2, feats, flipped.shape[1]), F32),
            pltpu.VMEM((2,) + w_qkv.shape, BF16),
            pltpu.VMEM((flipped.shape[1], 2 * feats), F32),
        ],
        (1 << 27, 2 << 20),
        "project",
    )(flipped, mate_rows, w_qkv, mate_w)
    got = lax.all_to_all(message, ("z", "y"), 0, 0, tiled=True)

    high = norm_gain.astype(BF16)
    low = (norm_gain - high.astype(F32)).astype(BF16)
    gain_rows = jnp.stack([high[0], low[0], high[1], low[1]])
    gain_tile = jnp.zeros((8, width), BF16)
    gain_tile = lax.dynamic_update_slice(
        gain_tile, gain_rows, (jnp.int32(0), (y_here * NC + c_here) * feats)
    )
    units = w_down.shape[1] // NY
    height = 4 * feats + 8
    pieces = call(
        pack_kernel,
        (shape((height, units), BF16),) * NY,
        [ANY] * 5,
        (ANY,) * NY,
        [pltpu.SemaphoreType.DMA((NY, 5))],
        (0, 2 << 20),
        "pack",
    )(w_gate_up, w_down, w_out, gain_tile, token)
    pieces = [pieces[0]] + [lax.ppermute(pieces[s], "y", ring(s, NY)) for s in range(1, NY)]
    ffn_part, out_part = call(
        sort_kernel,
        (shape((NY, 3 * feats, units), BF16), shape((NY, feats + 8, units), BF16)),
        [ANY] * NY,
        (ANY, ANY),
        [pltpu.SemaphoreType.DMA((NY, 2))],
        (0, 2 << 20),
        "sort",
    )(*pieces)
    ffn_weights = lax.all_gather(ffn_part, ("z", "c"), axis=0, tiled=False)
    out_pieces = []
    for s in range(NZ):
        piece = out_part if s == 0 else lax.ppermute(out_part, "z", ring(s, NZ))
        out_pieces += [piece, lax.ppermute(piece, "c", ring(1, NC))]

    qk, value_new, squares, rest = call(
        collect_kernel,
        (
            shape((2, rows, width), F32),
            shape((rows, width), BF16),
            shape((rows, 128), F32),
            shape((rows, width), BF16),
        ),
        [VMEM],
        (VMEM,) * 4,
        (),
        (1 << 20, 1 << 20),
        "collect",
    )(got)
    others = [lax.ppermute(squares, "x", ring(s, NX)) for s in range(1, NX)]
    half = HEAD_DIM // 2
    freqs = jnp.power(THETA, -(jnp.arange(half, dtype=F32) * 2.0 / HEAD_DIM))
    angles = lengths.astype(F32)[:, None] * freqs[None, :]
    cosine = jnp.cos(angles)
    sine = jnp.sin(angles)
    tables = jnp.stack(
        [jnp.concatenate([cosine, cosine], axis=1), jnp.concatenate([-sine, sine], axis=1)]
    )
    ends = jnp.cumsum(lengths)
    bounds = jnp.tile(jnp.stack([ends - lengths, ends], axis=1), (heads, 1))
    score, top, turned = call(
        score_kernel,
        (
            shape((blocks, wide, BLOCK), F32),
            shape((wide, 128), F32),
            shape((rows, width), BF16),
        ),
        [SMEM, VMEM, VMEM, VMEM, VMEM, HBM],
        (VMEM,) * 3,
        [pltpu.VMEM((blocks, BLOCK, width), BF16), pltpu.SemaphoreType.DMA((blocks,))],
        (1 << 28, 4 << 20),
        "score",
    )(lengths, qk, qk_gain, tables, bounds, cache_keys)
    key_new, partial, gains = call(
        attend_kernel,
        (
            shape((rows, width), BF16),
            shape((NX, rows, width), F32),
            shape((NZ, 8, width), F32),
        ),
        [SMEM] + [VMEM] * 11 + [HBM] + [ANY] * (2 * NZ),
        (VMEM,) * 3,
        [
            pltpu.VMEM((blocks, BLOCK, width), BF16),
            pltpu.VMEM((NZ, NC, NY, feats + 8, units), BF16),
            pltpu.VMEM((wide, width), F32),
            pltpu.VMEM((wide, 128), F32),
            pltpu.SemaphoreType.DMA((blocks,)),
            pltpu.SemaphoreType.DMA((NZ, 2)),
        ],
        (1 << 28, 6 << 20),
        "attend",
    )(lengths, squares, *others, qk, turned, value_new, qk_gain, tables, score, top, cache_values,
      *out_pieces)

    got = lax.all_to_all(partial, "x", 0, 0, tiled=True)
    message = call(
        fan_kernel,
        shape((NY * NX, rows, 2 * width), BF16),
        [VMEM] * 2,
        VMEM,
        (),
        (1 << 16, 1 << 19),
        "fan",
    )(got, rest)
    got = lax.all_to_all(message, ("y", "x"), 0, 0, tiled=True)
    mine = rows // NX
    own_mid, partial = call(
        ffn_kernel,
        (shape((mine, model), F32), shape((NY * NX, mine, model), F32)),
        [VMEM, VMEM, HBM],
        (VMEM, VMEM),
        [
            pltpu.VMEM(ffn_weights.shape, BF16),
            pltpu.VMEM((NY * rows, model), F32),
            pltpu.SemaphoreType.DMA((ffn_weights.shape[0],)),
        ],
        (1 << 28, 7 << 20),
        "feed_forward",
    )(got, gains, ffn_weights)
    got = lax.all_to_all(partial, ("y", "x"), 0, 0, tiled=True)
    message = call(
        finish_kernel,
        shape((NZ * NY * NC * NX, mine, feats), BF16),
        [VMEM] * 3,
        VMEM,
        (),
        (1 << 18, 1 << 19),
        "finish",
    )(got, own_mid, gains)
    hidden = lax.all_to_all(message, ("z", "y", "c", "x"), 0, 0, tiled=True)
    return hidden.reshape(-1, feats), key_new, value_new


def solution(mesh):
    fine = Mesh(mesh.devices.reshape(NZ, NY, NC, NX), ("z", "y", "c", "x"))
    req = ("z", "y", "c")
    return jax.shard_map(
        body,
        mesh=fine,
        in_specs=(
            P(None, req),
            P(req),
            P(None, req, "x"),
            P(None, "x"),
            P(req, "x"),
            P(req, "x"),
            P(req, "x"),
            P(None, req),
            P(None, req, "x"),
            P(req, "x"),
        ),
        out_specs=(P(None, req), P(req, "x"), P(req, "x")),
        check_vma=False,
    )
```

```python
import functools

import jax
import jax.numpy as jnp
from jax import lax
from jax.experimental import pallas as pl
from jax.experimental.pallas import tpu as pltpu
from jax.sharding import Mesh, PartitionSpec as P

HEAD_DIM = 128
EPS = 1e-06
THETA = 500000.0
NT = (((1,), (1,)), ((), ()))
BLOCK = 512
F32 = jnp.float32
BF16 = jnp.bfloat16
NZ, NY, NC, NX = 4, 4, 2, 4
VMEM = pl.BlockSpec(memory_space=pltpu.VMEM)
HBM = pl.BlockSpec(memory_space=pltpu.HBM)
ANY = pl.BlockSpec(memory_space=pl.ANY)
SMEM = pl.BlockSpec(memory_space=pltpu.SMEM)


def call(kernel, out_shape, in_specs, out_specs, scratch=(), cost=(1 << 20, 1 << 20), name=None, limit=4):
    return pl.pallas_call(
        kernel,
        out_shape=out_shape,
        in_specs=in_specs,
        out_specs=out_specs,
        scratch_shapes=list(scratch),
        compiler_params=pltpu.CompilerParams(vmem_limit_bytes=limit * 1024 * 1024),
        cost_estimate=pl.CostEstimate(flops=cost[0], bytes_accessed=cost[1], transcendentals=0),
        name=name,
    )


def hbm(array):
    return pltpu.with_memory_space_constraint(array, pltpu.HBM)


def shape(dims, dtype):
    return jax.ShapeDtypeStruct(dims, dtype)


def run(copies, sem):
    copies = [pltpu.make_async_copy(a, b, sem.at[i]) for i, (a, b) in enumerate(copies)]
    for copy in copies:
        copy.start()
    for copy in copies:
        copy.wait()


def pack_kernel(gate_up, down, token, *refs):
    outs, sem = refs[:NY], refs[NY]
    y = lax.axis_index("y")
    feats = down.shape[0]
    units = down.shape[1] // NY
    copies = []
    for s in range(NY):
        cols = pl.ds(pl.multiple_of(lax.rem(y + s, NY) * units, units), units)
        for part in range(3):
            source = down.at[:, cols] if part == 2 else gate_up.at[part, :, cols]
            copies.append((source, outs[s].at[pl.ds(part * feats, feats)]))
    run(copies, sem)


def sort_kernel(*refs):
    pieces, (out, sem) = refs[:NY], refs[NY + 1 :]
    y = lax.axis_index("y")
    run([(pieces[s], out.at[lax.rem(y + NY - s, NY)]) for s in range(NY)], sem)


def sort(pieces, token, name):
    return call(
        sort_kernel,
        shape((NY,) + pieces[0].shape, BF16),
        [ANY] * (NY + 1),
        ANY,
        [pltpu.SemaphoreType.DMA((NY,))],
        (0, 1 << 20),
        name,
        1,
    )(*pieces, token)


def join_kernel(first, second, token, out, sem):
    half = first.shape[0]
    run([(first, out.at[pl.ds(0, half)]), (second, out.at[pl.ds(half, half)])], sem)


def join(first, second, token):
    return call(
        join_kernel,
        shape((2 * first.shape[0],) + first.shape[1:], first.dtype),
        [ANY] * 3,
        ANY,
        [pltpu.SemaphoreType.DMA((2,))],
        (0, 1 << 20),
        "join",
        1,
    )(first, second, token)


def halves_kernel(up, dn, token, up_half, dn_half, sem):
    half = up_half.shape[0]
    copies = [
        pltpu.make_async_copy(up.at[pl.ds(0, half)], up_half, sem.at[0]),
        pltpu.make_async_copy(dn.at[pl.ds(half, half)], dn_half, sem.at[1]),
    ]
    for copy in copies:
        copy.start()
    for copy in copies:
        copy.wait()


def halves(up, dn, token):
    out = shape((up.shape[0] // 2,) + up.shape[1:], up.dtype)
    return call(
        halves_kernel,
        (out, out),
        [ANY] * 3,
        (ANY, ANY),
        [pltpu.SemaphoreType.DMA((2,))],
        (0, 1 << 20),
        "halves",
        1,
    )(up, dn, token)


def piece_copies(pieces, buf, sem):
    z = lax.axis_index("z")
    core = lax.axis_index("c")
    copies = []
    for m in range(NC):
        c = core if m == 0 else 1 - core
        for i, shift in enumerate((0, NZ - 1, 1, 2)):
            target = buf.at[lax.rem(z + shift, NZ), c]
            copies.append(pltpu.make_async_copy(pieces[m * 4 + i], target, sem.at[m, i]))
    return copies


def project_kernel(h_own, h_mate, w_own, w_mate, out, token, hbuf, wbuf, rows_buf, sem):
    core = lax.axis_index("c")
    copies = [
        pltpu.make_async_copy(w_own, wbuf.at[core], sem.at[0]),
        pltpu.make_async_copy(w_mate, wbuf.at[1 - core], sem.at[1]),
        pltpu.make_async_copy(h_own, hbuf.at[core], sem.at[2]),
        pltpu.make_async_copy(h_mate, hbuf.at[1 - core], sem.at[3]),
    ]
    for copy in copies:
        copy.start()
    copies[2].wait()
    copies[3].wait()
    rows_buf[...] = jnp.concatenate([hbuf[0].astype(F32).T, hbuf[1].astype(F32).T], axis=1)
    blocks, rows, _ = out.shape
    width = w_own.shape[2]
    chosen = jnp.concatenate(
        [
            rows_buf[pl.ds(pl.multiple_of((2 * b + core) * rows, rows), rows), :]
            for b in range(blocks)
        ],
        axis=0,
    ).astype(BF16)
    copies[0].wait()
    copies[1].wait()
    for g in range(3):
        weights = jnp.concatenate([wbuf[0, g], wbuf[1, g]], axis=0)
        part = jnp.dot(chosen, weights, preferred_element_type=F32).astype(BF16)
        out[:, :, g * width : (g + 1) * width] = part.reshape(blocks, rows, width)
    out[:, :, 3 * width :] = chosen.reshape(blocks, rows, chosen.shape[1])
    token[...] = jnp.zeros(token.shape, F32)


def quarter(ref, x):
    pair = ref[pl.ds(pl.multiple_of(x // 2 * 8, 8), 8), :]
    return jnp.where(lax.rem(x, 2) == 0, pair[:4], pair[4:])


def collect_kernel(got, qk, value, squares, rest, rest_buf):
    rows, width = value.shape
    total = got[0, :, : 3 * width].astype(F32)
    for i in range(1, got.shape[0]):
        total += got[i, :, : 3 * width].astype(F32)
    q = total[:, :width]
    k = total[:, width : 2 * width]
    qk[0] = q
    qk[1] = k
    value[...] = total[:, 2 * width :].astype(BF16)
    lane = lax.broadcasted_iota(jnp.int32, squares.shape[1:], 1)
    both = jnp.where(
        lane < 64, jnp.sum(q * q, axis=1, keepdims=True), jnp.sum(k * k, axis=1, keepdims=True)
    )
    for i in range(NX):
        squares[i] = both
    step = got.shape[2] - 3 * width
    for i in range(got.shape[0]):
        rest_buf[:, i * step : (i + 1) * step] = got[i, :, 3 * width :].astype(F32)
    rest[...] = quarter(rest_buf, lax.axis_index("x"))


def turn(values, cosine, sine):
    heads = values.shape[1] // HEAD_DIM
    parts = []
    for h in range(heads):
        v = values[:, h * HEAD_DIM : (h + 1) * HEAD_DIM]
        parts.append(v * cosine + pltpu.roll(v, HEAD_DIM // 2, 1) * sine)
    return jnp.concatenate(parts, axis=1)


def spread(values, heads):
    rows, width = values.shape
    wide = rows * heads
    row_head = lax.broadcasted_iota(jnp.int32, (wide, width), 0) // rows
    col_head = lax.broadcasted_iota(jnp.int32, (wide, width), 1) // HEAD_DIM
    return jnp.where(row_head == col_head, jnp.concatenate([values] * heads, axis=0), 0.0)


def used_rows(lengths, rows):
    used = lengths[0]
    for r in range(1, rows):
        used = used + lengths[r]
    return used


def score_kernel(lengths, qk, gains, tables, bounds, keys, score, top, turned, kbuf, sem):
    rows, width = turned.shape
    heads = width // HEAD_DIM
    blocks = score.shape[0]
    used = used_rows(lengths, rows)

    def fetch(i):
        return pltpu.make_async_copy(keys.at[pl.ds(i * BLOCK, BLOCK)], kbuf.at[i], sem.at[i])

    for i in range(blocks):
        @pl.when(i * BLOCK < used)
        def _():
            fetch(i).start()

    q = turn(qk[0] * gains[0:1, :], tables[0], tables[1]).astype(BF16)
    turned[...] = q
    q_block = spread(q.astype(F32), heads).astype(BF16)
    starts = bounds[:, 0:1]
    ends = bounds[:, 1:2]
    top[...] = jnp.full(top.shape, -jnp.inf, F32)
    for i in range(blocks):
        @pl.when(i * BLOCK < used)
        def _():
            fetch(i).wait()
            s = lax.dot_general(q_block, kbuf[i], NT, preferred_element_type=F32)
            place = lax.broadcasted_iota(jnp.int32, s.shape, 1) + i * BLOCK
            s = jnp.where((place >= starts) & (place < ends), s, -jnp.inf)
            score[i] = s
            top[...] = jnp.maximum(top[...], jnp.max(s, axis=1, keepdims=True))


def attend_kernel(lengths, squares_in, qk, turned, value, gains, tables, score, top, values, *refs):
    pieces = refs[: 4 * NC]
    key_out, partial, gain_out = refs[4 * NC : 4 * NC + 3]
    vbuf, wbuf, acc, total, vsem, wsem = refs[4 * NC + 3 :]
    rows, width = turned.shape
    heads = width // HEAD_DIM
    blocks = score.shape[0]
    model = width * NX
    used = used_rows(lengths, rows)

    def fetch(i):
        return pltpu.make_async_copy(values.at[pl.ds(i * BLOCK, BLOCK)], vbuf.at[i], vsem.at[i])

    for i in range(blocks):
        @pl.when(i * BLOCK < used)
        def _():
            fetch(i).start()
    copies = piece_copies(pieces, wbuf, wsem)
    for copy in copies:
        copy.start()

    squares = squares_in[0] + squares_in[1] + squares_in[2] + squares_in[3]
    q_factor = lax.rsqrt(squares[:, 0:1] / model + EPS)
    k_factor = lax.rsqrt(squares[:, 64:65] / model + EPS)
    new_key = turn(qk[1] * k_factor * gains[1:2, :], tables[0], tables[1]).astype(BF16)
    key_out[...] = new_key
    factor = jnp.concatenate([q_factor] * heads, axis=0) * HEAD_DIM ** (-0.5)
    q_all = spread(turned[...].astype(F32), heads)
    k_all = jnp.concatenate([new_key.astype(F32)] * heads, axis=0)
    v_all = jnp.concatenate([value[...].astype(F32)] * heads, axis=0)
    own = jnp.sum(q_all * k_all, axis=1, keepdims=True) * factor
    highest = jnp.maximum(own, top[:, 0:1] * factor)
    own_weight = jnp.exp(own - highest).astype(BF16).astype(F32)
    total[...] = jnp.broadcast_to(own_weight, total.shape)
    acc[...] = own_weight * v_all
    for i in range(blocks):
        @pl.when(i * BLOCK < used)
        def _():
            fetch(i).wait()
            w = jnp.exp(score[i] * factor - highest).astype(BF16)
            total[...] += jnp.sum(w.astype(F32), axis=1, keepdims=True)
            acc[...] += jnp.dot(w, vbuf[i], preferred_element_type=F32)
    result = acc[...] / total[:, 0:1]
    attended = jnp.concatenate(
        [
            result[h * rows : (h + 1) * rows, h * HEAD_DIM : (h + 1) * HEAD_DIM]
            for h in range(heads)
        ],
        axis=1,
    ).astype(BF16)
    for copy in copies:
        copy.wait()
    feats = width // (NY * NC)
    for b in range(NZ):
        weights = jnp.concatenate(
            [wbuf[b, c, y, :feats] for y in range(NY) for c in range(NC)], axis=0
        )
        a = lax.dot_general(attended, weights, NT, preferred_element_type=F32)
        mine = rows // NX
        for x in range(NX):
            partial[x, :, b * width : (b + 1) * width] = a[x * mine : (x + 1) * mine]
        both = wbuf[b, 0, 0, feats:].astype(F32)
        for y in range(NY):
            for c in range(NC):
                if y or c:
                    both += wbuf[b, c, y, feats:].astype(F32)
        gain_out[b, 0:1] = both[0:1] + both[1:2]
        gain_out[b, 1:2] = both[2:3] + both[3:4]


def fan_kernel(got, rest, gains, own_mid, out):
    total = got[0] + got[1] + got[2] + got[3]
    model = total.shape[1]
    power = jnp.sum(total * total, axis=1, keepdims=True) / model
    gain = jnp.concatenate([gains[z, 0:1] for z in range(NZ)], axis=1)
    mid = (rest[...] + total * lax.rsqrt(power + EPS) * gain).astype(BF16)
    mid32 = mid.astype(F32)
    own_mid[...] = mid32
    message = jnp.concatenate([mid32[:, : model // 2], mid32[:, model // 2 :]], axis=0).astype(BF16)
    for i in range(out.shape[0]):
        out[i] = message


def ffn_kernel(got, *refs):
    pieces = refs[: 4 * NC]
    out, wbuf, sem = refs[4 * NC :]
    copies = piece_copies(pieces, wbuf, sem)
    for copy in copies:
        copy.start()
    places, lines, span = got.shape
    mine = lines // 2
    width = span // 2
    whole = [got[d].astype(F32) for d in range(places)]

    def features(z):
        half, at = z // 2, (z % 2) * width
        return jnp.concatenate(
            [w[half * mine : (half + 1) * mine, at : at + width] for w in whole], axis=0
        ).astype(BF16)

    feats = wbuf.shape[3] // 3

    def weights(z, part):
        return jnp.concatenate(
            [
                wbuf[z, c, y, part * feats : (part + 1) * feats]
                for y in range(NY)
                for c in range(NC)
            ],
            axis=0,
        )

    for copy in copies:
        copy.wait()
    gate = lift = None
    for z in range(NZ):
        mid = features(z)
        g = jnp.dot(mid, weights(z, 0), preferred_element_type=F32)
        u = jnp.dot(mid, weights(z, 1), preferred_element_type=F32)
        gate = g if gate is None else gate + g
        lift = u if lift is None else lift + u
    act = (gate / (1.0 + jnp.exp(-gate)) * lift).astype(BF16)
    for z in range(NZ):
        f = lax.dot_general(act, weights(z, 2), NT, preferred_element_type=F32)
        half, at = z // 2, (z % 2) * width
        for d in range(places):
            out[d, half * mine : (half + 1) * mine, at : at + width] = f[d * mine : (d + 1) * mine]


def finish_kernel(got, own_mid, gains, out):
    total = got[0]
    for i in range(1, got.shape[0]):
        total += got[i]
    mine = own_mid.shape[0]
    total = jnp.concatenate([total[:mine], total[mine:]], axis=1)
    model = total.shape[1]
    power = jnp.sum(total * total, axis=1, keepdims=True) / model
    gain = jnp.concatenate([gains[z, 1:2] for z in range(NZ)], axis=1)
    hidden = (own_mid[...] + total * lax.rsqrt(power + EPS) * gain).astype(BF16)
    feats = out.shape[2]
    for r in range(model // feats):
        part = hidden[:, r * feats : (r + 1) * feats]
        for x in range(NX):
            out[r * NX + x] = part


def ring(shift, size):
    return [(i, (i + shift) % size) for i in range(size)]


def body(hidden_in, lengths, w_qkv, qk_gain, cache_keys, cache_values, w_out, norm_gain,
         w_gate_up, w_down):
    rows = lengths.shape[0]
    width = w_qkv.shape[2]
    heads = width // HEAD_DIM
    feats = hidden_in.shape[1]
    model = width * NX
    wide = rows * heads
    blocks = cache_keys.shape[0] // BLOCK
    y_here = lax.axis_index("y")
    c_here = lax.axis_index("c")

    flipped = hidden_in.T
    mate_rows = lax.ppermute(flipped, "c", ring(1, NC))
    mate_w = lax.ppermute(w_qkv, "c", ring(1, NC))
    message, started = call(
        project_kernel,
        (shape((NZ * NY, rows, 3 * width + 2 * feats), BF16), shape((8, 128), F32)),
        [ANY] * 4,
        (VMEM, VMEM),
        [
            pltpu.VMEM((2, feats, flipped.shape[1]), BF16),
            pltpu.VMEM((2,) + w_qkv.shape, BF16),
            pltpu.VMEM((flipped.shape[1], 2 * feats), F32),
            pltpu.SemaphoreType.DMA((4,)),
        ],
        (1 << 27, 2 << 20),
        "project",
        8,
    )(hbm(flipped), mate_rows, hbm(w_qkv), mate_w)
    got = lax.all_to_all(message, ("z", "y"), 0, 0, tiled=True)

    high = norm_gain.astype(BF16)
    low = (norm_gain - high.astype(F32)).astype(BF16)
    gain_rows = jnp.stack([high[0], low[0], high[1], low[1]])
    gain_tile = jnp.zeros((8, width), BF16)
    gain_tile = lax.dynamic_update_slice(
        gain_tile, gain_rows, (jnp.int32(0), (y_here * NC + c_here) * feats)
    )
    out_part = jnp.concatenate([w_out, gain_tile], axis=0)
    out_part = [out_part] + [lax.ppermute(out_part, "y", ring(s, NY)) for s in range(1, NY)]
    out_part = sort(out_part, started, "sort_out")
    units = w_down.shape[1] // NY
    ffn_part = call(
        pack_kernel,
        (shape((3 * feats, units), BF16),) * NY,
        [ANY] * 3,
        (ANY,) * NY,
        [pltpu.SemaphoreType.DMA((3 * NY,))],
        (0, 2 << 20),
        "pack",
        1,
    )(hbm(w_gate_up), hbm(w_down), started)
    ffn_part = [ffn_part[0]] + [lax.ppermute(ffn_part[s], "y", ring(s, NY)) for s in range(1, NY)]

    def near(part):
        return lax.ppermute(part, "z", ring(1, NZ)), lax.ppermute(part, "z", ring(-1, NZ))

    def far(up, dn, token):
        up_half, dn_half = halves(up, dn, token)
        return (
            lax.ppermute(up_half, "z", ring(1, NZ)),
            lax.ppermute(dn_half, "z", ring(-1, NZ)),
        )

    def both(pieces):
        return pieces + [lax.ppermute(p, "c", ring(1, NC)) for p in pieces]

    out_near = near(out_part)
    out_far = far(*out_near, started)

    qk, value_new, squares, rest = call(
        collect_kernel,
        (
            shape((2, rows, width), F32),
            shape((rows, width), BF16),
            shape((NX, rows, 128), F32),
            shape((rows // NX, model), F32),
        ),
        [VMEM],
        (VMEM,) * 4,
        [pltpu.VMEM((rows, model), F32)],
        (1 << 20, 1 << 20),
        "collect",
    )(got)
    ffn_part = sort(ffn_part, squares, "sort_ffn")
    ffn_near = near(ffn_part)
    squares = lax.all_to_all(squares, "x", 0, 0, tiled=True)
    half = HEAD_DIM // 2
    freqs = jnp.power(THETA, -(jnp.arange(half, dtype=F32) * 2.0 / HEAD_DIM))
    angles = lengths.astype(F32)[:, None] * freqs[None, :]
    cosine = jnp.cos(angles)
    sine = jnp.sin(angles)
    tables = jnp.stack(
        [jnp.concatenate([cosine, cosine], axis=1), jnp.concatenate([-sine, sine], axis=1)]
    )
    ends = jnp.cumsum(lengths)
    bounds = jnp.tile(jnp.stack([ends - lengths, ends], axis=1), (heads, 1))
    score, top, turned = call(
        score_kernel,
        (
            shape((blocks, wide, BLOCK), F32),
            shape((wide, 128), F32),
            shape((rows, width), BF16),
        ),
        [SMEM, VMEM, VMEM, VMEM, VMEM, HBM],
        (VMEM,) * 3,
        [pltpu.VMEM((blocks, BLOCK, width), BF16), pltpu.SemaphoreType.DMA((blocks,))],
        (1 << 28, 4 << 20),
        "score",
        8,
    )(lengths, qk, qk_gain, tables, bounds, hbm(cache_keys))
    out_pieces = both([out_part, *out_near, join(*out_far, top)])
    key_new, partial, gains = call(
        attend_kernel,
        (
            shape((rows, width), BF16),
            shape((NX, rows // NX, model), F32),
            shape((NZ, 8, width), F32),
        ),
        [SMEM] + [VMEM] * 8 + [HBM] + [ANY] * (4 * NC),
        (VMEM,) * 3,
        [
            pltpu.VMEM((blocks, BLOCK, width), BF16),
            pltpu.VMEM((NZ, NC, NY, feats + 8, units), BF16),
            pltpu.VMEM((wide, width), F32),
            pltpu.VMEM((wide, 128), F32),
            pltpu.SemaphoreType.DMA((blocks,)),
            pltpu.SemaphoreType.DMA((NC, 4)),
        ],
        (1 << 28, 6 << 20),
        "attend",
        12,
    )(lengths, squares, qk, turned, value_new, qk_gain, tables, score, top, hbm(cache_values),
      *out_pieces)

    ffn_far = far(*ffn_near, gains)

    got = lax.all_to_all(partial, "x", 0, 0, tiled=True)
    mine = rows // NX
    own_mid, message = call(
        fan_kernel,
        (shape((mine, model), F32), shape((NY * NX, 2 * mine, model // 2), BF16)),
        [VMEM] * 3,
        (VMEM, VMEM),
        (),
        (1 << 16, 1 << 19),
        "fan",
    )(got, rest, gains)
    got = lax.all_to_all(message, ("y", "x"), 0, 0, tiled=True)
    ffn_pieces = both([ffn_part, *ffn_near, join(*ffn_far, own_mid)])
    partial = call(
        ffn_kernel,
        shape((NY * NX, 2 * mine, model // 2), F32),
        [VMEM] + [ANY] * (4 * NC),
        VMEM,
        [
            pltpu.VMEM((NZ, NC) + ffn_part.shape, BF16),
            pltpu.SemaphoreType.DMA((NC, 4)),
        ],
        (1 << 28, 7 << 20),
        "feed_forward",
        16,
    )(got, *ffn_pieces)
    got = lax.all_to_all(partial, ("y", "x"), 0, 0, tiled=True)
    message = call(
        finish_kernel,
        shape((NZ * NY * NC * NX, mine, feats), BF16),
        [VMEM] * 3,
        VMEM,
        (),
        (1 << 18, 1 << 19),
        "finish",
    )(got, own_mid, gains)
    hidden = lax.all_to_all(message, ("z", "y", "c", "x"), 0, 0, tiled=True)
    return hidden.reshape(-1, feats), key_new, value_new


def solution(mesh):
    fine = Mesh(mesh.devices.reshape(NZ, NY, NC, NX), ("z", "y", "c", "x"))
    req = ("z", "y", "c")
    return jax.shard_map(
        body,
        mesh=fine,
        in_specs=(
            P(None, req),
            P(req),
            P(None, req, "x"),
            P(None, "x"),
            P(req, "x"),
            P(req, "x"),
            P(req, "x"),
            P(None, req),
            P(None, req, "x"),
            P(req, "x"),
        ),
        out_specs=(P(None, req), P(req, "x"), P(req, "x")),
        check_vma=False,
    )
```

```python
import functools

import jax
import jax.numpy as jnp
from jax import lax
from jax.experimental import pallas as pl
from jax.experimental.pallas import tpu as pltpu
from jax.sharding import Mesh, PartitionSpec as P

HEAD_DIM = 128
EPS = 1e-06
THETA = 500000.0
NT = (((1,), (1,)), ((), ()))
BLOCK = 512
F32 = jnp.float32
BF16 = jnp.bfloat16
NZ, NY, NC, NX = 4, 4, 2, 4
X = ("xh", "xl")
VMEM = pl.BlockSpec(memory_space=pltpu.VMEM)
HBM = pl.BlockSpec(memory_space=pltpu.HBM)
ANY = pl.BlockSpec(memory_space=pl.ANY)
SMEM = pl.BlockSpec(memory_space=pltpu.SMEM)


def call(kernel, out_shape, in_specs, out_specs, scratch=(), cost=(1 << 20, 1 << 20), name=None, limit=4):
    return pl.pallas_call(
        kernel,
        out_shape=out_shape,
        in_specs=in_specs,
        out_specs=out_specs,
        scratch_shapes=list(scratch),
        compiler_params=pltpu.CompilerParams(vmem_limit_bytes=limit * 1024 * 1024),
        cost_estimate=pl.CostEstimate(flops=cost[0], bytes_accessed=cost[1], transcendentals=0),
        name=name,
    )


def hbm(array):
    return pltpu.with_memory_space_constraint(array, pltpu.HBM)


def shape(dims, dtype):
    return jax.ShapeDtypeStruct(dims, dtype)


def run(copies, sem):
    copies = [pltpu.make_async_copy(a, b, sem.at[i]) for i, (a, b) in enumerate(copies)]
    for copy in copies:
        copy.start()
    for copy in copies:
        copy.wait()


def sort_kernel(*refs):
    pieces, (out, sem) = refs[:NY], refs[NY:]
    y = lax.axis_index("y")
    run([(pieces[s], out.at[lax.rem(y + NY - s, NY)]) for s in range(NY)], sem)


def join_kernel(*refs):
    out, sem = refs[-2:]
    pieces = refs[:-3]
    run([(piece, out.at[i]) for i, piece in enumerate(pieces)], sem)


def join(pieces, token, name):
    return call(
        join_kernel,
        shape((len(pieces),) + pieces[0].shape, BF16),
        [ANY] * (len(pieces) + 1),
        ANY,
        [pltpu.SemaphoreType.DMA((len(pieces),))],
        (0, 2 << 20),
        name,
        1,
    )(*pieces, token)


def piece_copies(pieces, buf, sem):
    z = lax.axis_index("z")
    core = lax.axis_index("c")
    copies = []
    for m in range(NC):
        c = core if m == 0 else 1 - core
        for i, shift in enumerate((0, NZ - 1, NZ - 2, NZ - 3)):
            target = buf.at[lax.rem(z + shift, NZ), c]
            copies.append(pltpu.make_async_copy(pieces[m].at[i], target, sem.at[m, i]))
    return copies


def project_kernel(h_own, h_mate, w_own, w_mate, gate_up, down, out, hbuf, wbuf, rows_buf, gbuf, dbuf, sem):
    core = lax.axis_index("c")
    copies = [
        pltpu.make_async_copy(h_own, hbuf.at[core], sem.at[0]),
        pltpu.make_async_copy(h_mate, hbuf.at[1 - core], sem.at[1]),
        pltpu.make_async_copy(w_own, wbuf.at[core], sem.at[2]),
        pltpu.make_async_copy(w_mate, wbuf.at[1 - core], sem.at[3]),
        pltpu.make_async_copy(gate_up, gbuf, sem.at[4]),
        pltpu.make_async_copy(down, dbuf, sem.at[5]),
    ]
    for copy in copies:
        copy.start()
    copies[0].wait()
    copies[1].wait()
    rows_buf[...] = jnp.concatenate([hbuf[0].astype(F32).T, hbuf[1].astype(F32).T], axis=1)
    blocks, lines, lanes = out.shape
    feats, width = w_own.shape[1:]
    rows = rows_buf.shape[0] // (blocks * NC)
    chosen = jnp.concatenate(
        [
            rows_buf[pl.ds(pl.multiple_of((2 * b + core) * rows, rows), rows), :]
            for b in range(blocks)
        ],
        axis=0,
    ).astype(BF16)
    copies[2].wait()
    copies[3].wait()
    at = 0
    for g in range(3):
        weights = jnp.concatenate([wbuf[0, g], wbuf[1, g]], axis=0)
        part = jnp.dot(chosen, weights, preferred_element_type=F32).astype(BF16)
        for t in range(width // lanes):
            out[:, at : at + rows] = part[:, t * lanes : (t + 1) * lanes].reshape(blocks, rows, lanes)
            at += rows
    out[:, at : at + rows] = chosen.reshape(blocks, rows, lanes)
    at += rows
    copies[4].wait()
    copies[5].wait()
    for b in range(blocks):
        cols = pl.ds(b * lanes, lanes)
        out[b, at : at + feats] = gbuf[0, :, cols]
        out[b, at + feats : at + 2 * feats] = gbuf[1, :, cols]
        out[b, at + 2 * feats : at + 3 * feats] = dbuf[:, cols]


def quarter(ref, x):
    pair = ref[pl.ds(pl.multiple_of(x // 2 * 8, 8), 8), :]
    return jnp.where(lax.rem(x, 2) == 0, pair[:4], pair[4:])


def collect_kernel(got, after, tables, bounds, gains, qk, value, squares, rest, ffn, rest_buf, sem):
    rows, width = value.shape
    blocks, lines, lanes = got.shape
    tiles = width // lanes
    at = (3 * tiles + 1) * rows
    copy = pltpu.make_async_copy(got.at[:, pl.ds(at, lines - at)], ffn, sem)
    copy.start()
    total = got[0, : 3 * width // lanes * rows].astype(F32)
    for i in range(1, blocks):
        total += got[i, : 3 * width // lanes * rows].astype(F32)

    def part(g):
        return jnp.concatenate(
            [total[(g * tiles + t) * rows : (g * tiles + t + 1) * rows] for t in range(tiles)], axis=1
        )

    q, k = part(0), part(1)
    qk[0] = q
    qk[1] = k
    value[...] = part(2).astype(BF16)
    lane = lax.broadcasted_iota(jnp.int32, squares.shape[1:], 1)
    both = jnp.where(
        lane < 64, jnp.sum(q * q, axis=1, keepdims=True), jnp.sum(k * k, axis=1, keepdims=True)
    )
    for i in range(NX):
        squares[i] = both
    for i in range(blocks):
        rest_buf[:, i * lanes : (i + 1) * lanes] = got[i, at - rows : at].astype(F32)
    rest[...] = quarter(rest_buf, lax.axis_index("xh") * 2 + lax.axis_index("xl"))
    copy.wait()


def turn(values, cosine, sine):
    heads = values.shape[1] // HEAD_DIM
    parts = []
    for h in range(heads):
        v = values[:, h * HEAD_DIM : (h + 1) * HEAD_DIM]
        parts.append(v * cosine + pltpu.roll(v, HEAD_DIM // 2, 1) * sine)
    return jnp.concatenate(parts, axis=1)


def spread(values, heads):
    rows, width = values.shape
    wide = rows * heads
    row_head = lax.broadcasted_iota(jnp.int32, (wide, width), 0) // rows
    col_head = lax.broadcasted_iota(jnp.int32, (wide, width), 1) // HEAD_DIM
    return jnp.where(row_head == col_head, jnp.concatenate([values] * heads, axis=0), 0.0)


def attend_kernel(squares_in, qk, value, gains, tables, bounds, keys, values, key_out,
                  out, score, top, kbuf, vbuf, acc, total, ksem, vsem):
    rows, width = value.shape
    heads = width // HEAD_DIM
    blocks = score.shape[0]
    model = width * NX
    used = jnp.max(bounds[...].astype(F32))

    def fetch(source, buf, sem, i):
        return pltpu.make_async_copy(source.at[pl.ds(i * BLOCK, BLOCK)], buf.at[i], sem.at[i])

    for source, buf, sem in ((keys, kbuf, ksem), (values, vbuf, vsem)):
        for i in range(blocks):
            @pl.when(i * BLOCK < used)
            def _():
                fetch(source, buf, sem, i).start()

    squares = squares_in[0] + squares_in[1] + squares_in[2] + squares_in[3]
    q_factor = lax.rsqrt(squares[:, 0:1] / model + EPS)
    k_factor = lax.rsqrt(squares[:, 64:65] / model + EPS)
    query = turn(qk[0] * q_factor * gains[0:1, :], tables[0], tables[1]).astype(BF16)
    new_key = turn(qk[1] * k_factor * gains[1:2, :], tables[0], tables[1]).astype(BF16)
    key_out[...] = new_key
    scale = HEAD_DIM ** (-0.5)
    q_all = spread(query.astype(F32), heads)
    q_block = q_all.astype(BF16)
    k_all = jnp.concatenate([new_key.astype(F32)] * heads, axis=0)
    v_all = jnp.concatenate([value[...].astype(F32)] * heads, axis=0)
    own = jnp.sum(q_all * k_all, axis=1, keepdims=True) * scale
    starts = bounds[:, 0:1]
    ends = bounds[:, 1:2]
    top[...] = jnp.broadcast_to(own, top.shape)
    for i in range(blocks):
        @pl.when(i * BLOCK < used)
        def _():
            fetch(keys, kbuf, ksem, i).wait()
            s = lax.dot_general(q_block, kbuf[i], NT, preferred_element_type=F32) * scale
            place = lax.broadcasted_iota(jnp.int32, s.shape, 1) + i * BLOCK
            s = jnp.where((place >= starts) & (place < ends), s, -jnp.inf)
            score[i] = s
            top[...] = jnp.maximum(top[...], jnp.max(s, axis=1, keepdims=True))
    highest = top[:, 0:1]
    own_weight = jnp.exp(own - highest).astype(BF16).astype(F32)
    total[...] = jnp.broadcast_to(own_weight, total.shape)
    acc[...] = own_weight * v_all
    for i in range(blocks):
        @pl.when(i * BLOCK < used)
        def _():
            fetch(values, vbuf, vsem, i).wait()
            w = jnp.exp(score[i] - highest).astype(BF16)
            total[...] += jnp.sum(w.astype(F32), axis=1, keepdims=True)
            acc[...] += jnp.dot(w, vbuf[i], preferred_element_type=F32)
    result = acc[...] / total[:, 0:1]
    out[...] = jnp.concatenate(
        [
            result[h * rows : (h + 1) * rows, h * HEAD_DIM : (h + 1) * HEAD_DIM]
            for h in range(heads)
        ],
        axis=1,
    ).astype(BF16)


def out_kernel(attended, *refs):
    pieces = refs[:NC]
    partial, gain_out, wbuf, sem = refs[NC:]
    rows, width = attended.shape
    copies = piece_copies(pieces, wbuf, sem)
    for copy in copies:
        copy.start()
    for copy in copies:
        copy.wait()
    feats = width // (NY * NC)
    mine = rows // NX
    for b in range(NZ):
        weights = jnp.concatenate(
            [wbuf[b, c, y, :feats] for y in range(NY) for c in range(NC)], axis=0
        )
        a = lax.dot_general(attended[...], weights, NT, preferred_element_type=F32)
        for x in range(NX):
            partial[x, :, b * width : (b + 1) * width] = a[x * mine : (x + 1) * mine]
        both = wbuf[b, 0, 0, feats:].astype(F32)
        for y in range(NY):
            for c in range(NC):
                if y or c:
                    both += wbuf[b, c, y, feats:].astype(F32)
        gain_out[b, 0:1] = both[0:1] + both[1:2]
        gain_out[b, 1:2] = both[2:3] + both[3:4]


def fan_kernel(got, rest, gains, own_mid, out):
    total = got[0] + got[1] + got[2] + got[3]
    model = total.shape[1]
    power = jnp.sum(total * total, axis=1, keepdims=True) / model
    gain = jnp.concatenate([gains[z, 0:1] for z in range(NZ)], axis=1)
    mid = (rest[...] + total * lax.rsqrt(power + EPS) * gain).astype(BF16)
    mid32 = mid.astype(F32)
    own_mid[...] = mid32
    message = jnp.concatenate([mid32[:, : model // 2], mid32[:, model // 2 :]], axis=0).astype(BF16)
    for i in range(out.shape[0]):
        out[i] = message


def ffn_kernel(got, own, own_mate, near, near_mate, out, wbuf, sem):
    core = lax.axis_index("c")
    copies = [
        pltpu.make_async_copy(own, wbuf.at[0, core], sem.at[0]),
        pltpu.make_async_copy(own_mate, wbuf.at[0, 1 - core], sem.at[1]),
        pltpu.make_async_copy(near, wbuf.at[1, core], sem.at[2]),
        pltpu.make_async_copy(near_mate, wbuf.at[1, 1 - core], sem.at[3]),
    ]
    for copy in copies:
        copy.start()
    places, lines, span = got.shape
    mine = lines // 2
    whole = [got[d].astype(F32) for d in range(places)]
    mid = [
        jnp.concatenate([w[half * mine : (half + 1) * mine] for w in whole], axis=0).astype(BF16)
        for half in range(2)
    ]
    blocks = wbuf.shape[2]
    feats = wbuf.shape[3] // 3
    for copy in copies:
        copy.wait()

    def weights(part, half):
        rows = range(half * blocks // 2, (half + 1) * blocks // 2)
        return jnp.concatenate(
            [
                jnp.concatenate(
                    [
                        wbuf[p, c, b, part * feats : (part + 1) * feats]
                        for b in rows
                        for c in range(NC)
                    ],
                    axis=0,
                )
                for p in range(2)
            ],
            axis=1,
        )

    gate = jnp.dot(mid[0], weights(0, 0), preferred_element_type=F32)
    gate += jnp.dot(mid[1], weights(0, 1), preferred_element_type=F32)
    lift = jnp.dot(mid[0], weights(1, 0), preferred_element_type=F32)
    lift += jnp.dot(mid[1], weights(1, 1), preferred_element_type=F32)
    act = (gate / (1.0 + jnp.exp(-gate)) * lift).astype(BF16)
    flat = [lax.dot_general(act, weights(2, h), NT, preferred_element_type=F32) for h in range(2)]
    for d in range(places):
        out[d] = jnp.concatenate([f[d * mine : (d + 1) * mine] for f in flat], axis=0).astype(BF16)


def finish_kernel(got, own_mid, gains, out):
    total = got[0].astype(F32)
    for i in range(1, got.shape[0]):
        total += got[i].astype(F32)
    mine = own_mid.shape[0]
    total = jnp.concatenate([total[:mine], total[mine:]], axis=1)
    model = total.shape[1]
    power = jnp.sum(total * total, axis=1, keepdims=True) / model
    gain = jnp.concatenate([gains[z, 1:2] for z in range(NZ)], axis=1)
    hidden = (own_mid[...] + total * lax.rsqrt(power + EPS) * gain).astype(BF16)
    feats = out.shape[2]
    for r in range(model // feats):
        part = hidden[:, r * feats : (r + 1) * feats]
        for x in range(NX):
            out[r * NX + x] = part


def ring(shift, size):
    return [(i, (i + shift) % size) for i in range(size)]


def body(hidden_in, lengths, w_qkv, qk_gain, cache_keys, cache_values, w_out, norm_gain,
         w_gate_up, w_down):
    rows = lengths.shape[0]
    width = w_qkv.shape[2]
    heads = width // HEAD_DIM
    feats = hidden_in.shape[1]
    model = width * NX
    wide = rows * heads
    blocks = cache_keys.shape[0] // BLOCK
    y_here = lax.axis_index("y")
    c_here = lax.axis_index("c")

    flipped = hidden_in.T
    mate_rows = lax.ppermute(flipped, "c", ring(1, NC))
    mate_w = lax.ppermute(w_qkv, "c", ring(1, NC))
    places = NZ * NY
    size = 3 * feats
    lanes = 128
    lines = (3 * width // lanes + 1) * rows + size
    message = call(
        project_kernel,
        shape((places, lines, lanes), BF16),
        [ANY] * 6,
        VMEM,
        [
            pltpu.VMEM((2, feats, flipped.shape[1]), BF16),
            pltpu.VMEM((2,) + w_qkv.shape, BF16),
            pltpu.VMEM((flipped.shape[1], 2 * feats), F32),
            pltpu.VMEM(w_gate_up.shape, BF16),
            pltpu.VMEM(w_down.shape, BF16),
            pltpu.SemaphoreType.DMA((6,)),
        ],
        (1 << 27, 2 << 20),
        "project",
        8,
    )(hbm(flipped), mate_rows, hbm(w_qkv), mate_w, hbm(w_gate_up), hbm(w_down))
    got = lax.all_to_all(message, ("z", "y"), 0, 0, tiled=True)

    high = norm_gain.astype(BF16)
    low = (norm_gain - high.astype(F32)).astype(BF16)
    gain_rows = jnp.stack([high[0], low[0], high[1], low[1]])
    gain_tile = jnp.zeros((8, width), BF16)
    gain_tile = lax.dynamic_update_slice(
        gain_tile, gain_rows, (jnp.int32(0), (y_here * NC + c_here) * feats)
    )
    part = jnp.concatenate([w_out, gain_tile], axis=0)
    part = call(
        sort_kernel,
        shape((NY,) + part.shape, BF16),
        [ANY] * NY,
        ANY,
        [pltpu.SemaphoreType.DMA((NY,))],
        (0, 1 << 20),
        "sort",
        1,
    )(part, *[lax.ppermute(part, "y", ring(s, NY)) for s in range(1, NY)])
    out_pieces = [part] + [lax.ppermute(part, "z", ring(s, NZ)) for s in range(1, NZ)]

    half = HEAD_DIM // 2
    freqs = jnp.power(THETA, -(jnp.arange(half, dtype=F32) * 2.0 / HEAD_DIM))
    angles = lengths.astype(F32)[:, None] * freqs[None, :]
    cosine = jnp.cos(angles)
    sine = jnp.sin(angles)
    tables = jnp.stack(
        [jnp.concatenate([cosine, cosine], axis=1), jnp.concatenate([-sine, sine], axis=1)]
    )
    ends = jnp.cumsum(lengths)
    bounds = jnp.tile(jnp.stack([ends - lengths, ends], axis=1), (heads, 1))
    gain_table = jnp.concatenate([qk_gain, jnp.zeros((6, width), F32)], axis=0)
    qk, value_new, squares, rest, ffn_own = call(
        collect_kernel,
        (
            shape((2, rows, width), F32),
            shape((rows, width), BF16),
            shape((NX, rows, 128), F32),
            shape((rows // NX, model), F32),
            shape((places, size, lanes), BF16),
        ),
        [VMEM] + [ANY] * 4,
        (VMEM,) * 4 + (ANY,),
        [pltpu.VMEM((rows, model), F32), pltpu.SemaphoreType.DMA],
        (1 << 20, 96 << 20),
        "collect",
        8,
    )(got, part, tables, bounds, gain_table)
    squares = lax.all_to_all(squares, X, 0, 0, tiled=True)
    out_own = join(out_pieces, squares, "join_out")
    out_mate = lax.ppermute(out_own, "c", ring(1, NC))
    key_new, attended = call(
        attend_kernel,
        (shape((rows, width), BF16), shape((rows, width), BF16)),
        [VMEM] * 6 + [ANY] * 2,
        (VMEM,) * 2,
        [
            pltpu.VMEM((blocks, wide, BLOCK), F32),
            pltpu.VMEM((wide, 128), F32),
            pltpu.VMEM((blocks, BLOCK, width), BF16),
            pltpu.VMEM((blocks, BLOCK, width), BF16),
            pltpu.VMEM((wide, width), F32),
            pltpu.VMEM((wide, 128), F32),
            pltpu.SemaphoreType.DMA((blocks,)),
            pltpu.SemaphoreType.DMA((blocks,)),
        ],
        (1 << 29, 8 << 20),
        "attend",
        16,
    )(squares, qk, value_new, gain_table, tables, bounds, hbm(cache_keys), hbm(cache_values))
    partial, gains = call(
        out_kernel,
        (shape((NX, rows // NX, model), F32), shape((NZ, 8, width), F32)),
        [VMEM] + [ANY] * NC,
        (VMEM,) * 2,
        [
            pltpu.VMEM((NZ, NC) + part.shape, BF16),
            pltpu.SemaphoreType.DMA((NC, 4)),
        ],
        (1 << 26, 2 << 20),
        "project_out",
        8,
    )(attended, out_own, out_mate)

    near = [(i, i ^ 1) for i in range(2)]
    ffn_near = lax.ppermute(ffn_own, "xl", near)
    got = lax.all_to_all(partial, X, 0, 0, tiled=True)
    mine = rows // NX
    group = ("z", "y", "xh")
    members = NZ * NY * NX // 2
    own_mid, message = call(
        fan_kernel,
        (shape((mine, model), F32), shape((members, 2 * mine, model // 2), BF16)),
        [VMEM] * 3,
        (VMEM, VMEM),
        (),
        (1 << 16, 1 << 19),
        "fan",
    )(got, rest, gains)
    ffn_near = join([ffn_near], own_mid, "hold")[0]
    ffn_pieces = []
    for piece in (ffn_own, ffn_near):
        ffn_pieces += [piece, lax.ppermute(piece, "c", ring(1, NC))]
    got = lax.all_to_all(message, group, 0, 0, tiled=True)
    partial = call(
        ffn_kernel,
        shape((members, 2 * mine, model // 2), BF16),
        [VMEM] + [ANY] * 4,
        VMEM,
        [
            pltpu.VMEM((2, NC) + ffn_own.shape, BF16),
            pltpu.SemaphoreType.DMA((4,)),
        ],
        (1 << 28, 4 << 20),
        "feed_forward",
        16,
    )(got, *ffn_pieces)
    got = lax.all_to_all(partial, group, 0, 0, tiled=True)
    message = call(
        finish_kernel,
        shape((NZ * NY * NC * NX, mine, feats), BF16),
        [VMEM] * 3,
        VMEM,
        (),
        (1 << 18, 1 << 19),
        "finish",
    )(got, own_mid, gains)
    hidden = lax.all_to_all(message, ("z", "y", "c") + X, 0, 0, tiled=True)
    return hidden.reshape(-1, feats), key_new, value_new


def solution(mesh):
    fine = Mesh(mesh.devices.reshape(NZ, NY, NC, 2, 2), ("z", "y", "c") + X)
    req = ("z", "y", "c")
    return jax.shard_map(
        body,
        mesh=fine,
        in_specs=(
            P(None, req),
            P(req),
            P(None, req, X),
            P(None, X),
            P(req, X),
            P(req, X),
            P(req, X),
            P(None, req),
            P(None, req, X),
            P(req, X),
        ),
        out_specs=(P(None, req), P(req, X), P(req, X)),
        check_vma=False,
    )
```

```python
import functools

import jax
import jax.numpy as jnp
from jax import lax
from jax.experimental import pallas as pl
from jax.experimental.pallas import tpu as pltpu
from jax.sharding import Mesh, PartitionSpec as P

HEAD_DIM = 128
EPS = 1e-06
THETA = 500000.0
NT = (((1,), (1,)), ((), ()))
BLOCK = 512
F32 = jnp.float32
BF16 = jnp.bfloat16
NZ, NY, NC, NX = 4, 4, 2, 4
Z = ("zh", "zl")
VMEM = pl.BlockSpec(memory_space=pltpu.VMEM)
HBM = pl.BlockSpec(memory_space=pltpu.HBM)
ANY = pl.BlockSpec(memory_space=pl.ANY)
SMEM = pl.BlockSpec(memory_space=pltpu.SMEM)


def call(kernel, out_shape, in_specs, out_specs, scratch=(), cost=(1 << 20, 1 << 20), name=None, limit=4):
    return pl.pallas_call(
        kernel,
        out_shape=out_shape,
        in_specs=in_specs,
        out_specs=out_specs,
        scratch_shapes=list(scratch),
        compiler_params=pltpu.CompilerParams(vmem_limit_bytes=limit * 1024 * 1024),
        cost_estimate=pl.CostEstimate(flops=cost[0], bytes_accessed=cost[1], transcendentals=0),
        name=name,
    )


def hbm(array):
    return pltpu.with_memory_space_constraint(array, pltpu.HBM)


def shape(dims, dtype):
    return jax.ShapeDtypeStruct(dims, dtype)


def run(copies, sem):
    copies = [pltpu.make_async_copy(a, b, sem.at[i]) for i, (a, b) in enumerate(copies)]
    for copy in copies:
        copy.start()
    for copy in copies:
        copy.wait()


def join_kernel(*refs):
    out, sem = refs[-2:]
    pieces = refs[:-3]
    run([(piece, out.at[i]) for i, piece in enumerate(pieces)], sem)


def join(pieces, token, name):
    return call(
        join_kernel,
        shape((len(pieces),) + pieces[0].shape, BF16),
        [ANY] * (len(pieces) + 1),
        ANY,
        [pltpu.SemaphoreType.DMA((len(pieces),))],
        (0, 2 << 20),
        name,
        1,
    )(*pieces, token)


def project_kernel(h_own, h_mate, w_own, w_mate, gate_up, down, out_w, gains, out, hbuf, wbuf, rows_buf,
                   gbuf, dbuf, obuf, nbuf, sem):
    core = lax.axis_index("c")
    copies = [
        pltpu.make_async_copy(h_own, hbuf.at[core], sem.at[0]),
        pltpu.make_async_copy(h_mate, hbuf.at[1 - core], sem.at[1]),
        pltpu.make_async_copy(w_own, wbuf.at[core], sem.at[2]),
        pltpu.make_async_copy(w_mate, wbuf.at[1 - core], sem.at[3]),
        pltpu.make_async_copy(gate_up, gbuf, sem.at[4]),
        pltpu.make_async_copy(down, dbuf, sem.at[5]),
        pltpu.make_async_copy(out_w, obuf, sem.at[6]),
        pltpu.make_async_copy(gains, nbuf, sem.at[7]),
    ]
    for copy in copies:
        copy.start()
    copies[0].wait()
    copies[1].wait()
    rows_buf[...] = jnp.concatenate([hbuf[0].astype(F32).T, hbuf[1].astype(F32).T], axis=1)
    blocks, lines, lanes = out.shape
    feats, width = w_own.shape[1:]
    rows = rows_buf.shape[0] // (blocks * NC)
    chosen = jnp.concatenate(
        [
            rows_buf[pl.ds(pl.multiple_of((2 * b + core) * rows, rows), rows), :]
            for b in range(blocks)
        ],
        axis=0,
    ).astype(BF16)
    copies[2].wait()
    copies[3].wait()
    at = 0
    for g in range(3):
        weights = jnp.concatenate([wbuf[0, g], wbuf[1, g]], axis=0)
        part = jnp.dot(chosen, weights, preferred_element_type=F32).astype(BF16)
        for t in range(width // lanes):
            out[:, at : at + rows] = part[:, t * lanes : (t + 1) * lanes].reshape(blocks, rows, lanes)
            at += rows
    out[:, at : at + rows] = chosen.reshape(blocks, rows, lanes)
    at += rows
    copies[4].wait()
    copies[5].wait()
    copies[6].wait()
    copies[7].wait()
    tile = jnp.concatenate([nbuf[...]] * (width // feats), axis=1)
    place = lax.axis_index("y") * NC + core
    tile = jnp.where(lax.broadcasted_iota(jnp.int32, tile.shape, 1) // feats == place, tile, 0.0)
    high = tile.astype(BF16).astype(F32)
    tile = jnp.concatenate([high, tile - high, jnp.zeros_like(tile), jnp.zeros_like(tile)], axis=0)
    tile = tile.astype(BF16)
    for t in range(width // lanes):
        low = at + 3 * feats + t * (feats + 8)
        cols = slice(t * lanes, (t + 1) * lanes)
        for b in range(blocks):
            out[b, low : low + feats] = obuf[:, cols]
            out[b, low + feats : low + feats + 8] = tile[:, cols]
    for b in range(blocks):
        cols = pl.ds(b * lanes, lanes)
        out[b, at : at + feats] = gbuf[0, :, cols]
        out[b, at + feats : at + 2 * feats] = gbuf[1, :, cols]
        out[b, at + 2 * feats : at + 3 * feats] = dbuf[:, cols]


def quarter(ref, x):
    pair = ref[pl.ds(pl.multiple_of(x // 2 * 8, 8), 8), :]
    return jnp.where(lax.rem(x, 2) == 0, pair[:4], pair[4:])


def collect_kernel(got, tables, bounds, gains, qk, value, squares, rest, ffn, out_w, buf, rest_buf, sem):
    rows, width = value.shape
    blocks, lines, lanes = got.shape
    tiles = width // lanes
    at = buf.shape[1]
    first = pltpu.make_async_copy(got.at[:, pl.ds(0, at)], buf, sem.at[0])
    second = pltpu.make_async_copy(got.at[:, pl.ds(at, ffn.shape[1])], ffn, sem.at[1])
    third = pltpu.make_async_copy(got.at[:, pl.ds(at + ffn.shape[1], out_w.shape[1])], out_w, sem.at[2])
    first.start()
    third.start()
    second.start()
    first.wait()
    total = buf[0, : at - rows].astype(F32)
    for i in range(1, blocks):
        total += buf[i, : at - rows].astype(F32)

    def part(g):
        return jnp.concatenate(
            [total[(g * tiles + t) * rows : (g * tiles + t + 1) * rows] for t in range(tiles)], axis=1
        )

    q, k = part(0), part(1)
    qk[0] = q
    qk[1] = k
    new = part(2).astype(BF16)
    value[...] = new
    qk[2] = new.astype(F32)
    lane = lax.broadcasted_iota(jnp.int32, squares.shape[1:], 1)
    both = jnp.where(
        lane < 64, jnp.sum(q * q, axis=1, keepdims=True), jnp.sum(k * k, axis=1, keepdims=True)
    )
    for i in range(NX):
        squares[i] = both
    for i in range(blocks):
        rest_buf[:, i * lanes : (i + 1) * lanes] = buf[i, at - rows : at].astype(F32)
    rest[...] = quarter(rest_buf, lax.axis_index("x"))
    second.wait()
    third.wait()


def turn(values, cosine, sine):
    heads = values.shape[1] // HEAD_DIM
    parts = []
    for h in range(heads):
        v = values[:, h * HEAD_DIM : (h + 1) * HEAD_DIM]
        parts.append(v * cosine + pltpu.roll(v, HEAD_DIM // 2, 1) * sine)
    return jnp.concatenate(parts, axis=1)


def spread(values, heads):
    rows, width = values.shape
    wide = rows * heads
    row_head = lax.broadcasted_iota(jnp.int32, (wide, width), 0) // rows
    col_head = lax.broadcasted_iota(jnp.int32, (wide, width), 1) // HEAD_DIM
    return jnp.where(row_head == col_head, jnp.concatenate([values] * heads, axis=0), 0.0)


def attend_kernel(squares_in, qk, gains, tables, bounds, keys, values, key_out,
                  out, score, top, kbuf, vbuf, acc, total, ksem, vsem):
    rows, width = out.shape
    heads = width // HEAD_DIM
    blocks = score.shape[0]
    model = width * NX
    used = jnp.max(bounds[...].astype(F32))

    def fetch(source, buf, sem, i):
        return pltpu.make_async_copy(source.at[pl.ds(i * BLOCK, BLOCK)], buf.at[i], sem.at[i])

    for source, buf, sem in ((keys, kbuf, ksem), (values, vbuf, vsem)):
        for i in range(blocks):
            @pl.when(i * BLOCK < used)
            def _():
                fetch(source, buf, sem, i).start()

    squares = squares_in[0] + squares_in[1] + squares_in[2] + squares_in[3]
    q_factor = lax.rsqrt(squares[:, 0:1] / model + EPS)
    k_factor = lax.rsqrt(squares[:, 64:65] / model + EPS)
    query = turn(qk[0] * q_factor * gains[0:1, :], tables[0], tables[1]).astype(BF16)
    new_key = turn(qk[1] * k_factor * gains[1:2, :], tables[0], tables[1]).astype(BF16)
    key_out[...] = new_key
    scale = HEAD_DIM ** (-0.5)
    q_all = spread(query.astype(F32), heads)
    q_block = q_all.astype(BF16)
    k_all = jnp.concatenate([new_key.astype(F32)] * heads, axis=0)
    v_all = jnp.concatenate([qk[2]] * heads, axis=0)
    own = jnp.sum(q_all * k_all, axis=1, keepdims=True) * scale
    starts = bounds[:, 0:1]
    ends = bounds[:, 1:2]
    top[...] = jnp.broadcast_to(own, top.shape)
    for i in range(blocks):
        @pl.when(i * BLOCK < used)
        def _():
            fetch(keys, kbuf, ksem, i).wait()
            s = lax.dot_general(q_block, kbuf[i], NT, preferred_element_type=F32) * scale
            place = lax.broadcasted_iota(jnp.int32, s.shape, 1) + i * BLOCK
            s = jnp.where((place >= starts) & (place < ends), s, -jnp.inf)
            score[i] = s
            top[...] = jnp.maximum(top[...], jnp.max(s, axis=1, keepdims=True))
    highest = top[:, 0:1]
    own_weight = jnp.exp(own - highest).astype(BF16).astype(F32)
    total[...] = jnp.broadcast_to(own_weight, total.shape)
    acc[...] = own_weight * v_all
    for i in range(blocks):
        @pl.when(i * BLOCK < used)
        def _():
            fetch(values, vbuf, vsem, i).wait()
            w = jnp.exp(score[i] - highest).astype(BF16)
            total[...] += jnp.sum(w.astype(F32), axis=1, keepdims=True)
            acc[...] += jnp.dot(w, vbuf[i], preferred_element_type=F32)
    result = acc[...] / total[:, 0:1]
    out[...] = jnp.concatenate(
        [
            result[h * rows : (h + 1) * rows, h * HEAD_DIM : (h + 1) * HEAD_DIM]
            for h in range(heads)
        ],
        axis=1,
    ).astype(BF16)


def out_kernel(attended, own, mate, partial, gain_out, wbuf, sem):
    rows, width = attended.shape
    core = lax.axis_index("c")
    copies = [
        pltpu.make_async_copy(own, wbuf.at[core], sem.at[0]),
        pltpu.make_async_copy(mate, wbuf.at[1 - core], sem.at[1]),
    ]
    for copy in copies:
        copy.start()
    for copy in copies:
        copy.wait()
    feats = width // (NY * NC)
    lanes = wbuf.shape[3]
    tiles = width // lanes
    step = wbuf.shape[2] // tiles
    mine = rows // NX
    for b in range(NZ):
        places = [(c, b * NY + y) for y in range(NY) for c in range(NC)]
        weights = jnp.concatenate(
            [
                jnp.concatenate([wbuf[c, p, t * step : t * step + feats] for c, p in places], axis=0)
                for t in range(tiles)
            ],
            axis=1,
        )
        a = lax.dot_general(attended[...], weights, NT, preferred_element_type=F32)
        for x in range(NX):
            partial[x, :, b * width : (b + 1) * width] = a[x * mine : (x + 1) * mine]
        for t in range(tiles):
            both = None
            for c, p in places:
                piece = wbuf[c, p, t * step + feats : (t + 1) * step].astype(F32)
                both = piece if both is None else both + piece
            gain_out[b, 0:2, t * lanes : (t + 1) * lanes] = both[0:2] + both[2:4]


def fan_kernel(got, rest, gains, own_mid, out):
    total = got[0] + got[1] + got[2] + got[3]
    model = total.shape[1]
    power = jnp.sum(total * total, axis=1, keepdims=True) / model
    gain = jnp.concatenate([gains[z, 0:1] for z in range(NZ)], axis=1)
    mid = (rest[...] + total * lax.rsqrt(power + EPS) * gain).astype(BF16)
    mid32 = mid.astype(F32)
    own_mid[...] = mid32
    message = jnp.concatenate([mid32[:, : model // 2], mid32[:, model // 2 :]], axis=0).astype(BF16)
    for i in range(out.shape[0]):
        out[i] = message


def ffn_kernel(got, own, own_mate, near, near_mate, out, wbuf, sem):
    core = lax.axis_index("c")
    copies = [
        pltpu.make_async_copy(own, wbuf.at[0, core], sem.at[0]),
        pltpu.make_async_copy(own_mate, wbuf.at[0, 1 - core], sem.at[1]),
        pltpu.make_async_copy(near, wbuf.at[1, core], sem.at[2]),
        pltpu.make_async_copy(near_mate, wbuf.at[1, 1 - core], sem.at[3]),
    ]
    for copy in copies:
        copy.start()
    places, lines, span = got.shape
    mine = lines // 2
    whole = [got[d].astype(F32) for d in range(places)]
    mid = [
        jnp.concatenate([w[half * mine : (half + 1) * mine] for w in whole], axis=0).astype(BF16)
        for half in range(2)
    ]
    blocks = wbuf.shape[2]
    feats = wbuf.shape[3] // 3
    for copy in copies:
        copy.wait()

    def weights(part, half):
        rows = range(half * blocks // 2, (half + 1) * blocks // 2)
        return jnp.concatenate(
            [
                jnp.concatenate(
                    [
                        wbuf[p, c, b, part * feats : (part + 1) * feats]
                        for b in rows
                        for c in range(NC)
                    ],
                    axis=0,
                )
                for p in range(2)
            ],
            axis=1,
        )

    gate = jnp.dot(mid[0], weights(0, 0), preferred_element_type=F32)
    gate += jnp.dot(mid[1], weights(0, 1), preferred_element_type=F32)
    lift = jnp.dot(mid[0], weights(1, 0), preferred_element_type=F32)
    lift += jnp.dot(mid[1], weights(1, 1), preferred_element_type=F32)
    act = (gate / (1.0 + jnp.exp(-gate)) * lift).astype(BF16)
    flat = [lax.dot_general(act, weights(2, h), NT, preferred_element_type=F32) for h in range(2)]
    for d in range(places):
        out[d] = jnp.concatenate([f[d * mine : (d + 1) * mine] for f in flat], axis=0).astype(BF16)


def finish_kernel(got, own_mid, gains, out):
    total = got[0].astype(F32)
    for i in range(1, got.shape[0]):
        total += got[i].astype(F32)
    mine = own_mid.shape[0]
    total = jnp.concatenate([total[:mine], total[mine:]], axis=1)
    model = total.shape[1]
    power = jnp.sum(total * total, axis=1, keepdims=True) / model
    gain = jnp.concatenate([gains[z, 1:2] for z in range(NZ)], axis=1)
    hidden = (own_mid[...] + total * lax.rsqrt(power + EPS) * gain).astype(BF16)
    feats = out.shape[2]
    for r in range(model // feats):
        part = hidden[:, r * feats : (r + 1) * feats]
        for x in range(NX):
            out[r * NX + x] = part


def ring(shift, size):
    return [(i, (i + shift) % size) for i in range(size)]


def body(hidden_in, lengths, w_qkv, qk_gain, cache_keys, cache_values, w_out, norm_gain,
         w_gate_up, w_down):
    rows = lengths.shape[0]
    width = w_qkv.shape[2]
    heads = width // HEAD_DIM
    feats = hidden_in.shape[1]
    model = width * NX
    wide = rows * heads
    blocks = cache_keys.shape[0] // BLOCK

    flipped = hidden_in.T
    mate_rows = lax.ppermute(flipped, "c", ring(1, NC))
    mate_w = lax.ppermute(w_qkv, "c", ring(1, NC))
    places = NZ * NY
    size = 3 * feats
    lanes = 128
    tiles = width // lanes
    head_lines = (3 * tiles + 1) * rows
    out_lines = tiles * (feats + 8)
    message = call(
        project_kernel,
        shape((places, head_lines + size + out_lines, lanes), BF16),
        [ANY] * 8,
        VMEM,
        [
            pltpu.VMEM((2, feats, flipped.shape[1]), BF16),
            pltpu.VMEM((2,) + w_qkv.shape, BF16),
            pltpu.VMEM((flipped.shape[1], 2 * feats), F32),
            pltpu.VMEM(w_gate_up.shape, BF16),
            pltpu.VMEM(w_down.shape, BF16),
            pltpu.VMEM(w_out.shape, BF16),
            pltpu.VMEM(norm_gain.shape, F32),
            pltpu.SemaphoreType.DMA((8,)),
        ],
        (1 << 27, 2 << 20),
        "project",
        8,
    )(hbm(flipped), mate_rows, hbm(w_qkv), mate_w, hbm(w_gate_up), hbm(w_down), hbm(w_out), hbm(norm_gain))
    got = lax.all_to_all(hbm(message), Z + ("y",), 0, 0, tiled=True)

    half = HEAD_DIM // 2
    freqs = jnp.power(THETA, -(jnp.arange(half, dtype=F32) * 2.0 / HEAD_DIM))
    angles = lengths.astype(F32)[:, None] * freqs[None, :]
    cosine = jnp.cos(angles)
    sine = jnp.sin(angles)
    tables = jnp.stack(
        [jnp.concatenate([cosine, cosine], axis=1), jnp.concatenate([-sine, sine], axis=1)]
    )
    ends = jnp.cumsum(lengths)
    bounds = jnp.tile(jnp.stack([ends - lengths, ends], axis=1), (heads, 1))
    gain_table = jnp.concatenate([qk_gain, jnp.zeros((6, width), F32)], axis=0)
    qk, value_new, squares, rest, ffn_own, out_own = call(
        collect_kernel,
        (
            shape((3, rows, width), F32),
            shape((rows, width), BF16),
            shape((NX, rows, 128), F32),
            shape((rows // NX, model), F32),
            shape((places, size, lanes), BF16),
            shape((places, out_lines, lanes), BF16),
        ),
        [ANY] * 4,
        (VMEM,) * 4 + (ANY,) * 2,
        [
            pltpu.VMEM((places, head_lines, lanes), BF16),
            pltpu.VMEM((rows, model), F32),
            pltpu.SemaphoreType.DMA((3,)),
        ],
        (1 << 20, 4 << 20),
        "collect",
        8,
    )(got, tables, bounds, gain_table)
    out_mate = lax.ppermute(out_own, "c", ring(1, NC))
    ffn_own = hbm(ffn_own)
    ffn_near = hbm(lax.ppermute(ffn_own, "zl", ring(1, 2)))
    squares = lax.all_to_all(squares, "x", 0, 0, tiled=True)
    key_new, attended = call(
        attend_kernel,
        (shape((rows, width), BF16), shape((rows, width), BF16)),
        [VMEM] * 5 + [ANY] * 2,
        (VMEM,) * 2,
        [
            pltpu.VMEM((blocks, wide, BLOCK), F32),
            pltpu.VMEM((wide, 128), F32),
            pltpu.VMEM((blocks, BLOCK, width), BF16),
            pltpu.VMEM((blocks, BLOCK, width), BF16),
            pltpu.VMEM((wide, width), F32),
            pltpu.VMEM((wide, 128), F32),
            pltpu.SemaphoreType.DMA((blocks,)),
            pltpu.SemaphoreType.DMA((blocks,)),
        ],
        (1 << 29, 8 << 20),
        "attend",
        16,
    )(squares, qk, gain_table, tables, bounds, hbm(cache_keys), hbm(cache_values))
    partial, gains = call(
        out_kernel,
        (shape((NX, rows // NX, model), F32), shape((NZ, 8, width), F32)),
        [VMEM] + [ANY] * NC,
        (VMEM,) * 2,
        [
            pltpu.VMEM((NC,) + out_own.shape, BF16),
            pltpu.SemaphoreType.DMA((2,)),
        ],
        (1 << 26, 2 << 20),
        "project_out",
        8,
    )(attended, out_own, out_mate)

    got = lax.all_to_all(partial, "x", 0, 0, tiled=True)
    mine = rows // NX
    group = ("zh", "y", "x")
    members = NZ * NY * NX // 2
    own_mid, message = call(
        fan_kernel,
        (shape((mine, model), F32), shape((members, 2 * mine, model // 2), BF16)),
        [VMEM] * 3,
        (VMEM, VMEM),
        (),
        (1 << 16, 1 << 19),
        "fan",
    )(got, rest, gains)
    ffn_near = hbm(join([ffn_near], own_mid, "hold")[0])
    ffn_pieces = []
    for piece in (ffn_own, ffn_near):
        ffn_pieces += [piece, hbm(lax.ppermute(piece, "c", ring(1, NC)))]
    got = lax.all_to_all(message, group, 0, 0, tiled=True)
    partial = call(
        ffn_kernel,
        shape((members, 2 * mine, model // 2), BF16),
        [VMEM] + [ANY] * 4,
        VMEM,
        [
            pltpu.VMEM((2, NC) + ffn_own.shape, BF16),
            pltpu.SemaphoreType.DMA((4,)),
        ],
        (1 << 28, 4 << 20),
        "feed_forward",
        16,
    )(got, *ffn_pieces)
    got = lax.all_to_all(partial, group, 0, 0, tiled=True)
    message = call(
        finish_kernel,
        shape((NZ * NY * NC * NX, mine, feats), BF16),
        [VMEM] * 3,
        VMEM,
        (),
        (1 << 18, 1 << 19),
        "finish",
    )(got, own_mid, gains)
    hidden = lax.all_to_all(message, Z + ("y", "c", "x"), 0, 0, tiled=True)
    return hidden.reshape(-1, feats), key_new, value_new


def solution(mesh):
    fine = Mesh(mesh.devices.reshape(2, 2, NY, NC, NX), Z + ("y", "c", "x"))
    req = Z + ("y", "c")
    return jax.shard_map(
        body,
        mesh=fine,
        in_specs=(
            P(None, req),
            P(req),
            P(None, req, "x"),
            P(None, "x"),
            P(req, "x"),
            P(req, "x"),
            P(req, "x"),
            P(None, req),
            P(None, req, "x"),
            P(req, "x"),
        ),
        out_specs=(P(None, req), P(req, "x"), P(req, "x")),
        check_vma=False,
    )
```

```python
import jax
import jax.numpy as jnp
from jax import lax
from jax.experimental import pallas as pl
from jax.experimental.pallas import tpu as pltpu
from jax.sharding import Mesh, PartitionSpec as P

HEAD_DIM = 128
EPS = 1e-06
THETA = 500000.0
NT = (((1,), (1,)), ((), ()))
BLOCK = 512
F32 = jnp.float32
BF16 = jnp.bfloat16
NZ, NY, NC, NX = 4, 4, 2, 4
Z = ("zh", "zl")
VMEM = pl.BlockSpec(memory_space=pltpu.VMEM)
HBM = pl.BlockSpec(memory_space=pltpu.HBM)
ANY = pl.BlockSpec(memory_space=pl.ANY)
SMEM = pl.BlockSpec(memory_space=pltpu.SMEM)


def call(kernel, out_shape, in_specs, out_specs, scratch=(), cost=(1 << 20, 1 << 20), name=None, limit=4):
    return pl.pallas_call(
        kernel,
        out_shape=out_shape,
        in_specs=in_specs,
        out_specs=out_specs,
        scratch_shapes=list(scratch),
        compiler_params=pltpu.CompilerParams(vmem_limit_bytes=limit * 1024 * 1024),
        cost_estimate=pl.CostEstimate(flops=cost[0], bytes_accessed=cost[1], transcendentals=0),
        name=name,
    )


def hbm(array):
    return pltpu.with_memory_space_constraint(array, pltpu.HBM)


def shape(dims, dtype):
    return jax.ShapeDtypeStruct(dims, dtype)


def hold_kernel(piece, token, out, sem):
    copy = pltpu.make_async_copy(piece, out, sem)
    copy.start()
    copy.wait()


def project_kernel(h_own, h_mate, w_own, w_mate, gate_up, down, out_w, gains, tables, bounds, scales,
                   out, hbuf, wbuf, rows_buf, gbuf, dbuf, obuf, nbuf, sem):
    core = lax.axis_index("c")
    copies = [
        pltpu.make_async_copy(h_own, hbuf.at[core], sem.at[0]),
        pltpu.make_async_copy(h_mate, hbuf.at[1 - core], sem.at[1]),
        pltpu.make_async_copy(w_own, wbuf.at[core], sem.at[2]),
        pltpu.make_async_copy(w_mate, wbuf.at[1 - core], sem.at[3]),
        pltpu.make_async_copy(gate_up, gbuf, sem.at[4]),
        pltpu.make_async_copy(down, dbuf, sem.at[5]),
        pltpu.make_async_copy(out_w, obuf, sem.at[6]),
        pltpu.make_async_copy(gains, nbuf, sem.at[7]),
    ]
    for copy in copies:
        copy.start()
    copies[0].wait()
    copies[1].wait()
    rows_buf[...] = jnp.concatenate([hbuf[0].astype(F32).T, hbuf[1].astype(F32).T], axis=1)
    blocks, lines, lanes = out.shape
    feats, width = w_own.shape[1:]
    rows = rows_buf.shape[0] // (blocks * NC)
    chosen = jnp.concatenate(
        [
            rows_buf[pl.ds(pl.multiple_of((2 * b + core) * rows, rows), rows), :]
            for b in range(blocks)
        ],
        axis=0,
    ).astype(BF16)
    copies[2].wait()
    copies[3].wait()
    at = 0
    for g in range(3):
        weights = jnp.concatenate([wbuf[0, g], wbuf[1, g]], axis=0)
        part = jnp.dot(chosen, weights, preferred_element_type=F32).astype(BF16)
        for t in range(width // lanes):
            out[:, at : at + rows] = part[:, t * lanes : (t + 1) * lanes].reshape(blocks, rows, lanes)
            at += rows
    out[:, at : at + rows] = chosen.reshape(blocks, rows, lanes)
    at += rows
    copies[4].wait()
    copies[5].wait()
    copies[6].wait()
    copies[7].wait()
    tile = jnp.concatenate([nbuf[...]] * (width // feats), axis=1)
    place = lax.axis_index("y") * NC + core
    tile = jnp.where(lax.broadcasted_iota(jnp.int32, tile.shape, 1) // feats == place, tile, 0.0)
    high = tile.astype(BF16).astype(F32)
    tile = jnp.concatenate([high, tile - high, jnp.zeros_like(tile), jnp.zeros_like(tile)], axis=0)
    tile = tile.astype(BF16)
    for t in range(width // lanes):
        low = at + 3 * feats + t * (feats + 8)
        cols = slice(t * lanes, (t + 1) * lanes)
        for b in range(blocks):
            out[b, low : low + feats] = obuf[:, cols]
            out[b, low + feats : low + feats + 8] = tile[:, cols]
    for b in range(blocks):
        cols = pl.ds(b * lanes, lanes)
        out[b, at : at + feats] = gbuf[0, :, cols]
        out[b, at + feats : at + 2 * feats] = gbuf[1, :, cols]
        out[b, at + 2 * feats : at + 3 * feats] = dbuf[:, cols]


def quarter(ref, x):
    pair = ref[pl.ds(pl.multiple_of(x // 2 * 8, 8), 8), :]
    return jnp.where(lax.rem(x, 2) == 0, pair[:4], pair[4:])


def collect_kernel(got, qk, value, squares, rest, ffn, buf, rest_buf, sem):
    rows, width = value.shape
    blocks, lines, lanes = got.shape
    tiles = width // lanes
    at = buf.shape[1]
    first = pltpu.make_async_copy(got.at[:, pl.ds(0, at)], buf, sem.at[0])
    second = pltpu.make_async_copy(got.at[:, pl.ds(at, ffn.shape[1])], ffn, sem.at[1])
    first.start()
    second.start()
    first.wait()
    total = buf[0, : at - rows].astype(F32)
    for i in range(1, blocks):
        total += buf[i, : at - rows].astype(F32)

    def part(g):
        return jnp.concatenate(
            [total[(g * tiles + t) * rows : (g * tiles + t + 1) * rows] for t in range(tiles)], axis=1
        )

    q, k = part(0), part(1)
    qk[0] = q
    qk[1] = k
    new = part(2).astype(BF16)
    value[...] = new
    qk[2] = new.astype(F32)
    lane = lax.broadcasted_iota(jnp.int32, squares.shape[1:], 1)
    both = jnp.where(
        lane < 64, jnp.sum(q * q, axis=1, keepdims=True), jnp.sum(k * k, axis=1, keepdims=True)
    )
    for i in range(NX):
        squares[i] = both
    for i in range(blocks):
        rest_buf[:, i * lanes : (i + 1) * lanes] = buf[i, at - rows : at].astype(F32)
    rest[...] = quarter(rest_buf, lax.axis_index("x"))
    second.wait()


def turn(values, cosine, sine):
    heads = values.shape[1] // HEAD_DIM
    parts = []
    for h in range(heads):
        v = values[:, h * HEAD_DIM : (h + 1) * HEAD_DIM]
        parts.append(v * cosine + pltpu.roll(v, HEAD_DIM // 2, 1) * sine)
    return jnp.concatenate(parts, axis=1)


def spread(values, heads):
    rows, width = values.shape
    wide = rows * heads
    row_head = lax.broadcasted_iota(jnp.int32, (wide, width), 0) // rows
    col_head = lax.broadcasted_iota(jnp.int32, (wide, width), 1) // HEAD_DIM
    return jnp.where(row_head == col_head, jnp.concatenate([values] * heads, axis=0), 0.0)


def attend_kernel(squares_in, qk, gains, tables, bounds, keys, values, key_out,
                  out, score, top, kbuf, vbuf, acc, total, ksem, vsem):
    rows, width = out.shape
    heads = width // HEAD_DIM
    blocks = score.shape[0]
    model = width * NX
    used = jnp.max(bounds[...].astype(F32))

    def fetch(source, buf, sem, i):
        return pltpu.make_async_copy(source.at[pl.ds(i * BLOCK, BLOCK)], buf.at[i], sem.at[i])

    for source, buf, sem in ((keys, kbuf, ksem), (values, vbuf, vsem)):
        for i in range(blocks):
            @pl.when(i * BLOCK < used)
            def _():
                fetch(source, buf, sem, i).start()

    squares = squares_in[0] + squares_in[1] + squares_in[2] + squares_in[3]
    q_factor = lax.rsqrt(squares[:, 0:1] / model + EPS)
    k_factor = lax.rsqrt(squares[:, 64:65] / model + EPS)
    query = turn(qk[0] * q_factor * gains[0:1, :], tables[0], tables[1]).astype(BF16)
    new_key = turn(qk[1] * k_factor * gains[1:2, :], tables[0], tables[1]).astype(BF16)
    key_out[...] = new_key
    scale = HEAD_DIM ** (-0.5)
    q_all = spread(query.astype(F32), heads)
    q_block = q_all.astype(BF16)
    k_all = jnp.concatenate([new_key.astype(F32)] * heads, axis=0)
    v_all = jnp.concatenate([qk[2]] * heads, axis=0)
    own = jnp.sum(q_all * k_all, axis=1, keepdims=True) * scale
    starts = bounds[:, 0:1]
    ends = bounds[:, 1:2]
    top[...] = jnp.broadcast_to(own, top.shape)
    for i in range(blocks):
        @pl.when(i * BLOCK < used)
        def _():
            fetch(keys, kbuf, ksem, i).wait()
            s = lax.dot_general(q_block, kbuf[i], NT, preferred_element_type=F32) * scale
            place = lax.broadcasted_iota(jnp.int32, s.shape, 1) + i * BLOCK
            s = jnp.where((place >= starts) & (place < ends), s, -jnp.inf)
            score[i] = s
            top[...] = jnp.maximum(top[...], jnp.max(s, axis=1, keepdims=True))
    highest = top[:, 0:1]
    own_weight = jnp.exp(own - highest).astype(BF16).astype(F32)
    total[...] = jnp.broadcast_to(own_weight, total.shape)
    acc[...] = own_weight * v_all
    for i in range(blocks):
        @pl.when(i * BLOCK < used)
        def _():
            fetch(values, vbuf, vsem, i).wait()
            w = jnp.exp(score[i] - highest).astype(BF16)
            total[...] += jnp.sum(w.astype(F32), axis=1, keepdims=True)
            acc[...] += jnp.dot(w, vbuf[i], preferred_element_type=F32)
    result = acc[...] / total[:, 0:1]
    out[...] = jnp.concatenate(
        [
            result[h * rows : (h + 1) * rows, h * HEAD_DIM : (h + 1) * HEAD_DIM]
            for h in range(heads)
        ],
        axis=1,
    ).astype(BF16)


def out_kernel(attended, own, mate, after, partial, gain_out, wbuf, sem):
    rows, width = attended.shape
    core = lax.axis_index("c")
    last = pl.ds(own.shape[1] - wbuf.shape[2], wbuf.shape[2])
    copies = [
        pltpu.make_async_copy(got.at[:, last], wbuf.at[place], sem.at[i])
        for i, (got, place) in enumerate(((own, core), (mate, 1 - core)))
    ]
    for copy in copies:
        copy.start()
    for copy in copies:
        copy.wait()
    feats = width // (NY * NC)
    lanes = wbuf.shape[3]
    tiles = width // lanes
    step = wbuf.shape[2] // tiles
    mine = rows // NX
    for b in range(NZ):
        places = [(c, b * NY + y) for y in range(NY) for c in range(NC)]
        weights = jnp.concatenate(
            [
                jnp.concatenate([wbuf[c, p, t * step : t * step + feats] for c, p in places], axis=0)
                for t in range(tiles)
            ],
            axis=1,
        )
        a = lax.dot_general(attended[...], weights, NT, preferred_element_type=F32)
        for x in range(NX):
            partial[x, :, b * width : (b + 1) * width] = a[x * mine : (x + 1) * mine]
        for t in range(tiles):
            both = None
            for c, p in places:
                piece = wbuf[c, p, t * step + feats : (t + 1) * step].astype(F32)
                both = piece if both is None else both + piece
            gain_out[b, 0:2, t * lanes : (t + 1) * lanes] = both[0:2] + both[2:4]


def fan_kernel(got, rest, gains, own_mid, out):
    total = got[0] + got[1] + got[2] + got[3]
    model = total.shape[1]
    power = jnp.sum(total * total, axis=1, keepdims=True) / model
    gain = jnp.concatenate([gains[z, 0:1] for z in range(NZ)], axis=1)
    mid = (rest[...] + total * lax.rsqrt(power + EPS) * gain).astype(BF16)
    mid32 = mid.astype(F32)
    own_mid[...] = mid32
    message = jnp.concatenate([mid32[:, : model // 2], mid32[:, model // 2 :]], axis=0).astype(BF16)
    for i in range(out.shape[0]):
        out[i] = message


def ffn_kernel(got, own, own_mate, near, near_mate, out, wbuf, sem):
    core = lax.axis_index("c")
    copies = [
        pltpu.make_async_copy(own, wbuf.at[0, core], sem.at[0]),
        pltpu.make_async_copy(own_mate, wbuf.at[0, 1 - core], sem.at[1]),
        pltpu.make_async_copy(near, wbuf.at[1, core], sem.at[2]),
        pltpu.make_async_copy(near_mate, wbuf.at[1, 1 - core], sem.at[3]),
    ]
    for copy in copies:
        copy.start()
    places, lines, span = got.shape
    mine = lines // 2
    whole = [got[d].astype(F32) for d in range(places)]
    mid = [
        jnp.concatenate([w[half * mine : (half + 1) * mine] for w in whole], axis=0).astype(BF16)
        for half in range(2)
    ]
    blocks = wbuf.shape[2]
    feats = wbuf.shape[3] // 3
    for copy in copies:
        copy.wait()

    def weights(part, half):
        rows = range(half * blocks // 2, (half + 1) * blocks // 2)
        return jnp.concatenate(
            [
                jnp.concatenate(
                    [
                        wbuf[p, c, b, part * feats : (part + 1) * feats]
                        for b in rows
                        for c in range(NC)
                    ],
                    axis=0,
                )
                for p in range(2)
            ],
            axis=1,
        )

    gate = jnp.dot(mid[0], weights(0, 0), preferred_element_type=F32)
    gate += jnp.dot(mid[1], weights(0, 1), preferred_element_type=F32)
    lift = jnp.dot(mid[0], weights(1, 0), preferred_element_type=F32)
    lift += jnp.dot(mid[1], weights(1, 1), preferred_element_type=F32)
    act = (gate / (1.0 + jnp.exp(-gate)) * lift).astype(BF16)
    flat = [lax.dot_general(act, weights(2, h), NT, preferred_element_type=F32) for h in range(2)]
    for d in range(places):
        out[d] = jnp.concatenate([f[d * mine : (d + 1) * mine] for f in flat], axis=0).astype(BF16)


def finish_kernel(got, own_mid, gains, out):
    total = got[0].astype(F32)
    for i in range(1, got.shape[0]):
        total += got[i].astype(F32)
    mine = own_mid.shape[0]
    total = jnp.concatenate([total[:mine], total[mine:]], axis=1)
    model = total.shape[1]
    power = jnp.sum(total * total, axis=1, keepdims=True) / model
    gain = jnp.concatenate([gains[z, 1:2] for z in range(NZ)], axis=1)
    hidden = (own_mid[...] + total * lax.rsqrt(power + EPS) * gain).astype(BF16)
    feats = out.shape[2]
    for r in range(model // feats):
        part = hidden[:, r * feats : (r + 1) * feats]
        for x in range(NX):
            out[r * NX + x] = part


def ring(shift, size):
    return [(i, (i + shift) % size) for i in range(size)]


def body(hidden_in, lengths, w_qkv, qk_gain, cache_keys, cache_values, w_out, norm_gain,
         w_gate_up, w_down):
    rows = lengths.shape[0]
    width = w_qkv.shape[2]
    heads = width // HEAD_DIM
    feats = hidden_in.shape[1]
    model = width * NX
    wide = rows * heads
    blocks = cache_keys.shape[0] // BLOCK

    flipped = hidden_in.T
    mate_rows = lax.ppermute(flipped, "c", ring(1, NC))
    mate_w = lax.ppermute(w_qkv, "c", ring(1, NC))
    half = HEAD_DIM // 2
    freqs = jnp.power(THETA, -(jnp.arange(half, dtype=F32) * 2.0 / HEAD_DIM))
    angles = lengths.astype(F32)[:, None] * freqs[None, :]
    cosine = jnp.cos(angles)
    sine = jnp.sin(angles)
    tables = jnp.stack(
        [jnp.concatenate([cosine, cosine], axis=1), jnp.concatenate([-sine, sine], axis=1)]
    )
    ends = jnp.cumsum(lengths)
    bounds = jnp.tile(jnp.stack([ends - lengths, ends], axis=1), (heads, 1))
    gain_table = jnp.concatenate([qk_gain, jnp.zeros((6, width), F32)], axis=0)
    places = NZ * NY
    size = 3 * feats
    lanes = 128
    tiles = width // lanes
    head_lines = (3 * tiles + 1) * rows
    out_lines = tiles * (feats + 8)
    message = call(
        project_kernel,
        shape((places, head_lines + size + out_lines, lanes), BF16),
        [ANY] * 11,
        VMEM,
        [
            pltpu.VMEM((2, feats, flipped.shape[1]), BF16),
            pltpu.VMEM((2,) + w_qkv.shape, BF16),
            pltpu.VMEM((flipped.shape[1], 2 * feats), F32),
            pltpu.VMEM(w_gate_up.shape, BF16),
            pltpu.VMEM(w_down.shape, BF16),
            pltpu.VMEM(w_out.shape, BF16),
            pltpu.VMEM(norm_gain.shape, F32),
            pltpu.SemaphoreType.DMA((8,)),
        ],
        (1 << 27, 2 << 20),
        "project",
        8,
    )(hbm(flipped), mate_rows, hbm(w_qkv), mate_w, hbm(w_gate_up), hbm(w_down), hbm(w_out), hbm(norm_gain),
      tables, bounds, gain_table)
    got = lax.all_to_all(message, Z + ("y",), 0, 0, tiled=True)

    mate = lax.ppermute(got, "c", ring(1, NC))
    qk, value_new, squares, rest, ffn_own = call(
        collect_kernel,
        (
            shape((3, rows, width), F32),
            shape((rows, width), BF16),
            shape((NX, rows, 128), F32),
            shape((rows // NX, model), F32),
            shape((places, size, lanes), BF16),
        ),
        [ANY],
        (VMEM,) * 4 + (ANY,),
        [
            pltpu.VMEM((places, head_lines, lanes), BF16),
            pltpu.VMEM((rows, model), F32),
            pltpu.SemaphoreType.DMA((2,)),
        ],
        (1 << 20, 4 << 20),
        "collect",
        8,
    )(got)
    ffn_mate = lax.ppermute(ffn_own, "c", ring(1, NC))
    near = lax.ppermute(ffn_own, "zl", ring(1, 2))
    squares = lax.all_to_all(squares, "x", 0, 0, tiled=True)
    key_new, attended = call(
        attend_kernel,
        (shape((rows, width), BF16), shape((rows, width), BF16)),
        [VMEM] * 5 + [ANY] * 2,
        (VMEM,) * 2,
        [
            pltpu.VMEM((blocks, wide, BLOCK), F32),
            pltpu.VMEM((wide, 128), F32),
            pltpu.VMEM((blocks, BLOCK, width), BF16),
            pltpu.VMEM((blocks, BLOCK, width), BF16),
            pltpu.VMEM((wide, width), F32),
            pltpu.VMEM((wide, 128), F32),
            pltpu.SemaphoreType.DMA((blocks,)),
            pltpu.SemaphoreType.DMA((blocks,)),
        ],
        (1 << 29, 8 << 20),
        "attend",
        16,
    )(squares, qk, gain_table, tables, bounds, hbm(cache_keys), hbm(cache_values))
    partial, gains = call(
        out_kernel,
        (shape((NX, rows // NX, model), F32), shape((NZ, 8, width), F32)),
        [VMEM] + [ANY] * 3,
        (VMEM,) * 2,
        [
            pltpu.VMEM((NC, places, out_lines, lanes), BF16),
            pltpu.SemaphoreType.DMA((2,)),
        ],
        (1 << 26, 2 << 20),
        "project_out",
        8,
    )(attended, got, mate, ffn_mate)

    summed = lax.all_to_all(partial, "x", 0, 0, tiled=True)
    mine = rows // NX
    group = ("zh", "y", "x")
    members = NZ * NY * NX // 2
    own_mid, message = call(
        fan_kernel,
        (shape((mine, model), F32), shape((members, 2 * mine, model // 2), BF16)),
        [VMEM] * 3,
        (VMEM, VMEM),
        (),
        (1 << 16, 1 << 19),
        "fan",
    )(summed, rest, gains)
    near = call(
        hold_kernel,
        shape(near.shape, BF16),
        [ANY] * 2,
        ANY,
        [pltpu.SemaphoreType.DMA],
        (0, 1 << 20),
        "hold",
        1,
    )(near, own_mid)
    near_mate = lax.ppermute(near, "c", ring(1, NC))
    got = lax.all_to_all(message, group, 0, 0, tiled=True)
    partial = call(
        ffn_kernel,
        shape((members, 2 * mine, model // 2), BF16),
        [VMEM] + [ANY] * 4,
        VMEM,
        [
            pltpu.VMEM((2, NC) + ffn_own.shape, BF16),
            pltpu.SemaphoreType.DMA((4,)),
        ],
        (1 << 28, 4 << 20),
        "feed_forward",
        16,
    )(got, ffn_own, ffn_mate, near, near_mate)
    got = lax.all_to_all(partial, group, 0, 0, tiled=True)
    message = call(
        finish_kernel,
        shape((NZ * NY * NC * NX, mine, feats), BF16),
        [VMEM] * 3,
        VMEM,
        (),
        (1 << 18, 1 << 19),
        "finish",
    )(got, own_mid, gains)
    hidden = lax.all_to_all(message, Z + ("y", "c", "x"), 0, 0, tiled=True)
    return hidden.reshape(-1, feats), key_new, value_new


def solution(mesh):
    fine = Mesh(mesh.devices.reshape(2, 2, NY, NC, NX), Z + ("y", "c", "x"))
    req = Z + ("y", "c")
    return jax.shard_map(
        body,
        mesh=fine,
        in_specs=(
            P(None, req),
            P(req),
            P(None, req, "x"),
            P(None, "x"),
            P(req, "x"),
            P(req, "x"),
            P(req, "x"),
            P(None, req),
            P(None, req, "x"),
            P(req, "x"),
        ),
        out_specs=(P(None, req), P(req, "x"), P(req, "x")),
        check_vma=False,
    )
```

```python
import jax
import jax.numpy as jnp
from jax import lax
from jax.experimental import pallas as pl
from jax.experimental.pallas import tpu as pltpu
from jax.sharding import Mesh, PartitionSpec as P

HEAD_DIM = 128
EPS = 1e-06
THETA = 500000.0
NT = (((1,), (1,)), ((), ()))
BLOCK = 512
F32 = jnp.float32
BF16 = jnp.bfloat16
NZ, NY, NC, NX = 4, 4, 2, 4
Z = ("zh", "zl")
VMEM = pl.BlockSpec(memory_space=pltpu.VMEM)
HBM = pl.BlockSpec(memory_space=pltpu.HBM)
ANY = pl.BlockSpec(memory_space=pl.ANY)
SMEM = pl.BlockSpec(memory_space=pltpu.SMEM)


def call(kernel, out_shape, in_specs, out_specs, scratch=(), cost=(1 << 20, 1 << 20), name=None, limit=4):
    return pl.pallas_call(
        kernel,
        out_shape=out_shape,
        in_specs=in_specs,
        out_specs=out_specs,
        scratch_shapes=list(scratch),
        compiler_params=pltpu.CompilerParams(vmem_limit_bytes=limit * 1024 * 1024),
        cost_estimate=pl.CostEstimate(flops=cost[0], bytes_accessed=cost[1], transcendentals=0),
        name=name,
    )


def hbm(array):
    return pltpu.with_memory_space_constraint(array, pltpu.HBM)


def shape(dims, dtype):
    return jax.ShapeDtypeStruct(dims, dtype)


def hold_kernel(piece, token, out, sem):
    copy = pltpu.make_async_copy(piece, out, sem)
    copy.start()
    copy.wait()


def project_kernel(h_own, h_mate, w_own, w_mate, gate_up, down, out_w, gains, trig, places, out, hbuf,
                   wbuf, rows_buf, gbuf, dbuf, obuf, nbuf, sem):
    core = lax.axis_index("c")
    pairs = (
        (h_own, hbuf.at[core]),
        (h_mate, hbuf.at[1 - core]),
        (w_own, wbuf.at[core]),
        (w_mate, wbuf.at[1 - core]),
        (gate_up, gbuf),
        (down, dbuf),
        (out_w, obuf),
        (gains, nbuf),
    )
    copies = [pltpu.make_async_copy(a, b, sem.at[i]) for i, (a, b) in enumerate(pairs)]
    for copy in copies:
        copy.start()
    copies[0].wait()
    copies[1].wait()
    rows_buf[...] = jnp.concatenate([hbuf[0].astype(F32).T, hbuf[1].astype(F32).T], axis=1)
    blocks, rows, _ = out.shape
    feats, width = w_own.shape[1:]
    lanes = 2 * feats
    chosen = jnp.concatenate(
        [
            rows_buf[pl.ds(pl.multiple_of((2 * b + core) * rows, rows), rows), :]
            for b in range(blocks)
        ],
        axis=0,
    ).astype(BF16)
    copies[2].wait()
    copies[3].wait()
    for g in range(3):
        weights = jnp.concatenate([wbuf[0, g], wbuf[1, g]], axis=0)
        part = jnp.dot(chosen, weights, preferred_element_type=F32).astype(BF16)
        out[:, :, g * width : (g + 1) * width] = part.reshape(blocks, rows, width)
    at = 3 * width
    out[:, :, at : at + lanes] = chosen.reshape(blocks, rows, lanes)
    at += lanes
    for copy in copies[4:]:
        copy.wait()
    steps = feats // rows
    for part in range(3):
        for i in range(steps):
            low = slice(i * rows, (i + 1) * rows)
            for b in range(blocks):
                cols = slice(b * lanes, (b + 1) * lanes)
                out[b, :, at : at + lanes] = dbuf[low, cols] if part == 2 else gbuf[part, low, cols]
            at += lanes
    both = jnp.concatenate([nbuf[0:1, :], nbuf[1:2, :]], axis=1)
    high = both.astype(BF16).astype(F32)
    tile = jnp.concatenate([high, both - high, jnp.zeros((rows - 2, lanes), F32)], axis=0).astype(BF16)
    for b in range(blocks):
        for i in range(steps):
            out[b, :, at + i * width : at + (i + 1) * width] = obuf[i * rows : (i + 1) * rows]
        out[b, :, at + steps * width :] = tile


def quarter(ref, x):
    pair = ref[pl.ds(pl.multiple_of(x // 2 * 8, 8), 8), :]
    return jnp.where(lax.rem(x, 2) == 0, pair[:4], pair[4:])


def collect_kernel(got, qk, value, squares, rest, ffn, buf, rest_buf, sem):
    rows, width = value.shape
    at = buf.shape[2]
    first = pltpu.make_async_copy(got.at[:, :, pl.ds(0, at)], buf, sem.at[0])
    second = pltpu.make_async_copy(got.at[:, :, pl.ds(at, ffn.shape[2])], ffn, sem.at[1])
    first.start()
    second.start()
    first.wait()
    total = buf[0, :, : 3 * width].astype(F32)
    for i in range(1, buf.shape[0]):
        total += buf[i, :, : 3 * width].astype(F32)
    q, k = total[:, :width], total[:, width : 2 * width]
    qk[0] = q
    qk[1] = k
    new = total[:, 2 * width :].astype(BF16)
    value[...] = new
    qk[2] = new.astype(F32)
    lane = lax.broadcasted_iota(jnp.int32, squares.shape[1:], 1)
    both = jnp.where(
        lane < 64, jnp.sum(q * q, axis=1, keepdims=True), jnp.sum(k * k, axis=1, keepdims=True)
    )
    for i in range(NX):
        squares[i] = both
    lanes = at - 3 * width
    for i in range(buf.shape[0]):
        rest_buf[:, i * lanes : (i + 1) * lanes] = buf[i, :, 3 * width :].astype(F32)
    rest[...] = quarter(rest_buf, lax.axis_index("x"))
    second.wait()


def turn(values, cosine, sine):
    heads = values.shape[1] // HEAD_DIM
    parts = []
    for h in range(heads):
        v = values[:, h * HEAD_DIM : (h + 1) * HEAD_DIM]
        parts.append(v * cosine + pltpu.roll(v, HEAD_DIM // 2, 1) * sine)
    return jnp.concatenate(parts, axis=1)


def spread(values, heads):
    rows, width = values.shape
    wide = rows * heads
    row_head = lax.broadcasted_iota(jnp.int32, (wide, width), 0) // rows
    col_head = lax.broadcasted_iota(jnp.int32, (wide, width), 1) // HEAD_DIM
    return jnp.where(row_head == col_head, jnp.concatenate([values] * heads, axis=0), 0.0)


def attend_kernel(squares_in, qk, trig, places, gains_in, keys, values, key_out,
                  out, score, top, kbuf, vbuf, acc, total, gains, ksem, vsem, gsem):
    rows, width = out.shape
    heads = width // HEAD_DIM
    blocks = score.shape[0]
    model = width * NX
    used = jnp.sum(places[0:1, :])
    gain_copy = pltpu.make_async_copy(gains_in, gains, gsem)
    gain_copy.start()

    def fetch(source, buf, sem, i):
        return pltpu.make_async_copy(source.at[pl.ds(i * BLOCK, BLOCK)], buf.at[i], sem.at[i])

    for source, buf, sem in ((keys, kbuf, ksem), (values, vbuf, vsem)):
        for i in range(blocks):
            @pl.when(i * BLOCK < used)
            def _():
                fetch(source, buf, sem, i).start()

    wide = heads * rows
    request = lax.rem(lax.broadcasted_iota(jnp.int32, (wide, 128), 0), rows)
    lane = lax.broadcasted_iota(jnp.int32, (wide, 128), 1)
    lengths = jnp.broadcast_to(places[0:1, :], (wide, 128))
    starts = jnp.sum(jnp.where(lane < request, lengths, 0.0), axis=1, keepdims=True)
    ends = jnp.sum(jnp.where(lane <= request, lengths, 0.0), axis=1, keepdims=True)
    starts = starts.astype(jnp.int32)
    ends = ends.astype(jnp.int32)
    angles = trig[...].T
    half = HEAD_DIM // 2
    cosine = jnp.concatenate([angles[:rows, :half], angles[:rows, :half]], axis=1)
    sine = jnp.concatenate([-angles[:rows, half:], angles[:rows, half:]], axis=1)
    squares = squares_in[0] + squares_in[1] + squares_in[2] + squares_in[3]
    gain_copy.wait()
    q_factor = lax.rsqrt(squares[:, 0:1] / model + EPS)
    k_factor = lax.rsqrt(squares[:, 64:65] / model + EPS)
    query = turn(qk[0] * q_factor * gains[0:1, :], cosine, sine).astype(BF16)
    new_key = turn(qk[1] * k_factor * gains[1:2, :], cosine, sine).astype(BF16)
    key_out[...] = new_key
    scale = HEAD_DIM ** (-0.5)
    q_all = spread(query.astype(F32), heads)
    q_block = q_all.astype(BF16)
    k_all = jnp.concatenate([new_key.astype(F32)] * heads, axis=0)
    v_all = jnp.concatenate([qk[2]] * heads, axis=0)
    own = jnp.sum(q_all * k_all, axis=1, keepdims=True) * scale
    top[...] = jnp.broadcast_to(own, top.shape)
    for i in range(blocks):
        @pl.when(i * BLOCK < used)
        def _():
            fetch(keys, kbuf, ksem, i).wait()
            s = lax.dot_general(q_block, kbuf[i], NT, preferred_element_type=F32) * scale
            place = lax.broadcasted_iota(jnp.int32, s.shape, 1) + i * BLOCK
            s = jnp.where((place >= starts) & (place < ends), s, -jnp.inf)
            score[i] = s
            top[...] = jnp.maximum(top[...], jnp.max(s, axis=1, keepdims=True))
    highest = top[:, 0:1]
    own_weight = jnp.exp(own - highest).astype(BF16).astype(F32)
    total[...] = jnp.broadcast_to(own_weight, total.shape)
    acc[...] = own_weight * v_all
    for i in range(blocks):
        @pl.when(i * BLOCK < used)
        def _():
            fetch(values, vbuf, vsem, i).wait()
            w = jnp.exp(score[i] - highest).astype(BF16)
            total[...] += jnp.sum(w.astype(F32), axis=1, keepdims=True)
            acc[...] += jnp.dot(w, vbuf[i], preferred_element_type=F32)
    result = acc[...] / total[:, 0:1]
    out[...] = jnp.concatenate(
        [
            result[h * rows : (h + 1) * rows, h * HEAD_DIM : (h + 1) * HEAD_DIM]
            for h in range(heads)
        ],
        axis=1,
    ).astype(BF16)


def out_kernel(attended, own, mate, after, partial, gain_out, wbuf, sem):
    rows, width = attended.shape
    core = lax.axis_index("c")
    last = pl.ds(own.shape[2] - wbuf.shape[3], wbuf.shape[3])
    copies = [
        pltpu.make_async_copy(got.at[:, :, last], wbuf.at[place], sem.at[i])
        for i, (got, place) in enumerate(((own, core), (mate, 1 - core)))
    ]
    for copy in copies:
        copy.start()
    for copy in copies:
        copy.wait()
    steps = (wbuf.shape[3] - 128) // width
    mine = rows // NX
    for b in range(NZ):
        weights = jnp.concatenate(
            [
                wbuf[c, b * NY + y, :, i * width : (i + 1) * width]
                for y in range(NY)
                for c in range(NC)
                for i in range(steps)
            ],
            axis=0,
        )
        a = lax.dot_general(attended[...], weights, NT, preferred_element_type=F32)
        for x in range(NX):
            partial[x, :, b * width : (b + 1) * width] = a[x * mine : (x + 1) * mine]
        for y in range(NY):
            two = [wbuf[c, b * NY + y, 0:8, steps * width :].astype(F32) for c in range(NC)]
            two = [t[0:1] + t[1:2] for t in two]
            for g in range(2):
                gain_out[b, g : g + 1, y * 128 : (y + 1) * 128] = jnp.concatenate(
                    [t[:, g * 64 : (g + 1) * 64] for t in two], axis=1
                )


def fan_kernel(got, rest, gains, own_mid, out):
    total = got[0] + got[1] + got[2] + got[3]
    model = total.shape[1]
    power = jnp.sum(total * total, axis=1, keepdims=True) / model
    gain = jnp.concatenate([gains[z, 0:1] for z in range(NZ)], axis=1)
    mid = (rest[...] + total * lax.rsqrt(power + EPS) * gain).astype(BF16)
    mid32 = mid.astype(F32)
    own_mid[...] = mid32
    message = jnp.concatenate([mid32[:, : model // 2], mid32[:, model // 2 :]], axis=0).astype(BF16)
    for i in range(out.shape[0]):
        out[i] = message


def ffn_kernel(got, own, own_mate, near, near_mate, out, wbuf, sem):
    core = lax.axis_index("c")
    copies = [
        pltpu.make_async_copy(own, wbuf.at[0, core], sem.at[0]),
        pltpu.make_async_copy(own_mate, wbuf.at[0, 1 - core], sem.at[1]),
        pltpu.make_async_copy(near, wbuf.at[1, core], sem.at[2]),
        pltpu.make_async_copy(near_mate, wbuf.at[1, 1 - core], sem.at[3]),
    ]
    for copy in copies:
        copy.start()
    places, lines, span = got.shape
    mine = lines // 2
    whole = [got[d].astype(F32) for d in range(places)]
    mid = [
        jnp.concatenate([w[half * mine : (half + 1) * mine] for w in whole], axis=0).astype(BF16)
        for half in range(2)
    ]
    blocks = wbuf.shape[2]
    lanes = 128
    steps = wbuf.shape[4] // (3 * lanes)
    for copy in copies:
        copy.wait()

    def weights(part, half):
        rows = range(half * blocks // 2, (half + 1) * blocks // 2)
        return jnp.concatenate(
            [
                jnp.concatenate(
                    [
                        wbuf[p, c, b, :, (part * steps + i) * lanes : (part * steps + i + 1) * lanes]
                        for b in rows
                        for c in range(NC)
                        for i in range(steps)
                    ],
                    axis=0,
                )
                for p in range(2)
            ],
            axis=1,
        )

    gate = jnp.dot(mid[0], weights(0, 0), preferred_element_type=F32)
    gate += jnp.dot(mid[1], weights(0, 1), preferred_element_type=F32)
    lift = jnp.dot(mid[0], weights(1, 0), preferred_element_type=F32)
    lift += jnp.dot(mid[1], weights(1, 1), preferred_element_type=F32)
    act = (gate / (1.0 + jnp.exp(-gate)) * lift).astype(BF16)
    flat = [lax.dot_general(act, weights(2, h), NT, preferred_element_type=F32) for h in range(2)]
    for d in range(places):
        out[d] = jnp.concatenate([f[d * mine : (d + 1) * mine] for f in flat], axis=0).astype(BF16)


def finish_kernel(got, own_mid, gains, out):
    total = got[0].astype(F32)
    for i in range(1, got.shape[0]):
        total += got[i].astype(F32)
    mine = own_mid.shape[0]
    total = jnp.concatenate([total[:mine], total[mine:]], axis=1)
    model = total.shape[1]
    power = jnp.sum(total * total, axis=1, keepdims=True) / model
    gain = jnp.concatenate([gains[z, 1:2] for z in range(NZ)], axis=1)
    hidden = (own_mid[...] + total * lax.rsqrt(power + EPS) * gain).astype(BF16)
    feats = out.shape[2]
    for r in range(model // feats):
        part = hidden[:, r * feats : (r + 1) * feats]
        for x in range(NX):
            out[r * NX + x] = part


def ring(shift, size):
    return [(i, (i + shift) % size) for i in range(size)]


def body(hidden_in, lengths, w_qkv, qk_gain, cache_keys, cache_values, w_out, norm_gain,
         w_gate_up, w_down):
    rows = lengths.shape[0]
    width = w_qkv.shape[2]
    heads = width // HEAD_DIM
    feats = hidden_in.shape[1]
    model = width * NX
    wide = rows * heads
    blocks = cache_keys.shape[0] // BLOCK

    flipped = hidden_in.T
    mate_rows = lax.ppermute(flipped, "c", ring(1, NC))
    mate_w = lax.ppermute(w_qkv, "c", ring(1, NC))
    half = HEAD_DIM // 2
    freqs = jnp.power(THETA, -(jnp.arange(half, dtype=F32) * 2.0 / HEAD_DIM))
    angles = lengths.astype(F32)[:, None] * freqs[None, :]
    cosine = jnp.cos(angles)
    sine = jnp.sin(angles)
    tables = jnp.stack(
        [jnp.concatenate([cosine, cosine], axis=1), jnp.concatenate([-sine, sine], axis=1)]
    )
    ends = jnp.cumsum(lengths)
    bounds = jnp.tile(jnp.stack([ends - lengths, ends], axis=1), (heads, 1))
    gain_table = jnp.concatenate([qk_gain, jnp.zeros((6, width), F32)], axis=0)
    places = NZ * NY
    half = HEAD_DIM // 2
    freqs = jnp.power(THETA, -(jnp.arange(half, dtype=F32) * 2.0 / HEAD_DIM))
    spots = jnp.pad(lengths.astype(F32), (0, 128 - rows))[None, :]
    angles = freqs[:, None] * spots
    trig = jnp.concatenate([jnp.cos(angles), jnp.sin(angles)], axis=0)
    spots = jnp.broadcast_to(spots, (8, 128))
    lanes = 128
    head_lanes = 3 * width + lanes
    tile_lanes = 3 * feats // rows * lanes
    out_lanes = feats // rows * width + lanes
    message = call(
        project_kernel,
        shape((places, rows, head_lanes + tile_lanes + out_lanes), BF16),
        [ANY] * 10,
        VMEM,
        [
            pltpu.VMEM((2, feats, flipped.shape[1]), BF16),
            pltpu.VMEM((2,) + w_qkv.shape, BF16),
            pltpu.VMEM((flipped.shape[1], 2 * feats), F32),
            pltpu.VMEM(w_gate_up.shape, BF16),
            pltpu.VMEM(w_down.shape, BF16),
            pltpu.VMEM(w_out.shape, BF16),
            pltpu.VMEM(norm_gain.shape, F32),
            pltpu.SemaphoreType.DMA((8,)),
        ],
        (1 << 27, 2 << 20),
        "project",
        8,
    )(hbm(flipped), mate_rows, hbm(w_qkv), mate_w, hbm(w_gate_up), hbm(w_down), hbm(w_out), hbm(norm_gain), trig, spots)
    got = lax.all_to_all(message, Z + ("y",), 0, 0, tiled=True)

    mate = lax.ppermute(got, "c", ring(1, NC))
    qk, value_new, squares, rest, ffn_own = call(
        collect_kernel,
        (
            shape((3, rows, width), F32),
            shape((rows, width), BF16),
            shape((NX, rows, 128), F32),
            shape((rows // NX, model), F32),
            shape((places, rows, tile_lanes), BF16),
        ),
        [ANY],
        (VMEM,) * 4 + (ANY,),
        [
            pltpu.VMEM((places, rows, head_lanes), BF16),
            pltpu.VMEM((rows, model), F32),
            pltpu.SemaphoreType.DMA((2,)),
        ],
        (1 << 20, 4 << 20),
        "collect",
        8,
    )(got)
    ffn_mate = lax.ppermute(ffn_own, "c", ring(1, NC))
    near = lax.ppermute(ffn_own, "zl", ring(1, 2))
    squares = lax.all_to_all(squares, "x", 0, 0, tiled=True)
    key_new, attended = call(
        attend_kernel,
        (shape((rows, width), BF16), shape((rows, width), BF16)),
        [VMEM] * 4 + [ANY] * 3,
        (VMEM,) * 2,
        [
            pltpu.VMEM((blocks, wide, BLOCK), F32),
            pltpu.VMEM((wide, 128), F32),
            pltpu.VMEM((blocks, BLOCK, width), BF16),
            pltpu.VMEM((blocks, BLOCK, width), BF16),
            pltpu.VMEM((wide, width), F32),
            pltpu.VMEM((wide, 128), F32),
            pltpu.VMEM((2, width), F32),
            pltpu.SemaphoreType.DMA((blocks,)),
            pltpu.SemaphoreType.DMA((blocks,)),
            pltpu.SemaphoreType.DMA,
        ],
        (1 << 29, 8 << 20),
        "attend",
        16,
    )(squares, qk, trig, spots, hbm(qk_gain), hbm(cache_keys), hbm(cache_values))
    partial, gains = call(
        out_kernel,
        (shape((NX, rows // NX, model), F32), shape((NZ, 8, width), F32)),
        [VMEM] + [ANY] * 3,
        (VMEM,) * 2,
        [
            pltpu.VMEM((NC, places, rows, out_lanes), BF16),
            pltpu.SemaphoreType.DMA((2,)),
        ],
        (1 << 26, 2 << 20),
        "project_out",
        8,
    )(attended, got, mate, ffn_mate)

    summed = lax.all_to_all(partial, "x", 0, 0, tiled=True)
    mine = rows // NX
    group = ("zh", "y", "x")
    members = NZ * NY * NX // 2
    own_mid, message = call(
        fan_kernel,
        (shape((mine, model), F32), shape((members, 2 * mine, model // 2), BF16)),
        [VMEM] * 3,
        (VMEM, VMEM),
        (),
        (1 << 16, 1 << 19),
        "fan",
    )(summed, rest, gains)
    near = call(
        hold_kernel,
        shape(near.shape, BF16),
        [ANY] * 2,
        ANY,
        [pltpu.SemaphoreType.DMA],
        (0, 1 << 20),
        "hold",
        1,
    )(near, own_mid)
    near_mate = lax.ppermute(near, "c", ring(1, NC))
    got = lax.all_to_all(message, group, 0, 0, tiled=True)
    partial = call(
        ffn_kernel,
        shape((members, 2 * mine, model // 2), BF16),
        [VMEM] + [ANY] * 4,
        VMEM,
        [
            pltpu.VMEM((2, NC) + ffn_own.shape, BF16),
            pltpu.SemaphoreType.DMA((4,)),
        ],
        (1 << 28, 4 << 20),
        "feed_forward",
        16,
    )(got, ffn_own, ffn_mate, near, near_mate)
    got = lax.all_to_all(partial, group, 0, 0, tiled=True)
    message = call(
        finish_kernel,
        shape((NZ * NY * NC * NX, mine, feats), BF16),
        [VMEM] * 3,
        VMEM,
        (),
        (1 << 18, 1 << 19),
        "finish",
    )(got, own_mid, gains)
    hidden = lax.all_to_all(message, Z + ("y", "c", "x"), 0, 0, tiled=True)
    return hidden.reshape(-1, feats), key_new, value_new


def solution(mesh):
    fine = Mesh(mesh.devices.reshape(2, 2, NY, NC, NX), Z + ("y", "c", "x"))
    req = Z + ("y", "c")
    return jax.shard_map(
        body,
        mesh=fine,
        in_specs=(
            P(None, req),
            P(req),
            P(None, req, "x"),
            P(None, "x"),
            P(req, "x"),
            P(req, "x"),
            P(req, "x"),
            P(None, req),
            P(None, req, "x"),
            P(req, "x"),
        ),
        out_specs=(P(None, req), P(req, "x"), P(req, "x")),
        check_vma=False,
    )
```

```python
import jax
import jax.numpy as jnp
from jax import lax
from jax.experimental import pallas as pl
from jax.experimental.pallas import tpu as pltpu
from jax.sharding import Mesh, PartitionSpec as P

HEAD_DIM = 128
EPS = 1e-06
THETA = 500000.0
NT = (((1,), (1,)), ((), ()))
BLOCK = 512
F32 = jnp.float32
BF16 = jnp.bfloat16
NZ, NY, NC, NX = 4, 4, 2, 4
Z = ("zh", "zl")
VMEM = pl.BlockSpec(memory_space=pltpu.VMEM)
HBM = pl.BlockSpec(memory_space=pltpu.HBM)
ANY = pl.BlockSpec(memory_space=pl.ANY)
SMEM = pl.BlockSpec(memory_space=pltpu.SMEM)


def call(kernel, out_shape, in_specs, out_specs, scratch=(), cost=(1 << 20, 1 << 20), name=None, limit=4):
    return pl.pallas_call(
        kernel,
        out_shape=out_shape,
        in_specs=in_specs,
        out_specs=out_specs,
        scratch_shapes=list(scratch),
        compiler_params=pltpu.CompilerParams(vmem_limit_bytes=limit * 1024 * 1024),
        cost_estimate=pl.CostEstimate(flops=cost[0], bytes_accessed=cost[1], transcendentals=0),
        name=name,
    )


def hbm(array):
    return pltpu.with_memory_space_constraint(array, pltpu.HBM)


def shape(dims, dtype):
    return jax.ShapeDtypeStruct(dims, dtype)


def hold_kernel(piece, token, out, sem):
    copy = pltpu.make_async_copy(piece, out, sem)
    copy.start()
    copy.wait()


def project_kernel(h_own, h_mate, w_own, w_mate, gate_up, down, out_w, gains, trig, places, out, hbuf,
                   wbuf, rows_buf, gbuf, dbuf, obuf, nbuf, sem):
    core = lax.axis_index("c")
    pairs = (
        (h_own, hbuf.at[core]),
        (h_mate, hbuf.at[1 - core]),
        (w_own, wbuf.at[core]),
        (w_mate, wbuf.at[1 - core]),
        (gate_up, gbuf),
        (down, dbuf),
        (out_w, obuf),
        (gains, nbuf),
    )
    copies = [pltpu.make_async_copy(a, b, sem.at[i]) for i, (a, b) in enumerate(pairs)]
    for copy in copies:
        copy.start()
    copies[0].wait()
    copies[1].wait()
    rows_buf[...] = jnp.concatenate([hbuf[0].astype(F32).T, hbuf[1].astype(F32).T], axis=1)
    blocks, rows, _ = out.shape
    feats, width = w_own.shape[1:]
    lanes = 2 * feats
    chosen = jnp.concatenate(
        [
            rows_buf[pl.ds(pl.multiple_of((2 * b + core) * rows, rows), rows), :]
            for b in range(blocks)
        ],
        axis=0,
    ).astype(BF16)
    copies[2].wait()
    copies[3].wait()
    for g in range(3):
        weights = jnp.concatenate([wbuf[0, g], wbuf[1, g]], axis=0)
        part = jnp.dot(chosen, weights, preferred_element_type=F32).astype(BF16)
        out[:, :, g * width : (g + 1) * width] = part.reshape(blocks, rows, width)
    at = 3 * width
    out[:, :, at : at + lanes] = chosen.reshape(blocks, rows, lanes)
    at += lanes
    for copy in copies[4:]:
        copy.wait()
    steps = feats // rows
    for part in range(3):
        for i in range(steps):
            low = slice(i * rows, (i + 1) * rows)
            for b in range(blocks):
                cols = slice(b * lanes, (b + 1) * lanes)
                out[b, :, at : at + lanes] = dbuf[low, cols] if part == 2 else gbuf[part, low, cols]
            at += lanes
    both = jnp.concatenate([nbuf[0:1, :], nbuf[1:2, :]], axis=1)
    high = both.astype(BF16).astype(F32)
    tile = jnp.concatenate([high, both - high, jnp.zeros((rows - 2, lanes), F32)], axis=0).astype(BF16)
    for b in range(blocks):
        for i in range(steps):
            out[b, :, at + i * width : at + (i + 1) * width] = obuf[i * rows : (i + 1) * rows]
        out[b, :, at + steps * width :] = tile


def quarter(ref, x):
    pair = ref[pl.ds(pl.multiple_of(x // 2 * 8, 8), 8), :]
    return jnp.where(lax.rem(x, 2) == 0, pair[:4], pair[4:])


def collect_kernel(got, gains, qk, value, squares, rest, gains_out, ffn, buf, rest_buf, sem):
    rows, width = value.shape
    at = buf.shape[2]
    first = pltpu.make_async_copy(got.at[:, :, pl.ds(0, at)], buf, sem.at[0])
    second = pltpu.make_async_copy(got.at[:, :, pl.ds(at, ffn.shape[2])], ffn, sem.at[1])
    third = pltpu.make_async_copy(gains, gains_out, sem.at[2])
    first.start()
    third.start()
    second.start()
    first.wait()
    total = buf[0, :, : 3 * width].astype(F32)
    for i in range(1, buf.shape[0]):
        total += buf[i, :, : 3 * width].astype(F32)
    q, k = total[:, :width], total[:, width : 2 * width]
    qk[0] = q
    qk[1] = k
    new = total[:, 2 * width :].astype(BF16)
    value[...] = new
    qk[2] = new.astype(F32)
    lane = lax.broadcasted_iota(jnp.int32, squares.shape[1:], 1)
    both = jnp.where(
        lane < 64, jnp.sum(q * q, axis=1, keepdims=True), jnp.sum(k * k, axis=1, keepdims=True)
    )
    for i in range(NX):
        squares[i] = both
    lanes = at - 3 * width
    for i in range(buf.shape[0]):
        rest_buf[:, i * lanes : (i + 1) * lanes] = buf[i, :, 3 * width :].astype(F32)
    rest[...] = quarter(rest_buf, lax.axis_index("x"))
    second.wait()
    third.wait()


def turn(values, cosine, sine):
    heads = values.shape[1] // HEAD_DIM
    parts = []
    for h in range(heads):
        v = values[:, h * HEAD_DIM : (h + 1) * HEAD_DIM]
        parts.append(v * cosine + pltpu.roll(v, HEAD_DIM // 2, 1) * sine)
    return jnp.concatenate(parts, axis=1)


def spread(values, heads):
    rows, width = values.shape
    wide = rows * heads
    row_head = lax.broadcasted_iota(jnp.int32, (wide, width), 0) // rows
    col_head = lax.broadcasted_iota(jnp.int32, (wide, width), 1) // HEAD_DIM
    return jnp.where(row_head == col_head, jnp.concatenate([values] * heads, axis=0), 0.0)


def attend_kernel(squares_in, qk, trig, places, gains, keys, values, key_out,
                  out, score):
    rows, width = out.shape
    heads = width // HEAD_DIM
    blocks = score.shape[0]
    model = width * NX
    used = jnp.sum(places[0:1, :])
    wide = heads * rows
    request = lax.rem(lax.broadcasted_iota(jnp.int32, (wide, 128), 0), rows)
    lane = lax.broadcasted_iota(jnp.int32, (wide, 128), 1)
    lengths = jnp.broadcast_to(places[0:1, :], (wide, 128))
    starts = jnp.sum(jnp.where(lane < request, lengths, 0.0), axis=1, keepdims=True)
    ends = jnp.sum(jnp.where(lane <= request, lengths, 0.0), axis=1, keepdims=True)
    starts = starts.astype(jnp.int32)
    ends = ends.astype(jnp.int32)
    angles = trig[...].T
    half = HEAD_DIM // 2
    cosine = jnp.concatenate([angles[:rows, :half], angles[:rows, :half]], axis=1)
    sine = jnp.concatenate([-angles[:rows, half:], angles[:rows, half:]], axis=1)
    squares = squares_in[0] + squares_in[1] + squares_in[2] + squares_in[3]
    q_factor = lax.rsqrt(squares[:, 0:1] / model + EPS)
    k_factor = lax.rsqrt(squares[:, 64:65] / model + EPS)
    query = turn(qk[0] * q_factor * gains[0:1, :], cosine, sine).astype(BF16)
    new_key = turn(qk[1] * k_factor * gains[1:2, :], cosine, sine).astype(BF16)
    key_out[...] = new_key
    scale = HEAD_DIM ** (-0.5)
    q_all = spread(query.astype(F32), heads)
    q_block = q_all.astype(BF16)
    k_all = jnp.concatenate([new_key.astype(F32)] * heads, axis=0)
    v_all = jnp.concatenate([qk[2]] * heads, axis=0)
    own = jnp.sum(q_all * k_all, axis=1, keepdims=True) * scale
    def raw(i):
        rows_here = keys[pl.ds(i * BLOCK, BLOCK), :]
        s = lax.dot_general(q_block, rows_here, NT, preferred_element_type=F32) * scale
        place = lax.broadcasted_iota(jnp.int32, s.shape, 1) + i * BLOCK
        return jnp.where((place >= starts) & (place < ends), s, -jnp.inf)

    def finish(size):
        highest = own
        for i in range(size):
            s = raw(i)
            score[i] = s
            highest = jnp.maximum(highest, jnp.max(s, axis=1, keepdims=True))
        own_weight = jnp.exp(own - highest).astype(BF16).astype(F32)
        total = own_weight
        acc = own_weight * v_all
        for i in range(size):
            w = jnp.exp(score[i] - highest).astype(BF16)
            total += jnp.sum(w.astype(F32), axis=1, keepdims=True)
            acc += jnp.dot(w, values[pl.ds(i * BLOCK, BLOCK), :], preferred_element_type=F32)
        result = acc / total
        out[...] = jnp.concatenate(
            [
                result[h * rows : (h + 1) * rows, h * HEAD_DIM : (h + 1) * HEAD_DIM]
                for h in range(heads)
            ],
            axis=1,
        ).astype(BF16)

    short = 2

    @pl.when(used <= short * BLOCK)
    def _():
        finish(short)

    @pl.when(used > short * BLOCK)
    def _():
        finish(blocks)


def out_kernel(attended, own, mate, after, partial, gain_out, wbuf, sem):
    rows, width = attended.shape
    core = lax.axis_index("c")
    last = pl.ds(own.shape[2] - wbuf.shape[3], wbuf.shape[3])
    copies = [
        pltpu.make_async_copy(got.at[:, :, last], wbuf.at[place], sem.at[i])
        for i, (got, place) in enumerate(((own, core), (mate, 1 - core)))
    ]
    for copy in copies:
        copy.start()
    for copy in copies:
        copy.wait()
    steps = (wbuf.shape[3] - 128) // width
    mine = rows // NX
    for b in range(NZ):
        weights = jnp.concatenate(
            [
                wbuf[c, b * NY + y, :, i * width : (i + 1) * width]
                for y in range(NY)
                for c in range(NC)
                for i in range(steps)
            ],
            axis=0,
        )
        a = lax.dot_general(attended[...], weights, NT, preferred_element_type=F32)
        for x in range(NX):
            partial[x, :, b * width : (b + 1) * width] = a[x * mine : (x + 1) * mine]
        for y in range(NY):
            two = [wbuf[c, b * NY + y, 0:8, steps * width :].astype(F32) for c in range(NC)]
            two = [t[0:1] + t[1:2] for t in two]
            for g in range(2):
                gain_out[b, g : g + 1, y * 128 : (y + 1) * 128] = jnp.concatenate(
                    [t[:, g * 64 : (g + 1) * 64] for t in two], axis=1
                )


def fan_kernel(got, rest, gains, own_mid, out):
    total = got[0] + got[1] + got[2] + got[3]
    model = total.shape[1]
    power = jnp.sum(total * total, axis=1, keepdims=True) / model
    gain = jnp.concatenate([gains[z, 0:1] for z in range(NZ)], axis=1)
    mid = (rest[...] + total * lax.rsqrt(power + EPS) * gain).astype(BF16)
    mid32 = mid.astype(F32)
    own_mid[...] = mid32
    message = jnp.concatenate([mid32[:, : model // 2], mid32[:, model // 2 :]], axis=0).astype(BF16)
    for i in range(out.shape[0]):
        out[i] = message


def ffn_kernel(got, own, own_mate, near, near_mate, out, wbuf, sem):
    core = lax.axis_index("c")
    copies = [
        pltpu.make_async_copy(own, wbuf.at[0, core], sem.at[0]),
        pltpu.make_async_copy(own_mate, wbuf.at[0, 1 - core], sem.at[1]),
        pltpu.make_async_copy(near, wbuf.at[1, core], sem.at[2]),
        pltpu.make_async_copy(near_mate, wbuf.at[1, 1 - core], sem.at[3]),
    ]
    for copy in copies:
        copy.start()
    places, lines, span = got.shape
    mine = lines // 2
    whole = [got[d].astype(F32) for d in range(places)]
    mid = [
        jnp.concatenate([w[half * mine : (half + 1) * mine] for w in whole], axis=0).astype(BF16)
        for half in range(2)
    ]
    blocks = wbuf.shape[2]
    lanes = 128
    steps = wbuf.shape[4] // (3 * lanes)
    for copy in copies:
        copy.wait()

    def weights(part, half):
        rows = range(half * blocks // 2, (half + 1) * blocks // 2)
        return jnp.concatenate(
            [
                jnp.concatenate(
                    [
                        wbuf[p, c, b, :, (part * steps + i) * lanes : (part * steps + i + 1) * lanes]
                        for b in rows
                        for c in range(NC)
                        for i in range(steps)
                    ],
                    axis=0,
                )
                for p in range(2)
            ],
            axis=1,
        )

    gate = jnp.dot(mid[0], weights(0, 0), preferred_element_type=F32)
    gate += jnp.dot(mid[1], weights(0, 1), preferred_element_type=F32)
    lift = jnp.dot(mid[0], weights(1, 0), preferred_element_type=F32)
    lift += jnp.dot(mid[1], weights(1, 1), preferred_element_type=F32)
    act = (gate / (1.0 + jnp.exp(-gate)) * lift).astype(BF16)
    flat = [lax.dot_general(act, weights(2, h), NT, preferred_element_type=F32) for h in range(2)]
    for d in range(places):
        out[d] = jnp.concatenate([f[d * mine : (d + 1) * mine] for f in flat], axis=0).astype(BF16)


def finish_kernel(got, own_mid, gains, out):
    total = got[0].astype(F32)
    for i in range(1, got.shape[0]):
        total += got[i].astype(F32)
    mine = own_mid.shape[0]
    total = jnp.concatenate([total[:mine], total[mine:]], axis=1)
    model = total.shape[1]
    power = jnp.sum(total * total, axis=1, keepdims=True) / model
    gain = jnp.concatenate([gains[z, 1:2] for z in range(NZ)], axis=1)
    hidden = (own_mid[...] + total * lax.rsqrt(power + EPS) * gain).astype(BF16)
    feats = out.shape[2]
    for r in range(model // feats):
        part = hidden[:, r * feats : (r + 1) * feats]
        for x in range(NX):
            out[r * NX + x] = part


def ring(shift, size):
    return [(i, (i + shift) % size) for i in range(size)]


def body(hidden_in, lengths, w_qkv, qk_gain, cache_keys, cache_values, w_out, norm_gain,
         w_gate_up, w_down):
    rows = lengths.shape[0]
    width = w_qkv.shape[2]
    heads = width // HEAD_DIM
    feats = hidden_in.shape[1]
    model = width * NX
    wide = rows * heads
    blocks = cache_keys.shape[0] // BLOCK

    flipped = hidden_in.T
    mate_rows = lax.ppermute(flipped, "c", ring(1, NC))
    mate_w = lax.ppermute(w_qkv, "c", ring(1, NC))
    half = HEAD_DIM // 2
    freqs = jnp.power(THETA, -(jnp.arange(half, dtype=F32) * 2.0 / HEAD_DIM))
    angles = lengths.astype(F32)[:, None] * freqs[None, :]
    cosine = jnp.cos(angles)
    sine = jnp.sin(angles)
    tables = jnp.stack(
        [jnp.concatenate([cosine, cosine], axis=1), jnp.concatenate([-sine, sine], axis=1)]
    )
    ends = jnp.cumsum(lengths)
    bounds = jnp.tile(jnp.stack([ends - lengths, ends], axis=1), (heads, 1))
    gain_table = jnp.concatenate([qk_gain, jnp.zeros((6, width), F32)], axis=0)
    places = NZ * NY
    half = HEAD_DIM // 2
    freqs = jnp.power(THETA, -(jnp.arange(half, dtype=F32) * 2.0 / HEAD_DIM))
    spots = jnp.pad(lengths.astype(F32), (0, 128 - rows))[None, :]
    angles = freqs[:, None] * spots
    trig = jnp.concatenate([jnp.cos(angles), jnp.sin(angles)], axis=0)
    spots = jnp.broadcast_to(spots, (8, 128))
    lanes = 128
    head_lanes = 3 * width + lanes
    tile_lanes = 3 * feats // rows * lanes
    out_lanes = feats // rows * width + lanes
    message = call(
        project_kernel,
        shape((places, rows, head_lanes + tile_lanes + out_lanes), BF16),
        [ANY] * 10,
        VMEM,
        [
            pltpu.VMEM((2, feats, flipped.shape[1]), BF16),
            pltpu.VMEM((2,) + w_qkv.shape, BF16),
            pltpu.VMEM((flipped.shape[1], 2 * feats), F32),
            pltpu.VMEM(w_gate_up.shape, BF16),
            pltpu.VMEM(w_down.shape, BF16),
            pltpu.VMEM(w_out.shape, BF16),
            pltpu.VMEM(norm_gain.shape, F32),
            pltpu.SemaphoreType.DMA((8,)),
        ],
        (1 << 27, 2 << 20),
        "project",
        8,
    )(hbm(flipped), mate_rows, hbm(w_qkv), mate_w, hbm(w_gate_up), hbm(w_down), hbm(w_out), hbm(norm_gain), trig, spots)
    got = lax.all_to_all(message, Z + ("y",), 0, 0, tiled=True)

    mate = lax.ppermute(got, "c", ring(1, NC))
    qk, value_new, squares, rest, gains_here, ffn_own = call(
        collect_kernel,
        (
            shape((3, rows, width), F32),
            shape((rows, width), BF16),
            shape((NX, rows, 128), F32),
            shape((rows // NX, model), F32),
            shape(qk_gain.shape, F32),
            shape((places, rows, tile_lanes), BF16),
        ),
        [ANY] * 2,
        (VMEM,) * 5 + (ANY,),
        [
            pltpu.VMEM((places, rows, head_lanes), BF16),
            pltpu.VMEM((rows, model), F32),
            pltpu.SemaphoreType.DMA((3,)),
        ],
        (1 << 20, 4 << 20),
        "collect",
        8,
    )(got, hbm(qk_gain))
    ffn_mate = lax.ppermute(ffn_own, "c", ring(1, NC))
    near = lax.ppermute(ffn_own, "zl", ring(1, 2))
    squares = lax.all_to_all(squares, "x", 0, 0, tiled=True)
    key_new, attended = call(
        attend_kernel,
        (shape((rows, width), BF16), shape((rows, width), BF16)),
        [VMEM] * 7,
        (VMEM,) * 2,
        [pltpu.VMEM((blocks, wide, BLOCK), F32)],
        (1 << 29, 8 << 20),
        "attend",
        16,
    )(squares, qk, trig, spots, gains_here, cache_keys, cache_values)
    partial, gains = call(
        out_kernel,
        (shape((NX, rows // NX, model), F32), shape((NZ, 8, width), F32)),
        [VMEM] + [ANY] * 3,
        (VMEM,) * 2,
        [
            pltpu.VMEM((NC, places, rows, out_lanes), BF16),
            pltpu.SemaphoreType.DMA((2,)),
        ],
        (1 << 26, 2 << 20),
        "project_out",
        8,
    )(attended, got, mate, ffn_mate)

    summed = lax.all_to_all(partial, "x", 0, 0, tiled=True)
    mine = rows // NX
    group = ("zh", "y", "x")
    members = NZ * NY * NX // 2
    own_mid, message = call(
        fan_kernel,
        (shape((mine, model), F32), shape((members, 2 * mine, model // 2), BF16)),
        [VMEM] * 3,
        (VMEM, VMEM),
        (),
        (1 << 16, 1 << 19),
        "fan",
    )(summed, rest, gains)
    near = call(
        hold_kernel,
        shape(near.shape, BF16),
        [ANY] * 2,
        ANY,
        [pltpu.SemaphoreType.DMA],
        (0, 1 << 20),
        "hold",
        1,
    )(near, own_mid)
    near_mate = lax.ppermute(near, "c", ring(1, NC))
    got = lax.all_to_all(message, group, 0, 0, tiled=True)
    partial = call(
        ffn_kernel,
        shape((members, 2 * mine, model // 2), BF16),
        [VMEM] + [ANY] * 4,
        VMEM,
        [
            pltpu.VMEM((2, NC) + ffn_own.shape, BF16),
            pltpu.SemaphoreType.DMA((4,)),
        ],
        (1 << 28, 4 << 20),
        "feed_forward",
        16,
    )(got, ffn_own, ffn_mate, near, near_mate)
    got = lax.all_to_all(partial, group, 0, 0, tiled=True)
    message = call(
        finish_kernel,
        shape((NZ * NY * NC * NX, mine, feats), BF16),
        [VMEM] * 3,
        VMEM,
        (),
        (1 << 18, 1 << 19),
        "finish",
    )(got, own_mid, gains)
    hidden = lax.all_to_all(message, Z + ("y", "c", "x"), 0, 0, tiled=True)
    return hidden.reshape(-1, feats), key_new, value_new


def solution(mesh):
    fine = Mesh(mesh.devices.reshape(2, 2, NY, NC, NX), Z + ("y", "c", "x"))
    req = Z + ("y", "c")
    return jax.shard_map(
        body,
        mesh=fine,
        in_specs=(
            P(None, req),
            P(req),
            P(None, req, "x"),
            P(None, "x"),
            P(req, "x"),
            P(req, "x"),
            P(req, "x"),
            P(None, req),
            P(None, req, "x"),
            P(req, "x"),
        ),
        out_specs=(P(None, req), P(req, "x"), P(req, "x")),
        check_vma=False,
    )
```

```python
import jax
import jax.numpy as jnp
from jax import lax
from jax.experimental import pallas as pl
from jax.experimental.pallas import tpu as pltpu
from jax.sharding import Mesh, PartitionSpec as P

HEAD_DIM = 128
EPS = 1e-06
THETA = 500000.0
NT = (((1,), (1,)), ((), ()))
BLOCK = 512
F32 = jnp.float32
BF16 = jnp.bfloat16
NZ, NY, NC, NX = 4, 4, 2, 4
Z = ("zh", "zl")
VMEM = pl.BlockSpec(memory_space=pltpu.VMEM)
HBM = pl.BlockSpec(memory_space=pltpu.HBM)
ANY = pl.BlockSpec(memory_space=pl.ANY)
SMEM = pl.BlockSpec(memory_space=pltpu.SMEM)


def call(kernel, out_shape, in_specs, out_specs, scratch=(), cost=(1 << 20, 1 << 20), name=None, limit=4):
    return pl.pallas_call(
        kernel,
        out_shape=out_shape,
        in_specs=in_specs,
        out_specs=out_specs,
        scratch_shapes=list(scratch),
        compiler_params=pltpu.CompilerParams(vmem_limit_bytes=limit * 1024 * 1024),
        cost_estimate=pl.CostEstimate(flops=cost[0], bytes_accessed=cost[1], transcendentals=0),
        name=name,
    )


def hbm(array):
    return pltpu.with_memory_space_constraint(array, pltpu.HBM)


def shape(dims, dtype):
    return jax.ShapeDtypeStruct(dims, dtype)


def hold_kernel(piece, token, out, sem):
    copy = pltpu.make_async_copy(piece, out, sem)
    copy.start()
    copy.wait()


def project_kernel(h_own, h_mate, w_own, w_mate, gate_up, down, out_w, gains, trig, places, out, hbuf,
                   wbuf, rows_buf, gbuf, dbuf, obuf, nbuf, sem):
    core = lax.axis_index("c")
    pairs = (
        (h_own, hbuf.at[core]),
        (h_mate, hbuf.at[1 - core]),
        (w_own, wbuf.at[core]),
        (w_mate, wbuf.at[1 - core]),
        (gate_up, gbuf),
        (down, dbuf),
        (out_w, obuf),
        (gains, nbuf),
    )
    copies = [pltpu.make_async_copy(a, b, sem.at[i]) for i, (a, b) in enumerate(pairs)]
    for copy in copies:
        copy.start()
    copies[0].wait()
    copies[1].wait()
    rows_buf[...] = jnp.concatenate([hbuf[0].astype(F32).T, hbuf[1].astype(F32).T], axis=1)
    blocks, rows, _ = out.shape
    feats, width = w_own.shape[1:]
    lanes = 2 * feats
    chosen = jnp.concatenate(
        [
            rows_buf[pl.ds(pl.multiple_of((2 * b + core) * rows, rows), rows), :]
            for b in range(blocks)
        ],
        axis=0,
    ).astype(BF16)
    copies[2].wait()
    copies[3].wait()
    for g in range(3):
        weights = jnp.concatenate([wbuf[0, g], wbuf[1, g]], axis=0)
        part = jnp.dot(chosen, weights, preferred_element_type=F32).astype(BF16)
        out[:, :, g * width : (g + 1) * width] = part.reshape(blocks, rows, width)
    at = 3 * width
    out[:, :, at : at + lanes] = chosen.reshape(blocks, rows, lanes)
    at += lanes
    for copy in copies[4:]:
        copy.wait()
    steps = feats // rows
    for part in range(3):
        for i in range(steps):
            low = slice(i * rows, (i + 1) * rows)
            for b in range(blocks):
                cols = slice(b * lanes, (b + 1) * lanes)
                out[b, :, at : at + lanes] = dbuf[low, cols] if part == 2 else gbuf[part, low, cols]
            at += lanes
    both = jnp.concatenate([nbuf[0:1, :], nbuf[1:2, :]], axis=1)
    high = both.astype(BF16).astype(F32)
    tile = jnp.concatenate([high, both - high, jnp.zeros((rows - 2, lanes), F32)], axis=0).astype(BF16)
    for b in range(blocks):
        for i in range(steps):
            out[b, :, at + i * width : at + (i + 1) * width] = obuf[i * rows : (i + 1) * rows]
        out[b, :, at + steps * width :] = tile


def quarter(ref, x):
    pair = ref[pl.ds(pl.multiple_of(x // 2 * 8, 8), 8), :]
    return jnp.where(lax.rem(x, 2) == 0, pair[:4], pair[4:])


def collect_kernel(got, qk, value, squares, rest, ffn, buf, rest_buf, sem):
    rows, width = value.shape
    at = buf.shape[2]
    first = pltpu.make_async_copy(got.at[:, :, pl.ds(0, at)], buf, sem.at[0])
    second = pltpu.make_async_copy(got.at[:, :, pl.ds(at, ffn.shape[2])], ffn, sem.at[1])
    first.start()
    second.start()
    first.wait()
    total = buf[0, :, : 3 * width].astype(F32)
    for i in range(1, buf.shape[0]):
        total += buf[i, :, : 3 * width].astype(F32)
    q, k = total[:, :width], total[:, width : 2 * width]
    qk[0] = q
    qk[1] = k
    new = total[:, 2 * width :].astype(BF16)
    value[...] = new
    qk[2] = new.astype(F32)
    lane = lax.broadcasted_iota(jnp.int32, squares.shape[1:], 1)
    both = jnp.where(
        lane < 64, jnp.sum(q * q, axis=1, keepdims=True), jnp.sum(k * k, axis=1, keepdims=True)
    )
    for i in range(NX):
        squares[i] = both
    lanes = at - 3 * width
    for i in range(buf.shape[0]):
        rest_buf[:, i * lanes : (i + 1) * lanes] = buf[i, :, 3 * width :].astype(F32)
    rest[...] = quarter(rest_buf, lax.axis_index("x"))
    second.wait()


def turn(values, cosine, sine):
    heads = values.shape[1] // HEAD_DIM
    parts = []
    for h in range(heads):
        v = values[:, h * HEAD_DIM : (h + 1) * HEAD_DIM]
        parts.append(v * cosine + pltpu.roll(v, HEAD_DIM // 2, 1) * sine)
    return jnp.concatenate(parts, axis=1)


def spread(values, heads):
    rows, width = values.shape
    wide = rows * heads
    row_head = lax.broadcasted_iota(jnp.int32, (wide, width), 0) // rows
    col_head = lax.broadcasted_iota(jnp.int32, (wide, width), 1) // HEAD_DIM
    return jnp.where(row_head == col_head, jnp.concatenate([values] * heads, axis=0), 0.0)


def attend_kernel(squares_in, qk, trig, places, gains, keys, values, key_out,
                  out, score):
    rows, width = out.shape
    heads = width // HEAD_DIM
    blocks = score.shape[0]
    model = width * NX
    used = jnp.sum(places[0:1, :])
    wide = heads * rows
    request = lax.rem(lax.broadcasted_iota(jnp.int32, (wide, 128), 0), rows)
    lane = lax.broadcasted_iota(jnp.int32, (wide, 128), 1)
    lengths = jnp.broadcast_to(places[0:1, :], (wide, 128))
    starts = jnp.sum(jnp.where(lane < request, lengths, 0.0), axis=1, keepdims=True)
    ends = jnp.sum(jnp.where(lane <= request, lengths, 0.0), axis=1, keepdims=True)
    starts = starts.astype(jnp.int32)
    ends = ends.astype(jnp.int32)
    angles = trig[...].T
    half = HEAD_DIM // 2
    cosine = jnp.concatenate([angles[:rows, :half], angles[:rows, :half]], axis=1)
    sine = jnp.concatenate([-angles[:rows, half:], angles[:rows, half:]], axis=1)
    squares = squares_in[0] + squares_in[1] + squares_in[2] + squares_in[3]
    q_factor = lax.rsqrt(squares[:, 0:1] / model + EPS)
    k_factor = lax.rsqrt(squares[:, 64:65] / model + EPS)
    query = turn(qk[0] * q_factor * gains[0:1, :], cosine, sine).astype(BF16)
    new_key = turn(qk[1] * k_factor * gains[1:2, :], cosine, sine).astype(BF16)
    key_out[...] = new_key
    scale = HEAD_DIM ** (-0.5)
    q_all = spread(query.astype(F32), heads)
    q_block = q_all.astype(BF16)
    k_all = jnp.concatenate([new_key.astype(F32)] * heads, axis=0)
    v_all = jnp.concatenate([qk[2]] * heads, axis=0)
    own = jnp.sum(q_all * k_all, axis=1, keepdims=True) * scale
    def raw(i):
        rows_here = keys[pl.ds(i * BLOCK, BLOCK), :]
        s = lax.dot_general(q_block, rows_here, NT, preferred_element_type=F32) * scale
        place = lax.broadcasted_iota(jnp.int32, s.shape, 1) + i * BLOCK
        return jnp.where((place >= starts) & (place < ends), s, -jnp.inf)

    def finish(size):
        highest = own
        for i in range(size):
            s = raw(i)
            score[i] = s
            highest = jnp.maximum(highest, jnp.max(s, axis=1, keepdims=True))
        own_weight = jnp.exp(own - highest).astype(BF16).astype(F32)
        total = own_weight
        acc = own_weight * v_all
        for i in range(size):
            w = jnp.exp(score[i] - highest).astype(BF16)
            total += jnp.sum(w.astype(F32), axis=1, keepdims=True)
            acc += jnp.dot(w, values[pl.ds(i * BLOCK, BLOCK), :], preferred_element_type=F32)
        result = acc / total
        out[...] = jnp.concatenate(
            [
                result[h * rows : (h + 1) * rows, h * HEAD_DIM : (h + 1) * HEAD_DIM]
                for h in range(heads)
            ],
            axis=1,
        ).astype(BF16)

    short = 2

    @pl.when(used <= short * BLOCK)
    def _():
        finish(short)

    @pl.when(used > short * BLOCK)
    def _():
        finish(blocks)


def out_kernel(attended, own, mate, after, partial, gain_out, wbuf, sem):
    rows, width = attended.shape
    core = lax.axis_index("c")
    last = pl.ds(own.shape[2] - wbuf.shape[3], wbuf.shape[3])
    copies = [
        pltpu.make_async_copy(got.at[:, :, last], wbuf.at[place], sem.at[i])
        for i, (got, place) in enumerate(((own, core), (mate, 1 - core)))
    ]
    for copy in copies:
        copy.start()
    for copy in copies:
        copy.wait()
    steps = (wbuf.shape[3] - 128) // width
    mine = rows // NX
    for b in range(NZ):
        weights = jnp.concatenate(
            [
                wbuf[c, b * NY + y, :, i * width : (i + 1) * width]
                for y in range(NY)
                for c in range(NC)
                for i in range(steps)
            ],
            axis=0,
        )
        a = lax.dot_general(attended[...], weights, NT, preferred_element_type=F32)
        for x in range(NX):
            partial[x, :, b * width : (b + 1) * width] = a[x * mine : (x + 1) * mine]
        for y in range(NY):
            two = [wbuf[c, b * NY + y, 0:8, steps * width :].astype(F32) for c in range(NC)]
            two = [t[0:1] + t[1:2] for t in two]
            for g in range(2):
                gain_out[b, g : g + 1, y * 128 : (y + 1) * 128] = jnp.concatenate(
                    [t[:, g * 64 : (g + 1) * 64] for t in two], axis=1
                )


def fan_kernel(got, rest, gains, own_mid, out):
    total = got[0] + got[1] + got[2] + got[3]
    model = total.shape[1]
    power = jnp.sum(total * total, axis=1, keepdims=True) / model
    gain = jnp.concatenate([gains[z, 0:1] for z in range(NZ)], axis=1)
    mid = (rest[...] + total * lax.rsqrt(power + EPS) * gain).astype(BF16)
    mid32 = mid.astype(F32)
    own_mid[...] = mid32
    message = jnp.concatenate([mid32[:, : model // 2], mid32[:, model // 2 :]], axis=0).astype(BF16)
    for i in range(out.shape[0]):
        out[i] = message


def ffn_kernel(got, own, own_mate, near, near_mate, out, wbuf, sem):
    core = lax.axis_index("c")
    copies = [
        pltpu.make_async_copy(own, wbuf.at[0, core], sem.at[0]),
        pltpu.make_async_copy(own_mate, wbuf.at[0, 1 - core], sem.at[1]),
        pltpu.make_async_copy(near, wbuf.at[1, core], sem.at[2]),
        pltpu.make_async_copy(near_mate, wbuf.at[1, 1 - core], sem.at[3]),
    ]
    for copy in copies:
        copy.start()
    places, lines, span = got.shape
    mine = lines // 2
    whole = [got[d].astype(F32) for d in range(places)]
    mid = [
        jnp.concatenate([w[half * mine : (half + 1) * mine] for w in whole], axis=0).astype(BF16)
        for half in range(2)
    ]
    blocks = wbuf.shape[2]
    lanes = 128
    steps = wbuf.shape[4] // (3 * lanes)
    for copy in copies:
        copy.wait()

    def weights(part, half):
        rows = range(half * blocks // 2, (half + 1) * blocks // 2)
        return jnp.concatenate(
            [
                jnp.concatenate(
                    [
                        wbuf[p, c, b, :, (part * steps + i) * lanes : (part * steps + i + 1) * lanes]
                        for b in rows
                        for c in range(NC)
                        for i in range(steps)
                    ],
                    axis=0,
                )
                for p in range(2)
            ],
            axis=1,
        )

    gate = jnp.dot(mid[0], weights(0, 0), preferred_element_type=F32)
    gate += jnp.dot(mid[1], weights(0, 1), preferred_element_type=F32)
    lift = jnp.dot(mid[0], weights(1, 0), preferred_element_type=F32)
    lift += jnp.dot(mid[1], weights(1, 1), preferred_element_type=F32)
    act = (gate / (1.0 + jnp.exp(-gate)) * lift).astype(BF16)
    flat = [lax.dot_general(act, weights(2, h), NT, preferred_element_type=F32) for h in range(2)]
    for d in range(places):
        out[d] = jnp.concatenate([f[d * mine : (d + 1) * mine] for f in flat], axis=0).astype(BF16)


def finish_kernel(got, own_mid, gains, out):
    total = got[0].astype(F32)
    for i in range(1, got.shape[0]):
        total += got[i].astype(F32)
    mine = own_mid.shape[0]
    total = jnp.concatenate([total[:mine], total[mine:]], axis=1)
    model = total.shape[1]
    power = jnp.sum(total * total, axis=1, keepdims=True) / model
    gain = jnp.concatenate([gains[z, 1:2] for z in range(NZ)], axis=1)
    hidden = (own_mid[...] + total * lax.rsqrt(power + EPS) * gain).astype(BF16)
    feats = out.shape[2]
    for r in range(model // feats):
        part = hidden[:, r * feats : (r + 1) * feats]
        for x in range(NX):
            out[r * NX + x] = part


def turn_kernel(got, out):
    rows = jnp.concatenate([got[i].astype(F32) for i in range(got.shape[0])], axis=0)
    out[...] = rows.T.astype(BF16)


def ring(shift, size):
    return [(i, (i + shift) % size) for i in range(size)]


def body(hidden_in, lengths, w_qkv, qk_gain, cache_keys, cache_values, w_out, norm_gain,
         w_gate_up, w_down):
    rows = lengths.shape[0]
    width = w_qkv.shape[2]
    heads = width // HEAD_DIM
    feats = hidden_in.shape[1]
    model = width * NX
    wide = rows * heads
    blocks = cache_keys.shape[0] // BLOCK

    flipped = hidden_in.T
    mate_rows = lax.ppermute(flipped, "c", ring(1, NC))
    mate_w = lax.ppermute(w_qkv, "c", ring(1, NC))
    half = HEAD_DIM // 2
    freqs = jnp.power(THETA, -(jnp.arange(half, dtype=F32) * 2.0 / HEAD_DIM))
    angles = lengths.astype(F32)[:, None] * freqs[None, :]
    cosine = jnp.cos(angles)
    sine = jnp.sin(angles)
    tables = jnp.stack(
        [jnp.concatenate([cosine, cosine], axis=1), jnp.concatenate([-sine, sine], axis=1)]
    )
    ends = jnp.cumsum(lengths)
    bounds = jnp.tile(jnp.stack([ends - lengths, ends], axis=1), (heads, 1))
    gain_table = jnp.concatenate([qk_gain, jnp.zeros((6, width), F32)], axis=0)
    places = NZ * NY
    half = HEAD_DIM // 2
    freqs = jnp.power(THETA, -(jnp.arange(half, dtype=F32) * 2.0 / HEAD_DIM))
    spots = jnp.pad(lengths.astype(F32), (0, 128 - rows))[None, :]
    angles = freqs[:, None] * spots
    trig = jnp.concatenate([jnp.cos(angles), jnp.sin(angles)], axis=0)
    spots = jnp.broadcast_to(spots, (8, 128))
    lanes = 128
    head_lanes = 3 * width + lanes
    tile_lanes = 3 * feats // rows * lanes
    out_lanes = feats // rows * width + lanes
    message = call(
        project_kernel,
        shape((places, rows, head_lanes + tile_lanes + out_lanes), BF16),
        [ANY] * 10,
        VMEM,
        [
            pltpu.VMEM((2, feats, flipped.shape[1]), BF16),
            pltpu.VMEM((2,) + w_qkv.shape, BF16),
            pltpu.VMEM((flipped.shape[1], 2 * feats), F32),
            pltpu.VMEM(w_gate_up.shape, BF16),
            pltpu.VMEM(w_down.shape, BF16),
            pltpu.VMEM(w_out.shape, BF16),
            pltpu.VMEM(norm_gain.shape, F32),
            pltpu.SemaphoreType.DMA((8,)),
        ],
        (1 << 27, 2 << 20),
        "project",
        8,
    )(hbm(flipped), mate_rows, hbm(w_qkv), mate_w, hbm(w_gate_up), hbm(w_down), hbm(w_out), hbm(norm_gain), trig, spots)
    got = lax.all_to_all(message, Z + ("y",), 0, 0, tiled=True)

    mate = lax.ppermute(got, "c", ring(1, NC))
    qk, value_new, squares, rest, ffn_own = call(
        collect_kernel,
        (
            shape((3, rows, width), F32),
            shape((rows, width), BF16),
            shape((NX, rows, 128), F32),
            shape((rows // NX, model), F32),
            shape((places, rows, tile_lanes), BF16),
        ),
        [ANY],
        (VMEM,) * 4 + (ANY,),
        [
            pltpu.VMEM((places, rows, head_lanes), BF16),
            pltpu.VMEM((rows, model), F32),
            pltpu.SemaphoreType.DMA((2,)),
        ],
        (1 << 20, 4 << 20),
        "collect",
        8,
    )(got)
    ffn_mate = lax.ppermute(ffn_own, "c", ring(1, NC))
    near = lax.ppermute(ffn_own, "zl", ring(1, 2))
    squares = lax.all_to_all(squares, "x", 0, 0, tiled=True)
    key_new, attended = call(
        attend_kernel,
        (shape((rows, width), BF16), shape((rows, width), BF16)),
        [VMEM] * 7,
        (VMEM,) * 2,
        [pltpu.VMEM((blocks, wide, BLOCK), F32)],
        (1 << 29, 8 << 20),
        "attend",
        16,
    )(squares, qk, trig, spots, qk_gain, cache_keys, cache_values)
    partial, gains = call(
        out_kernel,
        (shape((NX, rows // NX, model), F32), shape((NZ, 8, width), F32)),
        [VMEM] + [ANY] * 3,
        (VMEM,) * 2,
        [
            pltpu.VMEM((NC, places, rows, out_lanes), BF16),
            pltpu.SemaphoreType.DMA((2,)),
        ],
        (1 << 26, 2 << 20),
        "project_out",
        8,
    )(attended, got, mate, ffn_mate)

    summed = lax.all_to_all(partial, "x", 0, 0, tiled=True)
    mine = rows // NX
    group = ("zh", "y", "x")
    members = NZ * NY * NX // 2
    own_mid, message = call(
        fan_kernel,
        (shape((mine, model), F32), shape((members, 2 * mine, model // 2), BF16)),
        [VMEM] * 3,
        (VMEM, VMEM),
        (),
        (1 << 16, 1 << 19),
        "fan",
    )(summed, rest, gains)
    near = call(
        hold_kernel,
        shape(near.shape, BF16),
        [ANY] * 2,
        ANY,
        [pltpu.SemaphoreType.DMA],
        (0, 1 << 20),
        "hold",
        1,
    )(near, own_mid)
    near_mate = lax.ppermute(near, "c", ring(1, NC))
    got = lax.all_to_all(message, group, 0, 0, tiled=True)
    partial = call(
        ffn_kernel,
        shape((members, 2 * mine, model // 2), BF16),
        [VMEM] + [ANY] * 4,
        VMEM,
        [
            pltpu.VMEM((2, NC) + ffn_own.shape, BF16),
            pltpu.SemaphoreType.DMA((4,)),
        ],
        (1 << 28, 4 << 20),
        "feed_forward",
        16,
    )(got, ffn_own, ffn_mate, near, near_mate)
    got = lax.all_to_all(partial, group, 0, 0, tiled=True)
    message = call(
        finish_kernel,
        shape((NZ * NY * NC * NX, mine, feats), BF16),
        [VMEM] * 3,
        VMEM,
        (),
        (1 << 18, 1 << 19),
        "finish",
    )(got, own_mid, gains)
    hidden = lax.all_to_all(message, Z + ("y", "c", "x"), 0, 0, tiled=True)
    hidden = call(
        turn_kernel,
        shape((feats, hidden.shape[0] * mine), BF16),
        [VMEM],
        VMEM,
        (),
        (1 << 16, 1 << 18),
        "turn",
    )(hidden)
    return hidden.T, key_new, value_new


def solution(mesh):
    fine = Mesh(mesh.devices.reshape(2, 2, NY, NC, NX), Z + ("y", "c", "x"))
    req = Z + ("y", "c")
    return jax.shard_map(
        body,
        mesh=fine,
        in_specs=(
            P(None, req),
            P(req),
            P(None, req, "x"),
            P(None, "x"),
            P(req, "x"),
            P(req, "x"),
            P(req, "x"),
            P(None, req),
            P(None, req, "x"),
            P(req, "x"),
        ),
        out_specs=(P(None, req), P(req, "x"), P(req, "x")),
        check_vma=False,
    )
```

```python
import jax
import jax.numpy as jnp
from jax import lax
from jax.experimental import pallas as pl
from jax.experimental.pallas import tpu as pltpu
from jax.sharding import Mesh, PartitionSpec as P

HEAD_DIM = 128
EPS = 1e-06
THETA = 500000.0
NT = (((1,), (1,)), ((), ()))
BLOCK = 512
F32 = jnp.float32
BF16 = jnp.bfloat16
NZ, NY, NC, NX = 4, 4, 2, 4
Z = ("zh", "zl")
VMEM = pl.BlockSpec(memory_space=pltpu.VMEM)
HBM = pl.BlockSpec(memory_space=pltpu.HBM)
ANY = pl.BlockSpec(memory_space=pl.ANY)
SMEM = pl.BlockSpec(memory_space=pltpu.SMEM)


def call(kernel, out_shape, in_specs, out_specs, scratch=(), cost=(1 << 20, 1 << 20), name=None, limit=4):
    return pl.pallas_call(
        kernel,
        out_shape=out_shape,
        in_specs=in_specs,
        out_specs=out_specs,
        scratch_shapes=list(scratch),
        compiler_params=pltpu.CompilerParams(vmem_limit_bytes=limit * 1024 * 1024),
        cost_estimate=pl.CostEstimate(flops=cost[0], bytes_accessed=cost[1], transcendentals=0),
        name=name,
    )


def hbm(array):
    return pltpu.with_memory_space_constraint(array, pltpu.HBM)


def shape(dims, dtype):
    return jax.ShapeDtypeStruct(dims, dtype)


def hold_kernel(piece, token, out, sem):
    copy = pltpu.make_async_copy(piece, out, sem)
    copy.start()
    copy.wait()


def project_kernel(h_own, h_mate, w_own, w_mate, gate_up, down, out_w, gains, trig, places, out, hbuf,
                   wbuf, rows_buf, gbuf, dbuf, obuf, nbuf, sem):
    core = lax.axis_index("c")
    pairs = (
        (h_own, hbuf.at[core]),
        (h_mate, hbuf.at[1 - core]),
        (w_own, wbuf.at[core]),
        (w_mate, wbuf.at[1 - core]),
        (gate_up, gbuf),
        (down, dbuf),
        (out_w, obuf),
        (gains, nbuf),
    )
    copies = [pltpu.make_async_copy(a, b, sem.at[i]) for i, (a, b) in enumerate(pairs)]
    for copy in copies:
        copy.start()
    copies[0].wait()
    copies[1].wait()
    rows_buf[...] = jnp.concatenate([hbuf[0].astype(F32).T, hbuf[1].astype(F32).T], axis=1)
    blocks, rows, _ = out.shape
    feats, width = w_own.shape[1:]
    lanes = 2 * feats
    chosen = jnp.concatenate(
        [
            rows_buf[pl.ds(pl.multiple_of((2 * b + core) * rows, rows), rows), :]
            for b in range(blocks)
        ],
        axis=0,
    ).astype(BF16)
    copies[2].wait()
    copies[3].wait()
    for g in range(3):
        weights = jnp.concatenate([wbuf[0, g], wbuf[1, g]], axis=0)
        part = jnp.dot(chosen, weights, preferred_element_type=F32).astype(BF16)
        out[:, :, g * width : (g + 1) * width] = part.reshape(blocks, rows, width)
    for copy in copies[4:]:
        copy.wait()
    at = 3 * width
    x = lax.axis_index("x")
    both = jnp.concatenate([nbuf[0:1, :], nbuf[1:2, :]], axis=1)
    high = both.astype(BF16).astype(F32)
    rest = jnp.zeros((rows - 6, lanes), F32)
    for b in range(blocks):
        low = pl.multiple_of((2 * b + core) * rows + x // 2 * 8, 8)
        pair = rows_buf[pl.ds(low, 8), :]
        own = jnp.where(lax.rem(x, 2) == 0, pair[:4], pair[4:])
        out[b, :, at : at + lanes] = jnp.concatenate([own, high, both - high, rest], axis=0).astype(BF16)
    at += lanes
    steps = feats // rows
    for part in range(3):
        for i in range(steps):
            low = slice(i * rows, (i + 1) * rows)
            for b in range(blocks):
                cols = slice(b * lanes, (b + 1) * lanes)
                out[b, :, at : at + lanes] = dbuf[low, cols] if part == 2 else gbuf[part, low, cols]
            at += lanes
    for b in range(blocks):
        for i in range(steps):
            out[b, :, at + i * width : at + (i + 1) * width] = obuf[i * rows : (i + 1) * rows]


def collect_kernel(got, qk, value, squares, rest, ffn, buf, sem):
    rows, width = value.shape
    at = buf.shape[2]
    first = pltpu.make_async_copy(got.at[:, :, pl.ds(0, at)], buf, sem.at[0])
    second = pltpu.make_async_copy(got.at[:, :, pl.ds(at, ffn.shape[2])], ffn, sem.at[1])
    first.start()
    second.start()
    first.wait()
    total = buf[0, :, : 3 * width].astype(F32)
    for i in range(1, buf.shape[0]):
        total += buf[i, :, : 3 * width].astype(F32)
    q, k = total[:, :width], total[:, width : 2 * width]
    qk[0] = q
    qk[1] = k
    new = total[:, 2 * width :].astype(BF16)
    value[...] = new
    qk[2] = new.astype(F32)
    lane = lax.broadcasted_iota(jnp.int32, squares.shape[1:], 1)
    both = jnp.where(
        lane < 64, jnp.sum(q * q, axis=1, keepdims=True), jnp.sum(k * k, axis=1, keepdims=True)
    )
    for i in range(NX):
        squares[i] = both
    lanes = at - 3 * width
    for i in range(buf.shape[0]):
        rest[:, i * lanes : (i + 1) * lanes] = buf[i, :, 3 * width :].astype(F32)[:4]
    second.wait()


def turn(values, cosine, sine):
    heads = values.shape[1] // HEAD_DIM
    parts = []
    for h in range(heads):
        v = values[:, h * HEAD_DIM : (h + 1) * HEAD_DIM]
        parts.append(v * cosine + pltpu.roll(v, HEAD_DIM // 2, 1) * sine)
    return jnp.concatenate(parts, axis=1)


def spread(values, heads):
    rows, width = values.shape
    wide = rows * heads
    row_head = lax.broadcasted_iota(jnp.int32, (wide, width), 0) // rows
    col_head = lax.broadcasted_iota(jnp.int32, (wide, width), 1) // HEAD_DIM
    return jnp.where(row_head == col_head, jnp.concatenate([values] * heads, axis=0), 0.0)


def attend_kernel(squares_in, qk, trig, places, gains, keys, values, key_out,
                  out, score):
    rows, width = out.shape
    heads = width // HEAD_DIM
    blocks = score.shape[0]
    model = width * NX
    used = jnp.sum(places[0:1, :])
    wide = heads * rows
    request = lax.rem(lax.broadcasted_iota(jnp.int32, (wide, 128), 0), rows)
    lane = lax.broadcasted_iota(jnp.int32, (wide, 128), 1)
    lengths = jnp.broadcast_to(places[0:1, :], (wide, 128))
    starts = jnp.sum(jnp.where(lane < request, lengths, 0.0), axis=1, keepdims=True)
    ends = jnp.sum(jnp.where(lane <= request, lengths, 0.0), axis=1, keepdims=True)
    starts = starts.astype(jnp.int32)
    ends = ends.astype(jnp.int32)
    angles = trig[...].T
    half = HEAD_DIM // 2
    cosine = jnp.concatenate([angles[:rows, :half], angles[:rows, :half]], axis=1)
    sine = jnp.concatenate([-angles[:rows, half:], angles[:rows, half:]], axis=1)
    squares = squares_in[0] + squares_in[1] + squares_in[2] + squares_in[3]
    q_factor = lax.rsqrt(squares[:, 0:1] / model + EPS)
    k_factor = lax.rsqrt(squares[:, 64:65] / model + EPS)
    query = turn(qk[0] * q_factor * gains[0:1, :], cosine, sine).astype(BF16)
    new_key = turn(qk[1] * k_factor * gains[1:2, :], cosine, sine).astype(BF16)
    key_out[...] = new_key
    scale = HEAD_DIM ** (-0.5)
    q_all = spread(query.astype(F32), heads)
    q_block = q_all.astype(BF16)
    k_all = jnp.concatenate([new_key.astype(F32)] * heads, axis=0)
    v_all = jnp.concatenate([qk[2]] * heads, axis=0)
    own = jnp.sum(q_all * k_all, axis=1, keepdims=True) * scale
    def raw(i):
        rows_here = keys[pl.ds(i * BLOCK, BLOCK), :]
        s = lax.dot_general(q_block, rows_here, NT, preferred_element_type=F32) * scale
        place = lax.broadcasted_iota(jnp.int32, s.shape, 1) + i * BLOCK
        return jnp.where((place >= starts) & (place < ends), s, -jnp.inf)

    def finish(size):
        highest = own
        for i in range(size):
            s = raw(i)
            score[i] = s
            highest = jnp.maximum(highest, jnp.max(s, axis=1, keepdims=True))
        own_weight = jnp.exp(own - highest).astype(BF16).astype(F32)
        total = own_weight
        acc = own_weight * v_all
        for i in range(size):
            w = jnp.exp(score[i] - highest).astype(BF16)
            total += jnp.sum(w.astype(F32), axis=1, keepdims=True)
            acc += jnp.dot(w, values[pl.ds(i * BLOCK, BLOCK), :], preferred_element_type=F32)
        result = acc / total
        out[...] = jnp.concatenate(
            [
                result[h * rows : (h + 1) * rows, h * HEAD_DIM : (h + 1) * HEAD_DIM]
                for h in range(heads)
            ],
            axis=1,
        ).astype(BF16)

    short = 2

    @pl.when(used <= short * BLOCK)
    def _():
        finish(short)

    @pl.when(used > short * BLOCK)
    def _():
        finish(blocks)


def out_kernel(attended, own, mate, after, partial, gain_out, wbuf, gbuf, sem):
    rows, width = attended.shape
    core = lax.axis_index("c")
    last = pl.ds(own.shape[2] - wbuf.shape[3], wbuf.shape[3])
    head = pl.ds(3 * width, gbuf.shape[3])
    copies = []
    for i, (got, place) in enumerate(((own, core), (mate, 1 - core))):
        copies.append(pltpu.make_async_copy(got.at[:, :, last], wbuf.at[place], sem.at[i, 0]))
        copies.append(pltpu.make_async_copy(got.at[:, :, head], gbuf.at[place], sem.at[i, 1]))
    for copy in copies:
        copy.start()
    for copy in copies:
        copy.wait()
    steps = wbuf.shape[3] // width
    mine = rows // NX
    for b in range(NZ):
        weights = jnp.concatenate(
            [
                wbuf[c, b * NY + y, :, i * width : (i + 1) * width]
                for y in range(NY)
                for c in range(NC)
                for i in range(steps)
            ],
            axis=0,
        )
        a = lax.dot_general(attended[...], weights, NT, preferred_element_type=F32)
        for x in range(NX):
            partial[x, :, b * width : (b + 1) * width] = a[x * mine : (x + 1) * mine]
        for y in range(NY):
            two = [gbuf[c, b * NY + y].astype(F32) for c in range(NC)]
            two = [t[4:5] + t[5:6] for t in two]
            for g in range(2):
                gain_out[b, g : g + 1, y * 128 : (y + 1) * 128] = jnp.concatenate(
                    [t[:, g * 64 : (g + 1) * 64] for t in two], axis=1
                )


def fan_kernel(got, rest, gains, own_mid, out):
    total = got[0] + got[1] + got[2] + got[3]
    model = total.shape[1]
    power = jnp.sum(total * total, axis=1, keepdims=True) / model
    gain = jnp.concatenate([gains[z, 0:1] for z in range(NZ)], axis=1)
    mid = (rest[...] + total * lax.rsqrt(power + EPS) * gain).astype(BF16)
    mid32 = mid.astype(F32)
    own_mid[...] = mid32
    message = jnp.concatenate([mid32[:, : model // 2], mid32[:, model // 2 :]], axis=0).astype(BF16)
    for i in range(out.shape[0]):
        out[i] = message


def ffn_kernel(got, own, own_mate, near, near_mate, out, wbuf, sem):
    core = lax.axis_index("c")
    copies = [
        pltpu.make_async_copy(own, wbuf.at[0, core], sem.at[0]),
        pltpu.make_async_copy(own_mate, wbuf.at[0, 1 - core], sem.at[1]),
        pltpu.make_async_copy(near, wbuf.at[1, core], sem.at[2]),
        pltpu.make_async_copy(near_mate, wbuf.at[1, 1 - core], sem.at[3]),
    ]
    for copy in copies:
        copy.start()
    places, lines, span = got.shape
    mine = lines // 2
    whole = [got[d].astype(F32) for d in range(places)]
    mid = [
        jnp.concatenate([w[half * mine : (half + 1) * mine] for w in whole], axis=0).astype(BF16)
        for half in range(2)
    ]
    blocks = wbuf.shape[2]
    lanes = 128
    steps = wbuf.shape[4] // (3 * lanes)
    for copy in copies:
        copy.wait()

    def weights(part, half):
        rows = range(half * blocks // 2, (half + 1) * blocks // 2)
        return jnp.concatenate(
            [
                jnp.concatenate(
                    [
                        wbuf[p, c, b, :, (part * steps + i) * lanes : (part * steps + i + 1) * lanes]
                        for b in rows
                        for c in range(NC)
                        for i in range(steps)
                    ],
                    axis=0,
                )
                for p in range(2)
            ],
            axis=1,
        )

    gate = jnp.dot(mid[0], weights(0, 0), preferred_element_type=F32)
    gate += jnp.dot(mid[1], weights(0, 1), preferred_element_type=F32)
    lift = jnp.dot(mid[0], weights(1, 0), preferred_element_type=F32)
    lift += jnp.dot(mid[1], weights(1, 1), preferred_element_type=F32)
    act = (gate / (1.0 + jnp.exp(-gate)) * lift).astype(BF16)
    flat = [lax.dot_general(act, weights(2, h), NT, preferred_element_type=F32) for h in range(2)]
    for d in range(places):
        out[d] = jnp.concatenate([f[d * mine : (d + 1) * mine] for f in flat], axis=0).astype(BF16)


def finish_kernel(got, own_mid, gains, out):
    total = got[0].astype(F32)
    for i in range(1, got.shape[0]):
        total += got[i].astype(F32)
    mine = own_mid.shape[0]
    total = jnp.concatenate([total[:mine], total[mine:]], axis=1)
    model = total.shape[1]
    power = jnp.sum(total * total, axis=1, keepdims=True) / model
    gain = jnp.concatenate([gains[z, 1:2] for z in range(NZ)], axis=1)
    hidden = (own_mid[...] + total * lax.rsqrt(power + EPS) * gain).astype(BF16)
    feats = out.shape[2]
    for r in range(model // feats):
        part = hidden[:, r * feats : (r + 1) * feats]
        for x in range(NX):
            out[r * NX + x] = part


def turn_kernel(got, out):
    rows = jnp.concatenate([got[i].astype(F32) for i in range(got.shape[0])], axis=0)
    out[...] = rows.T.astype(BF16)


def ring(shift, size):
    return [(i, (i + shift) % size) for i in range(size)]


def body(hidden_in, lengths, w_qkv, qk_gain, cache_keys, cache_values, w_out, norm_gain,
         w_gate_up, w_down):
    rows = lengths.shape[0]
    width = w_qkv.shape[2]
    heads = width // HEAD_DIM
    feats = hidden_in.shape[1]
    model = width * NX
    wide = rows * heads
    blocks = cache_keys.shape[0] // BLOCK

    flipped = hidden_in.T
    mate_rows = lax.ppermute(flipped, "c", ring(1, NC))
    mate_w = lax.ppermute(w_qkv, "c", ring(1, NC))
    half = HEAD_DIM // 2
    freqs = jnp.power(THETA, -(jnp.arange(half, dtype=F32) * 2.0 / HEAD_DIM))
    angles = lengths.astype(F32)[:, None] * freqs[None, :]
    cosine = jnp.cos(angles)
    sine = jnp.sin(angles)
    tables = jnp.stack(
        [jnp.concatenate([cosine, cosine], axis=1), jnp.concatenate([-sine, sine], axis=1)]
    )
    ends = jnp.cumsum(lengths)
    bounds = jnp.tile(jnp.stack([ends - lengths, ends], axis=1), (heads, 1))
    gain_table = jnp.concatenate([qk_gain, jnp.zeros((6, width), F32)], axis=0)
    places = NZ * NY
    half = HEAD_DIM // 2
    freqs = jnp.power(THETA, -(jnp.arange(half, dtype=F32) * 2.0 / HEAD_DIM))
    spots = jnp.pad(lengths.astype(F32), (0, 128 - rows))[None, :]
    angles = freqs[:, None] * spots
    trig = jnp.concatenate([jnp.cos(angles), jnp.sin(angles)], axis=0)
    spots = jnp.broadcast_to(spots, (8, 128))
    lanes = 128
    head_lanes = 3 * width + lanes
    tile_lanes = 3 * feats // rows * lanes
    out_lanes = feats // rows * width
    message = call(
        project_kernel,
        shape((places, rows, head_lanes + tile_lanes + out_lanes), BF16),
        [ANY] * 10,
        VMEM,
        [
            pltpu.VMEM((2, feats, flipped.shape[1]), BF16),
            pltpu.VMEM((2,) + w_qkv.shape, BF16),
            pltpu.VMEM((flipped.shape[1], 2 * feats), F32),
            pltpu.VMEM(w_gate_up.shape, BF16),
            pltpu.VMEM(w_down.shape, BF16),
            pltpu.VMEM(w_out.shape, BF16),
            pltpu.VMEM(norm_gain.shape, F32),
            pltpu.SemaphoreType.DMA((8,)),
        ],
        (1 << 27, 2 << 20),
        "project",
        8,
    )(hbm(flipped), mate_rows, hbm(w_qkv), mate_w, hbm(w_gate_up), hbm(w_down), hbm(w_out), hbm(norm_gain), trig, spots)
    got = lax.all_to_all(message, Z + ("y",), 0, 0, tiled=True)

    mate = lax.ppermute(got, "c", ring(1, NC))
    qk, value_new, squares, rest, ffn_own = call(
        collect_kernel,
        (
            shape((3, rows, width), F32),
            shape((rows, width), BF16),
            shape((NX, rows, 128), F32),
            shape((rows // NX, model), F32),
            shape((places, rows, tile_lanes), BF16),
        ),
        [ANY],
        (VMEM,) * 4 + (ANY,),
        [
            pltpu.VMEM((places, rows, head_lanes), BF16),
            pltpu.SemaphoreType.DMA((2,)),
        ],
        (1 << 20, 4 << 20),
        "collect",
        8,
    )(got)
    ffn_mate = lax.ppermute(ffn_own, "c", ring(1, NC))
    near = lax.ppermute(ffn_own, "zl", ring(1, 2))
    squares = lax.all_to_all(squares, "x", 0, 0, tiled=True)
    key_new, attended = call(
        attend_kernel,
        (shape((rows, width), BF16), shape((rows, width), BF16)),
        [VMEM] * 7,
        (VMEM,) * 2,
        [pltpu.VMEM((blocks, wide, BLOCK), F32)],
        (1 << 29, 8 << 20),
        "attend",
        16,
    )(squares, qk, trig, spots, qk_gain, cache_keys, cache_values)
    partial, gains = call(
        out_kernel,
        (shape((NX, rows // NX, model), F32), shape((NZ, 8, width), F32)),
        [VMEM] + [ANY] * 3,
        (VMEM,) * 2,
        [
            pltpu.VMEM((NC, places, rows, out_lanes), BF16),
            pltpu.VMEM((NC, places, rows, lanes), BF16),
            pltpu.SemaphoreType.DMA((2, 2)),
        ],
        (1 << 26, 2 << 20),
        "project_out",
        8,
    )(attended, got, mate, ffn_mate)

    summed = lax.all_to_all(partial, "x", 0, 0, tiled=True)
    mine = rows // NX
    group = ("zh", "y", "x")
    members = NZ * NY * NX // 2
    own_mid, message = call(
        fan_kernel,
        (shape((mine, model), F32), shape((members, 2 * mine, model // 2), BF16)),
        [VMEM] * 3,
        (VMEM, VMEM),
        (),
        (1 << 16, 1 << 19),
        "fan",
    )(summed, rest, gains)
    near = call(
        hold_kernel,
        shape(near.shape, BF16),
        [ANY] * 2,
        ANY,
        [pltpu.SemaphoreType.DMA],
        (0, 1 << 20),
        "hold",
        1,
    )(near, own_mid)
    near_mate = lax.ppermute(near, "c", ring(1, NC))
    got = lax.all_to_all(message, group, 0, 0, tiled=True)
    partial = call(
        ffn_kernel,
        shape((members, 2 * mine, model // 2), BF16),
        [VMEM] + [ANY] * 4,
        VMEM,
        [
            pltpu.VMEM((2, NC) + ffn_own.shape, BF16),
            pltpu.SemaphoreType.DMA((4,)),
        ],
        (1 << 28, 4 << 20),
        "feed_forward",
        16,
    )(got, ffn_own, ffn_mate, near, near_mate)
    got = lax.all_to_all(partial, group, 0, 0, tiled=True)
    message = call(
        finish_kernel,
        shape((NZ * NY * NC * NX, mine, feats), BF16),
        [VMEM] * 3,
        VMEM,
        (),
        (1 << 18, 1 << 19),
        "finish",
    )(got, own_mid, gains)
    hidden = lax.all_to_all(message, Z + ("y", "c", "x"), 0, 0, tiled=True)
    hidden = call(
        turn_kernel,
        shape((feats, hidden.shape[0] * mine), BF16),
        [VMEM],
        VMEM,
        (),
        (1 << 16, 1 << 18),
        "turn",
    )(hidden)
    return hidden.T, key_new, value_new


def solution(mesh):
    fine = Mesh(mesh.devices.reshape(2, 2, NY, NC, NX), Z + ("y", "c", "x"))
    req = Z + ("y", "c")
    return jax.shard_map(
        body,
        mesh=fine,
        in_specs=(
            P(None, req),
            P(req),
            P(None, req, "x"),
            P(None, "x"),
            P(req, "x"),
            P(req, "x"),
            P(req, "x"),
            P(None, req),
            P(None, req, "x"),
            P(req, "x"),
        ),
        out_specs=(P(None, req), P(req, "x"), P(req, "x")),
        check_vma=False,
    )
```

```python
import jax
import jax.numpy as jnp
from jax import lax
from jax.experimental import pallas as pl
from jax.experimental.pallas import tpu as pltpu
from jax.sharding import Mesh, PartitionSpec as P

HEAD_DIM = 128
EPS = 1e-06
THETA = 500000.0
NT = (((1,), (1,)), ((), ()))
BLOCK = 512
F32 = jnp.float32
BF16 = jnp.bfloat16
NZ, NY, NC, NX = 4, 4, 2, 4
Z = ("zh", "zl")
VMEM = pl.BlockSpec(memory_space=pltpu.VMEM)
HBM = pl.BlockSpec(memory_space=pltpu.HBM)
ANY = pl.BlockSpec(memory_space=pl.ANY)
SMEM = pl.BlockSpec(memory_space=pltpu.SMEM)


def call(kernel, out_shape, in_specs, out_specs, scratch=(), cost=(1 << 20, 1 << 20), name=None, limit=4):
    return pl.pallas_call(
        kernel,
        out_shape=out_shape,
        in_specs=in_specs,
        out_specs=out_specs,
        scratch_shapes=list(scratch),
        compiler_params=pltpu.CompilerParams(vmem_limit_bytes=limit * 1024 * 1024),
        cost_estimate=pl.CostEstimate(flops=cost[0], bytes_accessed=cost[1], transcendentals=0),
        name=name,
    )


def hbm(array):
    return pltpu.with_memory_space_constraint(array, pltpu.HBM)


def shape(dims, dtype):
    return jax.ShapeDtypeStruct(dims, dtype)


def hold_kernel(piece, token, out, sem):
    copy = pltpu.make_async_copy(piece, out, sem)
    copy.start()
    copy.wait()


def project_kernel(h_own, h_mate, w_own, w_mate, gate_up, down, out_w, gains, trig, places, out, hbuf,
                   wbuf, rows_buf, gbuf, dbuf, obuf, nbuf, sem):
    core = lax.axis_index("c")
    pairs = (
        (h_own, hbuf.at[core]),
        (h_mate, hbuf.at[1 - core]),
        (w_own, wbuf.at[core]),
        (w_mate, wbuf.at[1 - core]),
        (gate_up, gbuf),
        (down, dbuf),
        (out_w, obuf),
        (gains, nbuf),
    )
    copies = [pltpu.make_async_copy(a, b, sem.at[i]) for i, (a, b) in enumerate(pairs)]
    for copy in copies:
        copy.start()
    copies[0].wait()
    copies[1].wait()
    rows_buf[...] = jnp.concatenate([hbuf[0].astype(F32).T, hbuf[1].astype(F32).T], axis=1)
    blocks, rows, _ = out.shape
    feats, width = w_own.shape[1:]
    lanes = 2 * feats
    chosen = jnp.concatenate(
        [
            rows_buf[pl.ds(pl.multiple_of((2 * b + core) * rows, rows), rows), :]
            for b in range(blocks)
        ],
        axis=0,
    ).astype(BF16)
    copies[2].wait()
    copies[3].wait()
    for g in range(3):
        weights = jnp.concatenate([wbuf[0, g], wbuf[1, g]], axis=0)
        part = jnp.dot(chosen, weights, preferred_element_type=F32).astype(BF16)
        out[:, :, g * width : (g + 1) * width] = part.reshape(blocks, rows, width)
    for copy in copies[4:]:
        copy.wait()
    at = 3 * width
    x = lax.axis_index("x")
    both = jnp.concatenate([nbuf[0:1, :], nbuf[1:2, :]], axis=1)
    high = both.astype(BF16).astype(F32)
    rest = jnp.zeros((rows - 6, lanes), F32)
    for b in range(blocks):
        low = pl.multiple_of((2 * b + core) * rows + x // 2 * 8, 8)
        pair = rows_buf[pl.ds(low, 8), :]
        own = jnp.where(lax.rem(x, 2) == 0, pair[:4], pair[4:])
        out[b, :, at : at + lanes] = jnp.concatenate([own, high, both - high, rest], axis=0).astype(BF16)
    at += lanes
    steps = feats // rows
    for part in range(3):
        for i in range(steps):
            low = slice(i * rows, (i + 1) * rows)
            for b in range(blocks):
                cols = slice(b * lanes, (b + 1) * lanes)
                out[b, :, at : at + lanes] = dbuf[low, cols] if part == 2 else gbuf[part, low, cols]
            at += lanes
    for b in range(blocks):
        for i in range(steps):
            out[b, :, at + i * width : at + (i + 1) * width] = obuf[i * rows : (i + 1) * rows]


def collect_kernel(got, qk, value, squares, rest, ffn, sem):
    rows, width = value.shape
    lanes = 128
    at = 3 * width + lanes
    copy = pltpu.make_async_copy(got.at[:, :, pl.ds(at, ffn.shape[2])], ffn, sem)
    copy.start()
    blocks = got.shape[0]
    total = got[0, :, : 3 * width].astype(F32)
    for i in range(1, blocks):
        total += got[i, :, : 3 * width].astype(F32)
    q, k = total[:, :width], total[:, width : 2 * width]
    qk[0] = q
    qk[1] = k
    new = total[:, 2 * width :].astype(BF16)
    value[...] = new
    qk[2] = new.astype(F32)
    lane = lax.broadcasted_iota(jnp.int32, squares.shape[1:], 1)
    both = jnp.where(
        lane < 64, jnp.sum(q * q, axis=1, keepdims=True), jnp.sum(k * k, axis=1, keepdims=True)
    )
    for i in range(NX):
        squares[i] = both
    for i in range(blocks):
        rest[:, i * lanes : (i + 1) * lanes] = got[i, :, 3 * width : at].astype(F32)[:4]
    copy.wait()


def turn(values, cosine, sine):
    heads = values.shape[1] // HEAD_DIM
    parts = []
    for h in range(heads):
        v = values[:, h * HEAD_DIM : (h + 1) * HEAD_DIM]
        parts.append(v * cosine + pltpu.roll(v, HEAD_DIM // 2, 1) * sine)
    return jnp.concatenate(parts, axis=1)


def spread(values, heads):
    rows, width = values.shape
    wide = rows * heads
    row_head = lax.broadcasted_iota(jnp.int32, (wide, width), 0) // rows
    col_head = lax.broadcasted_iota(jnp.int32, (wide, width), 1) // HEAD_DIM
    return jnp.where(row_head == col_head, jnp.concatenate([values] * heads, axis=0), 0.0)


def attend_kernel(squares_in, qk, trig, places, gains, keys, values, key_out,
                  out, score):
    rows, width = out.shape
    heads = width // HEAD_DIM
    blocks = score.shape[0]
    model = width * NX
    used = jnp.sum(places[0:1, :])
    wide = heads * rows
    request = lax.rem(lax.broadcasted_iota(jnp.int32, (wide, 128), 0), rows)
    lane = lax.broadcasted_iota(jnp.int32, (wide, 128), 1)
    lengths = jnp.broadcast_to(places[0:1, :], (wide, 128))
    starts = jnp.sum(jnp.where(lane < request, lengths, 0.0), axis=1, keepdims=True)
    ends = jnp.sum(jnp.where(lane <= request, lengths, 0.0), axis=1, keepdims=True)
    starts = starts.astype(jnp.int32)
    ends = ends.astype(jnp.int32)
    angles = trig[...].T
    half = HEAD_DIM // 2
    cosine = jnp.concatenate([angles[:rows, :half], angles[:rows, :half]], axis=1)
    sine = jnp.concatenate([-angles[:rows, half:], angles[:rows, half:]], axis=1)
    squares = squares_in[0] + squares_in[1] + squares_in[2] + squares_in[3]
    q_factor = lax.rsqrt(squares[:, 0:1] / model + EPS)
    k_factor = lax.rsqrt(squares[:, 64:65] / model + EPS)
    query = turn(qk[0] * q_factor * gains[0:1, :], cosine, sine).astype(BF16)
    new_key = turn(qk[1] * k_factor * gains[1:2, :], cosine, sine).astype(BF16)
    key_out[...] = new_key
    scale = HEAD_DIM ** (-0.5)
    q_all = spread(query.astype(F32), heads)
    q_block = q_all.astype(BF16)
    k_all = jnp.concatenate([new_key.astype(F32)] * heads, axis=0)
    v_all = jnp.concatenate([qk[2]] * heads, axis=0)
    own = jnp.sum(q_all * k_all, axis=1, keepdims=True) * scale
    def raw(i):
        rows_here = keys[pl.ds(i * BLOCK, BLOCK), :]
        s = lax.dot_general(q_block, rows_here, NT, preferred_element_type=F32) * scale
        place = lax.broadcasted_iota(jnp.int32, s.shape, 1) + i * BLOCK
        return jnp.where((place >= starts) & (place < ends), s, -jnp.inf)

    def finish(size):
        highest = own
        for i in range(size):
            s = raw(i)
            score[i] = s
            highest = jnp.maximum(highest, jnp.max(s, axis=1, keepdims=True))
        own_weight = jnp.exp(own - highest).astype(BF16).astype(F32)
        total = own_weight
        acc = own_weight * v_all
        for i in range(size):
            w = jnp.exp(score[i] - highest).astype(BF16)
            total += jnp.sum(w.astype(F32), axis=1, keepdims=True)
            acc += jnp.dot(w, values[pl.ds(i * BLOCK, BLOCK), :], preferred_element_type=F32)
        result = acc / total
        out[...] = jnp.concatenate(
            [
                result[h * rows : (h + 1) * rows, h * HEAD_DIM : (h + 1) * HEAD_DIM]
                for h in range(heads)
            ],
            axis=1,
        ).astype(BF16)

    short = 2

    @pl.when(used <= short * BLOCK)
    def _():
        finish(short)

    @pl.when(used > short * BLOCK)
    def _():
        finish(blocks)


def by_core(work, own, mate):
    core = lax.axis_index("c")

    @pl.when(core == 0)
    def _():
        work(own, mate)

    @pl.when(core == 1)
    def _():
        work(mate, own)


def out_kernel(attended, own, mate, after, partial, gain_out):
    rows, width = attended.shape
    head = 3 * width
    lanes = 128
    steps = 4
    last = own.shape[2] - steps * width
    mine = rows // NX

    def work(*cores):
        for b in range(NZ):
            weights = jnp.concatenate(
                [
                    cores[c][b * NY + y, :, last + i * width : last + (i + 1) * width]
                    for y in range(NY)
                    for c in range(NC)
                    for i in range(steps)
                ],
                axis=0,
            )
            a = lax.dot_general(attended[...], weights, NT, preferred_element_type=F32)
            for x in range(NX):
                partial[x, :, b * width : (b + 1) * width] = a[x * mine : (x + 1) * mine]
            for y in range(NY):
                two = [cores[c][b * NY + y, :, head : head + lanes].astype(F32) for c in range(NC)]
                two = [t[4:5] + t[5:6] for t in two]
                for g in range(2):
                    gain_out[b, g : g + 1, y * lanes : (y + 1) * lanes] = jnp.concatenate(
                        [t[:, g * 64 : (g + 1) * 64] for t in two], axis=1
                    )

    by_core(work, own, mate)


def fan_kernel(got, rest, gains, own_mid, out):
    total = got[0] + got[1] + got[2] + got[3]
    model = total.shape[1]
    power = jnp.sum(total * total, axis=1, keepdims=True) / model
    gain = jnp.concatenate([gains[z, 0:1] for z in range(NZ)], axis=1)
    mid = (rest[...] + total * lax.rsqrt(power + EPS) * gain).astype(BF16)
    mid32 = mid.astype(F32)
    own_mid[...] = mid32
    message = jnp.concatenate([mid32[:, : model // 2], mid32[:, model // 2 :]], axis=0).astype(BF16)
    for i in range(out.shape[0]):
        out[i] = message


def ffn_kernel(got, own, own_mate, near, near_mate, out):
    places, lines, span = got.shape
    mine = lines // 2
    whole = [got[d].astype(F32) for d in range(places)]
    mid = [
        jnp.concatenate([w[half * mine : (half + 1) * mine] for w in whole], axis=0).astype(BF16)
        for half in range(2)
    ]
    blocks = own.shape[0]
    lanes = 128
    steps = own.shape[2] // (3 * lanes)

    def work(*cores):
        def weights(part, half):
            rows = range(half * blocks // 2, (half + 1) * blocks // 2)
            return jnp.concatenate(
                [
                    jnp.concatenate(
                        [
                            cores[c][p][b, :, (part * steps + i) * lanes : (part * steps + i + 1) * lanes]
                            for b in rows
                            for c in range(NC)
                            for i in range(steps)
                        ],
                        axis=0,
                    )
                    for p in range(2)
                ],
                axis=1,
            )

        gate = jnp.dot(mid[0], weights(0, 0), preferred_element_type=F32)
        gate += jnp.dot(mid[1], weights(0, 1), preferred_element_type=F32)
        lift = jnp.dot(mid[0], weights(1, 0), preferred_element_type=F32)
        lift += jnp.dot(mid[1], weights(1, 1), preferred_element_type=F32)
        act = (gate / (1.0 + jnp.exp(-gate)) * lift).astype(BF16)
        flat = [lax.dot_general(act, weights(2, h), NT, preferred_element_type=F32) for h in range(2)]
        for d in range(places):
            out[d] = jnp.concatenate([f[d * mine : (d + 1) * mine] for f in flat], axis=0).astype(BF16)

    by_core(work, (own, near), (own_mate, near_mate))


def finish_kernel(got, own_mid, gains, out):
    total = got[0].astype(F32)
    for i in range(1, got.shape[0]):
        total += got[i].astype(F32)
    mine = own_mid.shape[0]
    total = jnp.concatenate([total[:mine], total[mine:]], axis=1)
    model = total.shape[1]
    power = jnp.sum(total * total, axis=1, keepdims=True) / model
    gain = jnp.concatenate([gains[z, 1:2] for z in range(NZ)], axis=1)
    hidden = (own_mid[...] + total * lax.rsqrt(power + EPS) * gain).astype(BF16)
    feats = out.shape[2]
    for r in range(model // feats):
        part = hidden[:, r * feats : (r + 1) * feats]
        for x in range(NX):
            out[r * NX + x] = part


def turn_kernel(got, out):
    rows = jnp.concatenate([got[i].astype(F32) for i in range(got.shape[0])], axis=0)
    out[...] = rows.T.astype(BF16)


def ring(shift, size):
    return [(i, (i + shift) % size) for i in range(size)]


def body(hidden_in, lengths, w_qkv, qk_gain, cache_keys, cache_values, w_out, norm_gain,
         w_gate_up, w_down):
    rows = lengths.shape[0]
    width = w_qkv.shape[2]
    heads = width // HEAD_DIM
    feats = hidden_in.shape[1]
    model = width * NX
    wide = rows * heads
    blocks = cache_keys.shape[0] // BLOCK

    flipped = hidden_in.T
    mate_rows = lax.ppermute(flipped, "c", ring(1, NC))
    mate_w = lax.ppermute(w_qkv, "c", ring(1, NC))
    half = HEAD_DIM // 2
    freqs = jnp.power(THETA, -(jnp.arange(half, dtype=F32) * 2.0 / HEAD_DIM))
    angles = lengths.astype(F32)[:, None] * freqs[None, :]
    cosine = jnp.cos(angles)
    sine = jnp.sin(angles)
    tables = jnp.stack(
        [jnp.concatenate([cosine, cosine], axis=1), jnp.concatenate([-sine, sine], axis=1)]
    )
    ends = jnp.cumsum(lengths)
    bounds = jnp.tile(jnp.stack([ends - lengths, ends], axis=1), (heads, 1))
    gain_table = jnp.concatenate([qk_gain, jnp.zeros((6, width), F32)], axis=0)
    places = NZ * NY
    half = HEAD_DIM // 2
    freqs = jnp.power(THETA, -(jnp.arange(half, dtype=F32) * 2.0 / HEAD_DIM))
    spots = jnp.pad(lengths.astype(F32), (0, 128 - rows))[None, :]
    angles = freqs[:, None] * spots
    trig = jnp.concatenate([jnp.cos(angles), jnp.sin(angles)], axis=0)
    spots = jnp.broadcast_to(spots, (8, 128))
    lanes = 128
    head_lanes = 3 * width + lanes
    tile_lanes = 3 * feats // rows * lanes
    out_lanes = feats // rows * width
    message = call(
        project_kernel,
        shape((places, rows, head_lanes + tile_lanes + out_lanes), BF16),
        [ANY] * 10,
        VMEM,
        [
            pltpu.VMEM((2, feats, flipped.shape[1]), BF16),
            pltpu.VMEM((2,) + w_qkv.shape, BF16),
            pltpu.VMEM((flipped.shape[1], 2 * feats), F32),
            pltpu.VMEM(w_gate_up.shape, BF16),
            pltpu.VMEM(w_down.shape, BF16),
            pltpu.VMEM(w_out.shape, BF16),
            pltpu.VMEM(norm_gain.shape, F32),
            pltpu.SemaphoreType.DMA((8,)),
        ],
        (1 << 27, 2 << 20),
        "project",
        8,
    )(hbm(flipped), mate_rows, hbm(w_qkv), mate_w, hbm(w_gate_up), hbm(w_down), hbm(w_out), hbm(norm_gain), trig, spots)
    got = lax.all_to_all(message, Z + ("y",), 0, 0, tiled=True)

    mate = lax.ppermute(got, "c", ring(1, NC))
    qk, value_new, squares, rest, ffn_own = call(
        collect_kernel,
        (
            shape((3, rows, width), F32),
            shape((rows, width), BF16),
            shape((NX, rows, 128), F32),
            shape((rows // NX, model), F32),
            shape((places, rows, tile_lanes), BF16),
        ),
        [VMEM],
        (VMEM,) * 4 + (ANY,),
        [pltpu.SemaphoreType.DMA],
        (1 << 20, 4 << 20),
        "collect",
        8,
    )(got)
    ffn_mate = lax.ppermute(ffn_own, "c", ring(1, NC))
    near = lax.ppermute(ffn_own, "zl", ring(1, 2))
    squares = lax.all_to_all(squares, "x", 0, 0, tiled=True)
    key_new, attended = call(
        attend_kernel,
        (shape((rows, width), BF16), shape((rows, width), BF16)),
        [VMEM] * 7,
        (VMEM,) * 2,
        [pltpu.VMEM((blocks, wide, BLOCK), F32)],
        (1 << 29, 8 << 20),
        "attend",
        16,
    )(squares, qk, trig, spots, qk_gain, cache_keys, cache_values)
    partial, gains = call(
        out_kernel,
        (shape((NX, rows // NX, model), F32), shape((NZ, 8, width), F32)),
        [VMEM] * 3 + [ANY],
        (VMEM,) * 2,
        (),
        (1 << 26, 2 << 20),
        "project_out",
        8,
    )(attended, got, mate, ffn_mate)

    summed = lax.all_to_all(partial, "x", 0, 0, tiled=True)
    mine = rows // NX
    group = ("zh", "y", "x")
    members = NZ * NY * NX // 2
    own_mid, message = call(
        fan_kernel,
        (shape((mine, model), F32), shape((members, 2 * mine, model // 2), BF16)),
        [VMEM] * 3,
        (VMEM, VMEM),
        (),
        (1 << 16, 1 << 19),
        "fan",
    )(summed, rest, gains)
    near = call(
        hold_kernel,
        shape(near.shape, BF16),
        [ANY] * 2,
        ANY,
        [pltpu.SemaphoreType.DMA],
        (0, 1 << 20),
        "hold",
        1,
    )(near, own_mid)
    near_mate = lax.ppermute(near, "c", ring(1, NC))
    got = lax.all_to_all(message, group, 0, 0, tiled=True)
    partial = call(
        ffn_kernel,
        shape((members, 2 * mine, model // 2), BF16),
        [VMEM] * 5,
        VMEM,
        (),
        (1 << 28, 4 << 20),
        "feed_forward",
        16,
    )(got, ffn_own, ffn_mate, near, near_mate)
    got = lax.all_to_all(partial, group, 0, 0, tiled=True)
    message = call(
        finish_kernel,
        shape((NZ * NY * NC * NX, mine, feats), BF16),
        [VMEM] * 3,
        VMEM,
        (),
        (1 << 18, 1 << 19),
        "finish",
    )(got, own_mid, gains)
    hidden = lax.all_to_all(message, Z + ("y", "c", "x"), 0, 0, tiled=True)
    hidden = call(
        turn_kernel,
        shape((feats, hidden.shape[0] * mine), BF16),
        [VMEM],
        VMEM,
        (),
        (1 << 16, 1 << 18),
        "turn",
    )(hidden)
    return hidden.T, key_new, value_new


def solution(mesh):
    fine = Mesh(mesh.devices.reshape(2, 2, NY, NC, NX), Z + ("y", "c", "x"))
    req = Z + ("y", "c")
    return jax.shard_map(
        body,
        mesh=fine,
        in_specs=(
            P(None, req),
            P(req),
            P(None, req, "x"),
            P(None, "x"),
            P(req, "x"),
            P(req, "x"),
            P(req, "x"),
            P(None, req),
            P(None, req, "x"),
            P(req, "x"),
        ),
        out_specs=(P(None, req), P(req, "x"), P(req, "x")),
        check_vma=False,
    )
```

```python
import jax
import jax.numpy as jnp
from jax import lax
from jax.experimental import pallas as pl
from jax.experimental.pallas import tpu as pltpu
from jax.sharding import Mesh, PartitionSpec as P

HEAD_DIM = 128
EPS = 1e-06
THETA = 500000.0
NT = (((1,), (1,)), ((), ()))
BLOCK = 512
F32 = jnp.float32
BF16 = jnp.bfloat16
NZ, NY, NC, NX = 4, 4, 2, 4
Z = ("zh", "zl")
VMEM = pl.BlockSpec(memory_space=pltpu.VMEM)
HBM = pl.BlockSpec(memory_space=pltpu.HBM)
ANY = pl.BlockSpec(memory_space=pl.ANY)
SMEM = pl.BlockSpec(memory_space=pltpu.SMEM)


def call(kernel, out_shape, in_specs, out_specs, scratch=(), cost=(1 << 20, 1 << 20), name=None, limit=4):
    return pl.pallas_call(
        kernel,
        out_shape=out_shape,
        in_specs=in_specs,
        out_specs=out_specs,
        scratch_shapes=list(scratch),
        compiler_params=pltpu.CompilerParams(vmem_limit_bytes=limit * 1024 * 1024),
        cost_estimate=pl.CostEstimate(flops=cost[0], bytes_accessed=cost[1], transcendentals=0),
        name=name,
    )


def hbm(array):
    return pltpu.with_memory_space_constraint(array, pltpu.HBM)


def shape(dims, dtype):
    return jax.ShapeDtypeStruct(dims, dtype)


def hold_kernel(piece, token, out, sem):
    copy = pltpu.make_async_copy(piece, out, sem)
    copy.start()
    copy.wait()


def project_kernel(h_own, h_mate, w_own, w_mate, gate_up, down, out_w, gains, trig, places, out, hbuf,
                   wbuf, rows_buf, gbuf, dbuf, obuf, nbuf, sem):
    core = lax.axis_index("c")
    pairs = (
        (h_own, hbuf.at[core]),
        (h_mate, hbuf.at[1 - core]),
        (w_own, wbuf.at[core]),
        (w_mate, wbuf.at[1 - core]),
        (gate_up, gbuf),
        (down, dbuf),
        (out_w, obuf),
        (gains, nbuf),
    )
    copies = [pltpu.make_async_copy(a, b, sem.at[i]) for i, (a, b) in enumerate(pairs)]
    for copy in copies:
        copy.start()
    copies[0].wait()
    copies[1].wait()
    rows_buf[...] = jnp.concatenate([hbuf[0].astype(F32).T, hbuf[1].astype(F32).T], axis=1)
    blocks, rows, _ = out.shape
    feats, width = w_own.shape[1:]
    lanes = 2 * feats
    chosen = jnp.concatenate(
        [
            rows_buf[pl.ds(pl.multiple_of((2 * b + core) * rows, rows), rows), :]
            for b in range(blocks)
        ],
        axis=0,
    ).astype(BF16)
    copies[2].wait()
    copies[3].wait()
    for g in range(3):
        weights = jnp.concatenate([wbuf[0, g], wbuf[1, g]], axis=0)
        part = jnp.dot(chosen, weights, preferred_element_type=F32).astype(BF16)
        out[:, :, g * width : (g + 1) * width] = part.reshape(blocks, rows, width)
    for copy in copies[4:]:
        copy.wait()
    at = 3 * width
    x = lax.axis_index("x")
    both = jnp.concatenate([nbuf[0:1, :], nbuf[1:2, :]], axis=1)
    high = both.astype(BF16).astype(F32)
    rest = jnp.zeros((rows - 6, lanes), F32)
    for b in range(blocks):
        low = pl.multiple_of((2 * b + core) * rows + x // 2 * 8, 8)
        pair = rows_buf[pl.ds(low, 8), :]
        own = jnp.where(lax.rem(x, 2) == 0, pair[:4], pair[4:])
        out[b, :, at : at + lanes] = jnp.concatenate([own, high, both - high, rest], axis=0).astype(BF16)
    at += lanes
    steps = feats // rows
    for part in range(3):
        for i in range(steps):
            low = slice(i * rows, (i + 1) * rows)
            for b in range(blocks):
                cols = slice(b * lanes, (b + 1) * lanes)
                out[b, :, at : at + lanes] = dbuf[low, cols] if part == 2 else gbuf[part, low, cols]
            at += lanes
    for b in range(blocks):
        for i in range(steps):
            out[b, :, at + i * width : at + (i + 1) * width] = obuf[i * rows : (i + 1) * rows]


def collect_kernel(got, qk, value, squares, rest, ffn, sem):
    rows, width = value.shape
    lanes = 128
    at = 3 * width + lanes
    copy = pltpu.make_async_copy(got.at[:, :, pl.ds(at, ffn.shape[2])], ffn, sem)
    copy.start()
    blocks = got.shape[0]
    total = got[0, :, : 3 * width].astype(F32)
    for i in range(1, blocks):
        total += got[i, :, : 3 * width].astype(F32)
    q, k = total[:, :width], total[:, width : 2 * width]
    qk[0] = q
    qk[1] = k
    new = total[:, 2 * width :].astype(BF16)
    value[...] = new
    qk[2] = new.astype(F32)
    lane = lax.broadcasted_iota(jnp.int32, squares.shape[1:], 1)
    both = jnp.where(
        lane < 64, jnp.sum(q * q, axis=1, keepdims=True), jnp.sum(k * k, axis=1, keepdims=True)
    )
    for i in range(NX):
        squares[i] = both
    for i in range(blocks):
        rest[:, i * lanes : (i + 1) * lanes] = got[i, :, 3 * width : at].astype(F32)[:4]
    copy.wait()


def turn(values, cosine, sine):
    heads = values.shape[1] // HEAD_DIM
    parts = []
    for h in range(heads):
        v = values[:, h * HEAD_DIM : (h + 1) * HEAD_DIM]
        parts.append(v * cosine + pltpu.roll(v, HEAD_DIM // 2, 1) * sine)
    return jnp.concatenate(parts, axis=1)


def spread(values, heads):
    rows, width = values.shape
    wide = rows * heads
    row_head = lax.broadcasted_iota(jnp.int32, (wide, width), 0) // rows
    col_head = lax.broadcasted_iota(jnp.int32, (wide, width), 1) // HEAD_DIM
    return jnp.where(row_head == col_head, jnp.concatenate([values] * heads, axis=0), 0.0)


def attend_kernel(squares_in, qk, trig, places, gains, keys, values, key_out,
                  out, score):
    rows, width = out.shape
    heads = width // HEAD_DIM
    blocks = score.shape[0]
    model = width * NX
    used = jnp.sum(places[0:1, :])
    wide = heads * rows
    request = lax.rem(lax.broadcasted_iota(jnp.int32, (wide, 128), 0), rows)
    lane = lax.broadcasted_iota(jnp.int32, (wide, 128), 1)
    lengths = jnp.broadcast_to(places[0:1, :], (wide, 128))
    starts = jnp.sum(jnp.where(lane < request, lengths, 0.0), axis=1, keepdims=True)
    ends = jnp.sum(jnp.where(lane <= request, lengths, 0.0), axis=1, keepdims=True)
    starts = starts.astype(jnp.int32)
    ends = ends.astype(jnp.int32)
    angles = trig[...].T
    half = HEAD_DIM // 2
    cosine = jnp.concatenate([angles[:rows, :half], angles[:rows, :half]], axis=1)
    sine = jnp.concatenate([-angles[:rows, half:], angles[:rows, half:]], axis=1)
    squares = squares_in[0] + squares_in[1] + squares_in[2] + squares_in[3]
    q_factor = lax.rsqrt(squares[:, 0:1] / model + EPS)
    k_factor = lax.rsqrt(squares[:, 64:65] / model + EPS)
    query = turn(qk[0] * q_factor * gains[0:1, :], cosine, sine).astype(BF16)
    new_key = turn(qk[1] * k_factor * gains[1:2, :], cosine, sine).astype(BF16)
    key_out[...] = new_key
    scale = HEAD_DIM ** (-0.5)
    q_all = spread(query.astype(F32), heads)
    q_block = q_all.astype(BF16)
    k_all = jnp.concatenate([new_key.astype(F32)] * heads, axis=0)
    v_all = jnp.concatenate([qk[2]] * heads, axis=0)
    own = jnp.sum(q_all * k_all, axis=1, keepdims=True) * scale
    def raw(i):
        rows_here = keys[pl.ds(i * BLOCK, BLOCK), :]
        s = lax.dot_general(q_block, rows_here, NT, preferred_element_type=F32) * scale
        place = lax.broadcasted_iota(jnp.int32, s.shape, 1) + i * BLOCK
        return jnp.where((place >= starts) & (place < ends), s, -jnp.inf)

    def finish(size):
        highest = own
        for i in range(size):
            s = raw(i)
            score[i] = s
            highest = jnp.maximum(highest, jnp.max(s, axis=1, keepdims=True))
        own_weight = jnp.exp(own - highest).astype(BF16).astype(F32)
        total = own_weight
        acc = own_weight * v_all
        for i in range(size):
            w = jnp.exp(score[i] - highest).astype(BF16)
            total += jnp.sum(w.astype(F32), axis=1, keepdims=True)
            acc += jnp.dot(w, values[pl.ds(i * BLOCK, BLOCK), :], preferred_element_type=F32)
        result = acc / total
        out[...] = jnp.concatenate(
            [
                result[h * rows : (h + 1) * rows, h * HEAD_DIM : (h + 1) * HEAD_DIM]
                for h in range(heads)
            ],
            axis=1,
        ).astype(BF16)

    short = 2

    @pl.when(used <= short * BLOCK)
    def _():
        finish(short)

    @pl.when(used > short * BLOCK)
    def _():
        finish(blocks)


def by_core(work, own, mate):
    core = lax.axis_index("c")

    @pl.when(core == 0)
    def _():
        work(own, mate)

    @pl.when(core == 1)
    def _():
        work(mate, own)


def out_kernel(attended, own, mate, after, partial, gain_out):
    rows, width = attended.shape
    head = 3 * width
    lanes = 128
    steps = 4
    last = own.shape[2] - steps * width
    mine = rows // NX

    def work(*cores):
        for b in range(NZ):
            weights = jnp.concatenate(
                [
                    cores[c][b * NY + y, :, last + i * width : last + (i + 1) * width]
                    for y in range(NY)
                    for c in range(NC)
                    for i in range(steps)
                ],
                axis=0,
            )
            a = lax.dot_general(attended[...], weights, NT, preferred_element_type=F32)
            for x in range(NX):
                partial[x, :, b * width : (b + 1) * width] = a[x * mine : (x + 1) * mine]
            for y in range(NY):
                two = [cores[c][b * NY + y, :, head : head + lanes].astype(F32) for c in range(NC)]
                two = [t[4:5] + t[5:6] for t in two]
                for g in range(2):
                    gain_out[b, g : g + 1, y * lanes : (y + 1) * lanes] = jnp.concatenate(
                        [t[:, g * 64 : (g + 1) * 64] for t in two], axis=1
                    )

    by_core(work, own, mate)


def fan_kernel(got, rest, gains, own_mid, out):
    total = got[0] + got[1] + got[2] + got[3]
    model = total.shape[1]
    power = jnp.sum(total * total, axis=1, keepdims=True) / model
    gain = jnp.concatenate([gains[z, 0:1] for z in range(NZ)], axis=1)
    mid = (rest[...] + total * lax.rsqrt(power + EPS) * gain).astype(BF16)
    mid32 = mid.astype(F32)
    own_mid[...] = mid32
    message = jnp.concatenate([mid32[:, : model // 2], mid32[:, model // 2 :]], axis=0).astype(BF16)
    for i in range(out.shape[0]):
        out[i] = message


def ffn_kernel(got, own, own_mate, near, near_mate, out):
    places, lines, span = got.shape
    mine = lines // 2
    whole = [got[d].astype(F32) for d in range(places)]
    mid = [
        jnp.concatenate([w[half * mine : (half + 1) * mine] for w in whole], axis=0).astype(BF16)
        for half in range(2)
    ]
    blocks = own.shape[0]
    lanes = 128
    steps = own.shape[2] // (3 * lanes)

    def work(*cores):
        def weights(part, half):
            rows = range(half * blocks // 2, (half + 1) * blocks // 2)
            return jnp.concatenate(
                [
                    jnp.concatenate(
                        [
                            cores[c][p][b, :, (part * steps + i) * lanes : (part * steps + i + 1) * lanes]
                            for b in rows
                            for c in range(NC)
                            for i in range(steps)
                        ],
                        axis=0,
                    )
                    for p in range(2)
                ],
                axis=1,
            )

        gate = jnp.dot(mid[0], weights(0, 0), preferred_element_type=F32)
        gate += jnp.dot(mid[1], weights(0, 1), preferred_element_type=F32)
        lift = jnp.dot(mid[0], weights(1, 0), preferred_element_type=F32)
        lift += jnp.dot(mid[1], weights(1, 1), preferred_element_type=F32)
        act = (gate / (1.0 + jnp.exp(-gate)) * lift).astype(BF16)
        flat = [lax.dot_general(act, weights(2, h), NT, preferred_element_type=F32) for h in range(2)]
        for d in range(places):
            out[d] = jnp.concatenate([f[d * mine : (d + 1) * mine] for f in flat], axis=0).astype(BF16)

    by_core(work, (own, near), (own_mate, near_mate))


def finish_kernel(got, own_mid, gains, out):
    total = got[0].astype(F32)
    for i in range(1, got.shape[0]):
        total += got[i].astype(F32)
    mine = own_mid.shape[0]
    total = jnp.concatenate([total[:mine], total[mine:]], axis=1)
    model = total.shape[1]
    power = jnp.sum(total * total, axis=1, keepdims=True) / model
    gain = jnp.concatenate([gains[z, 1:2] for z in range(NZ)], axis=1)
    hidden = (own_mid[...] + total * lax.rsqrt(power + EPS) * gain).astype(BF16)
    feats = out.shape[2]
    for r in range(model // feats):
        part = hidden[:, r * feats : (r + 1) * feats]
        for x in range(NX):
            out[r * NX + x] = part


def turn_kernel(got, out):
    rows = jnp.concatenate([got[i].astype(F32) for i in range(got.shape[0])], axis=0)
    out[...] = rows.T.astype(BF16)


def ring(shift, size):
    return [(i, (i + shift) % size) for i in range(size)]


def body(hidden_in, lengths, w_qkv, qk_gain, cache_keys, cache_values, w_out, norm_gain,
         w_gate_up, w_down):
    rows = lengths.shape[0]
    width = w_qkv.shape[2]
    heads = width // HEAD_DIM
    feats = hidden_in.shape[1]
    model = width * NX
    wide = rows * heads
    blocks = cache_keys.shape[0] // BLOCK

    flipped = hidden_in.T
    mate_rows = lax.ppermute(flipped, "c", ring(1, NC))
    mate_w = lax.ppermute(w_qkv, "c", ring(1, NC))
    half = HEAD_DIM // 2
    freqs = jnp.power(THETA, -(jnp.arange(half, dtype=F32) * 2.0 / HEAD_DIM))
    angles = lengths.astype(F32)[:, None] * freqs[None, :]
    cosine = jnp.cos(angles)
    sine = jnp.sin(angles)
    tables = jnp.stack(
        [jnp.concatenate([cosine, cosine], axis=1), jnp.concatenate([-sine, sine], axis=1)]
    )
    ends = jnp.cumsum(lengths)
    bounds = jnp.tile(jnp.stack([ends - lengths, ends], axis=1), (heads, 1))
    gain_table = jnp.concatenate([qk_gain, jnp.zeros((6, width), F32)], axis=0)
    places = NZ * NY
    half = HEAD_DIM // 2
    freqs = jnp.power(THETA, -(jnp.arange(half, dtype=F32) * 2.0 / HEAD_DIM))
    spots = jnp.pad(lengths.astype(F32), (0, 128 - rows))[None, :]
    angles = freqs[:, None] * spots
    trig = jnp.concatenate([jnp.cos(angles), jnp.sin(angles)], axis=0)
    spots = jnp.broadcast_to(spots, (8, 128))
    lanes = 128
    head_lanes = 3 * width + lanes
    tile_lanes = 3 * feats // rows * lanes
    out_lanes = feats // rows * width
    message = call(
        project_kernel,
        shape((places, rows, head_lanes + tile_lanes + out_lanes), BF16),
        [ANY] * 10,
        VMEM,
        [
            pltpu.VMEM((2, feats, flipped.shape[1]), BF16),
            pltpu.VMEM((2,) + w_qkv.shape, BF16),
            pltpu.VMEM((flipped.shape[1], 2 * feats), F32),
            pltpu.VMEM(w_gate_up.shape, BF16),
            pltpu.VMEM(w_down.shape, BF16),
            pltpu.VMEM(w_out.shape, BF16),
            pltpu.VMEM(norm_gain.shape, F32),
            pltpu.SemaphoreType.DMA((8,)),
        ],
        (1 << 27, 2 << 20),
        "project",
        8,
    )(hbm(flipped), mate_rows, hbm(w_qkv), mate_w, hbm(w_gate_up), hbm(w_down), hbm(w_out), hbm(norm_gain), trig, spots)
    got = lax.all_to_all(message, Z + ("y",), 0, 0, tiled=True)

    mate = lax.ppermute(got, "c", ring(1, NC))
    qk, value_new, squares, rest, ffn_own = call(
        collect_kernel,
        (
            shape((3, rows, width), F32),
            shape((rows, width), BF16),
            shape((NX, rows, 128), F32),
            shape((rows // NX, model), F32),
            shape((places, rows, tile_lanes), BF16),
        ),
        [VMEM],
        (VMEM,) * 4 + (ANY,),
        [pltpu.SemaphoreType.DMA],
        (1 << 20, 4 << 20),
        "collect",
        8,
    )(got)
    ffn_mate = lax.ppermute(ffn_own, "c", ring(1, NC))
    near = lax.ppermute(ffn_own, "zl", ring(1, 2))
    squares = lax.all_to_all(squares, "x", 0, 0, tiled=True)
    key_new, attended = call(
        attend_kernel,
        (shape((rows, width), BF16), shape((rows, width), BF16)),
        [VMEM] * 7,
        (VMEM,) * 2,
        [pltpu.VMEM((blocks, wide, BLOCK), F32)],
        (1 << 29, 8 << 20),
        "attend",
        16,
    )(squares, qk, trig, spots, qk_gain, cache_keys, cache_values)
    partial, gains = call(
        out_kernel,
        (shape((NX, rows // NX, model), F32), shape((NZ, 8, width), F32)),
        [VMEM] * 3 + [ANY],
        (VMEM,) * 2,
        (),
        (1 << 26, 2 << 20),
        "project_out",
        8,
    )(attended, got, mate, ffn_mate)

    summed = lax.all_to_all(partial, "x", 0, 0, tiled=True)
    mine = rows // NX
    group = ("x", "zh", "y")
    members = NZ * NY * NX // 2
    own_mid, message = call(
        fan_kernel,
        (shape((mine, model), F32), shape((members, 2 * mine, model // 2), BF16)),
        [VMEM] * 3,
        (VMEM, VMEM),
        (),
        (1 << 16, 1 << 19),
        "fan",
    )(summed, rest, gains)
    near = call(
        hold_kernel,
        shape(near.shape, BF16),
        [ANY] * 2,
        ANY,
        [pltpu.SemaphoreType.DMA],
        (0, 1 << 20),
        "hold",
        1,
    )(near, own_mid)
    near_mate = lax.ppermute(near, "c", ring(1, NC))
    got = lax.all_to_all(message, group, 0, 0, tiled=True)
    partial = call(
        ffn_kernel,
        shape((members, 2 * mine, model // 2), BF16),
        [VMEM] * 5,
        VMEM,
        (),
        (1 << 28, 4 << 20),
        "feed_forward",
        16,
    )(got, ffn_own, ffn_mate, near, near_mate)
    got = lax.all_to_all(partial, group, 0, 0, tiled=True)
    message = call(
        finish_kernel,
        shape((NZ * NY * NC * NX, mine, feats), BF16),
        [VMEM] * 3,
        VMEM,
        (),
        (1 << 18, 1 << 19),
        "finish",
    )(got, own_mid, gains)
    hidden = lax.all_to_all(message, Z + ("y", "c", "x"), 0, 0, tiled=True)
    hidden = call(
        turn_kernel,
        shape((feats, hidden.shape[0] * mine), BF16),
        [VMEM],
        VMEM,
        (),
        (1 << 16, 1 << 18),
        "turn",
    )(hidden)
    return hidden.T, key_new, value_new


def solution(mesh):
    fine = Mesh(mesh.devices.reshape(2, 2, NY, NC, NX), Z + ("y", "c", "x"))
    req = Z + ("y", "c")
    return jax.shard_map(
        body,
        mesh=fine,
        in_specs=(
            P(None, req),
            P(req),
            P(None, req, "x"),
            P(None, "x"),
            P(req, "x"),
            P(req, "x"),
            P(req, "x"),
            P(None, req),
            P(None, req, "x"),
            P(req, "x"),
        ),
        out_specs=(P(None, req), P(req, "x"), P(req, "x")),
        check_vma=False,
    )
```
